32 devices in a mesh: blk: 16 (over z, y, x), sub: 2 (over core).
Axes of the slice: x: 2, y: 2, z: 4, core: 2. Of those that a mesh axis runs over, the one named last changes fastest.
Arguments:
- velocity: float32 [3, 1190112], P(None, ('blk', 'sub')), may hold values from -4 to 4, as said below
- pressure_load: float32 [1190112], P(('blk', 'sub')), may hold values from -24 to 24, as said below
- local_map: int32 [216, 8192], P(None, ('blk', 'sub')), may hold values from 0 to 37190, as said below
- stiff_geo: float32 [3, 8192], P(None, ('blk', 'sub')), may hold values from 0.1 to 1
- mass_geo: float32 [8192], P(('blk', 'sub')), may hold values from 1 to 10
Outputs:
- vel_applied: float32 [3, 1190112], P(None, ('blk', 'sub'))
- pressure: float32 [1190112], P(('blk', 'sub'))
- new_residual: float32 [1190112], P(('blk', 'sub'))
The draws below stay inside these ranges and needn't reach their ends.
Inputs may be any that keep to these rules, and one draw needn't show every extreme that they name: `velocity`: copies of one node stored on neighbouring devices hold equal values. `pressure_load`: copies of one node stored on neighbouring devices hold equal values. `local_map`: the 256 columns of each device name that device's 2 x 4 x 32 elements, each once, in any order; the element at position (ex, ez, ey) lists for node n = 36 i + 6 j + k the local index ((5 ex + i) * 21 + 5 ez + j) * 161 + 5 ey + k.
All inputs are finite; a program needn't handle non-finite values.
Results may differ from the reference program's by a relative error of at most 0.0003.
The reference program's roundings to bfloat16 on the way count: a program that leaves them out, or rounds other values in their place, can miss the bound.
Values sent between devices are 32-bit elements; how exact they have to be, the bound alone decides.
A program may use at most 64 MiB of HBM per device.

```python
import math
import jax
import jax.numpy as jnp
import numpy as np
from jax import lax

EX = 2
EZ = 4
EY = 32
CHEB_ITERS = 8
E_DEV = 256
ELEMS = 8192
NX = 11
NZ = 21
NY = 161
NLOC = 37191
NODES = 1190112
N_BLK = 16
N_SUB = 2


def node_places():
    flat_index = jnp.arange(NODES, dtype=jnp.int32)
    device_index = flat_index // NLOC
    local_index = flat_index % NLOC
    place_x = device_index % N_SUB * (NX - 1) + local_index // (NZ * NY)
    place_z = device_index // N_SUB * (NZ - 1) + local_index // NY % NZ
    place_y = local_index % NY
    return (place_x, place_z, place_y)


def draw_velocity(key, part):
    place_x, place_z, place_y = node_places()
    shape_all = (3, N_SUB * (NX - 1) + 1, N_BLK * (NZ - 1) + 1, NY)
    whole_field = jnp.clip(jax.random.normal(key, shape_all, jnp.float32), -4.0, 4.0)
    return whole_field[:, place_x, place_z, place_y]


def draw_pressure_load(key, part):
    place_x, place_z, place_y = node_places()
    length_z = N_BLK * (NZ - 1) + 1
    shape_all = (N_SUB * (NX - 1) + 1, length_z, NY)
    along_ramp = jnp.arange(length_z, dtype=jnp.float32) / (length_z - 1)
    whole_field = 2.0 * jnp.clip(jax.random.normal(key, shape_all, jnp.float32), -4.0, 4.0) * (1.0 + 2.0 * along_ramp)[None, :, None]
    return whole_field[place_x, place_z, place_y]


def draw_local_map(key, part):
    device_count = ELEMS // E_DEV
    orders = jax.vmap(lambda device_number: jax.random.permutation(jax.random.fold_in(key, device_number), E_DEV))(jnp.arange(device_count))
    element = orders.reshape(-1).astype(jnp.int32)
    elem_x = element // (EZ * EY)
    elem_z = element // EY % EZ
    elem_y = element % EY
    node_index = jnp.arange(216, dtype=jnp.int32)
    place_x = 5 * elem_x[None, :] + (node_index // 36)[:, None]
    place_z = 5 * elem_z[None, :] + (node_index // 6 % 6)[:, None]
    place_y = 5 * elem_y[None, :] + (node_index % 6)[:, None]
    return ((place_x * NZ + place_z) * NY + place_y).astype(jnp.int32)


def levels(key, shape, pieces, low, largest):
    def one(dim, blocks):
        draws = jax.random.uniform(jax.random.fold_in(jax.random.fold_in(key, 6), dim), (blocks,), jnp.float32, low / len(pieces), largest / len(pieces))
        return jnp.repeat(jnp.exp(draws), shape[dim] // blocks).reshape((-1,) + (1,) * (len(shape) - dim - 1))

    level = one(*pieces[0])
    for cut in pieces[1:]:
        level = level * one(*cut)
    return level


def setup_inputs(seed: int = 0) -> dict:
    keys = jax.random.split(jax.random.key(seed), 6)
    return {
        "velocity": draw_velocity(jax.random.fold_in(keys[5], 71), 0),
        "pressure_load": draw_pressure_load(jax.random.fold_in(keys[5], 71), 0),
        "local_map": draw_local_map(jax.random.fold_in(keys[5], 71), 0),
        "stiff_geo": jnp.clip(jnp.exp(math.log(1.0) - 2.3025851 * jax.random.uniform(keys[3], (3, ELEMS), jnp.float32) ** levels(keys[3], (3, ELEMS), ((1, 32),), -0.2, 0.2)), 0.1, 1.0),
        "mass_geo": jnp.clip(jnp.exp(math.log(10.0) - 2.3025851 * jax.random.uniform(keys[4], (ELEMS,), jnp.float32) ** levels(keys[4], (ELEMS,), ((0, 32),), -0.2, 0.2)), 1.0, 10.0),
    }


PRECISE = lax.Precision.HIGHEST
DAMPING = 0.3
MASS_SHARE = 0.05
SPECTRUM_LOW = 0.15
SPECTRUM_HIGH = 4.5
OFFSETS = [(a, b, c) for a in (0, 1) for b in (0, 1) for c in (0, 1)]

def spectral_tables():
    seven_root = math.sqrt(7.0)
    inner_point = math.sqrt(1.0 / 3.0 - 2.0 * seven_root / 21.0)
    outer_point = math.sqrt(1.0 / 3.0 + 2.0 * seven_root / 21.0)
    points = np.array([-1.0, -outer_point, -inner_point, inner_point, outer_point, 1.0])
    legendre = (63.0 * points ** 5 - 70.0 * points ** 3 + 15.0 * points) / 8.0
    weights = 2.0 / (30.0 * legendre ** 2)
    derivative = np.zeros((6, 6))
    for row_index in range(6):
        for col_index in range(6):
            if row_index != col_index:
                derivative[row_index, col_index] = legendre[row_index] / (legendre[col_index] * (points[row_index] - points[col_index]))
    derivative[0, 0] = -7.5
    derivative[5, 5] = 7.5
    identity = np.eye(6)
    directions = [np.kron(np.kron(derivative, identity), identity), np.kron(np.kron(identity, derivative), identity), np.kron(np.kron(identity, identity), derivative)]
    node_weight = np.kron(np.kron(weights, weights), weights)
    stiff_diagonal = np.stack([(operator_block ** 2).T @ node_weight for operator_block in directions])
    linear = np.stack([(1.0 - points) / 2.0, (1.0 + points) / 2.0], 1)
    vertex_interp = np.kron(np.kron(linear, linear), linear)
    coarse_blocks = [vertex_interp.T @ (operator_block.T @ (node_weight[:, None] * operator_block)) @ vertex_interp for operator_block in directions]
    coarse_blocks.append(MASS_SHARE * (vertex_interp.T @ (node_weight[:, None] * vertex_interp)))
    coarse_numbers = np.stack(coarse_blocks)
    eight_range = np.arange(8)
    coarse_diag_numbers = np.stack([coarse_block[eight_range, eight_range] for coarse_block in coarse_blocks])
    return (derivative, np.concatenate(directions, 0), node_weight, stiff_diagonal, coarse_numbers, coarse_diag_numbers, linear)

def line_interp(linear, elem_count):
    matrix = np.zeros((5 * elem_count + 1, elem_count + 1))
    for node_index in range(5 * elem_count + 1):
        element_index = min(node_index // 5, elem_count - 1)
        local_index = node_index - 5 * element_index
        matrix[node_index, element_index] = linear[local_index, 0]
        matrix[node_index, element_index + 1] = linear[local_index, 1]
    return matrix

def duplicate_weight(node_count, part_count, position):
    places = jnp.arange(node_count)
    shared = (places == 0) & (position > 0) | (places == node_count - 1) & (position < part_count - 1)
    return jnp.where(shared, 0.5, 1.0).astype(jnp.float32)

def gradients(values, derivative):
    grad_x = jnp.einsum('im,...mjke->...ijke', derivative, values, precision=PRECISE)
    grad_z = jnp.einsum('jm,...imke->...ijke', derivative, values, precision=PRECISE)
    grad_y = jnp.einsum('km,...ijme->...ijke', derivative, values, precision=PRECISE)
    return (grad_x, grad_z, grad_y)

def divergence(flux_terms, derivative):
    return jnp.einsum('mi,...mjke->...ijke', derivative, flux_terms[0], precision=PRECISE) + jnp.einsum('mj,...imke->...ijke', derivative, flux_terms[1], precision=PRECISE) + jnp.einsum('mk,...ijme->...ijke', derivative, flux_terms[2], precision=PRECISE)

def spread_nodes(values, node_ids):
    flat_ids = node_ids.reshape(-1)

    def one_row(single_row):
        return jax.ops.segment_sum(single_row.reshape(-1), flat_ids, num_segments=NLOC)
    return jax.vmap(one_row)(values)

def coarse_coefficients(node_ids, stiff_rows, mass_row):
    corner = node_ids[0]
    slot_index = ((corner // (NZ * NY) // 5 * EZ + corner // NY % NZ // 5) * EY + corner % NY // 5).astype(jnp.int32)
    packed = jnp.concatenate([stiff_rows, mass_row[None, :]], 0)
    return jnp.zeros((4, E_DEV), jnp.float32).at[:, slot_index].set(packed).reshape(4, EX, EZ, EY)

def gather_corners(result):
    summed = jnp.zeros((EX + 1, EZ + 1, EY + 1), result.dtype)
    for index_pos, (a, b, c) in enumerate(OFFSETS):
        summed = summed + jnp.pad(result[index_pos], ((a, 1 - a), (b, 1 - b), (c, 1 - c)))
    return summed

def coarse_local(vertex, element_coefs, coarse_table):
    corners = jnp.stack([lax.slice(vertex, (a, b, c), (a + EX, b + EZ, c + EY)) for a, b, c in OFFSETS])
    result = jnp.einsum('quv,qxzy,vxzy->uxzy', coarse_table, element_coefs, corners, precision=PRECISE)
    return gather_corners(result)

def assemble_all(node_field):
    across = node_field.at[:, 1:, :, 0].add(node_field[:, :-1, :, -1])
    across = across.at[:, :-1, :, -1].add(node_field[:, 1:, :, 0])
    along_pipe = across.at[1:, :, :, :, 0].add(across[:-1, :, :, :, -1])
    along_pipe = along_pipe.at[:-1, :, :, :, -1].add(across[1:, :, :, :, 0])
    return along_pipe

def reference(velocity, pressure_load, local_map, stiff_geo, mass_geo):
    derivative, stacked, node_weight, stiff_diagonal, coarse_numbers, coarse_diag_numbers, linear = spectral_tables()
    devices = N_BLK * N_SUB
    derive_full = jnp.asarray(derivative, jnp.float32)
    derive_half = lax.optimization_barrier(derive_full.astype(jnp.bfloat16)).astype(jnp.float32)
    weight_cube = jnp.asarray(node_weight, jnp.float32).reshape(6, 6, 6, 1)
    weight_flat = jnp.asarray(node_weight, jnp.float32)
    diag_table = jnp.asarray(stiff_diagonal, jnp.float32)
    coarse_table = jnp.asarray(coarse_numbers, jnp.float32)
    coarse_diag_table = jnp.asarray(coarse_diag_numbers, jnp.float32)
    line_x = jnp.asarray(line_interp(linear, EX), jnp.float32)
    line_z = jnp.asarray(line_interp(linear, EZ), jnp.float32)
    line_y = jnp.asarray(line_interp(linear, EY), jnp.float32)
    device_maps = local_map.reshape(216, devices, E_DEV).transpose(1, 0, 2)
    stiffs = stiff_geo.reshape(3, devices, E_DEV).transpose(1, 0, 2)
    masses = mass_geo.reshape(devices, E_DEV)

    def velocity_device(packed):
        values, node_ids, stiff_rows, mass_row = packed
        element = lax.optimization_barrier(values[:, node_ids].astype(jnp.bfloat16)).astype(jnp.float32).reshape(3, 6, 6, 6, E_DEV)
        gradient_parts = gradients(element, derive_half)
        scaled = [lax.optimization_barrier((gradient_parts[direction] * weight_cube * stiff_rows[direction]).astype(jnp.bfloat16)).astype(jnp.float32) for direction in range(3)]
        returned = divergence(scaled, derive_half) + mass_row * weight_cube * element
        return spread_nodes(returned, node_ids)

    def diagonal_device(packed):
        node_ids, stiff_rows, mass_row = packed
        element_diagonal = diag_table[0][:, None] * stiff_rows[0][None, :] + diag_table[1][:, None] * stiff_rows[1][None, :] + diag_table[2][:, None] * stiff_rows[2][None, :] + (MASS_SHARE * mass_row)[None, :] * weight_flat[:, None]
        return spread_nodes(element_diagonal[None], node_ids)[0]

    def pressure_device(packed):
        values, node_ids, stiff_rows, mass_row = packed
        element = values[node_ids].reshape(6, 6, 6, E_DEV)
        gradient_parts = gradients(element, derive_full)
        scaled = [gradient_parts[direction] * weight_cube * stiff_rows[direction] for direction in range(3)]
        returned = divergence(scaled, derive_full) + MASS_SHARE * mass_row * weight_cube * element
        return spread_nodes(returned[None], node_ids)[0]

    def assemble_nodes(partial_value):
        node_grid = partial_value.reshape(N_BLK, N_SUB, partial_value.shape[1], NX, NZ, NY)
        return assemble_all(node_grid).reshape(devices, partial_value.shape[1], NLOC)

    def apply_pressure(node_field):
        partial_value = lax.map(pressure_device, (node_field, device_maps, stiffs, masses))
        return assemble_nodes(partial_value[:, None])[:, 0]

    def assemble_vertices(partial_value):
        vertex_grid = partial_value.reshape(N_BLK, N_SUB, partial_value.shape[1], EX + 1, EZ + 1, EY + 1)
        return assemble_all(vertex_grid).reshape(partial_value.shape)
    vel_devices = velocity.reshape(3, devices, NLOC).transpose(1, 0, 2)
    vel_partial = lax.map(velocity_device, (vel_devices, device_maps, stiffs, masses))
    vel_applied = assemble_nodes(vel_partial).transpose(1, 0, 2).reshape(3, devices * NLOC)
    diag_field = assemble_nodes(jax.vmap(diagonal_device)((device_maps, stiffs, masses))[:, None])[:, 0]
    weight_x = duplicate_weight(NX, N_SUB, jnp.arange(N_SUB)[:, None])
    weight_z = duplicate_weight(NZ, N_BLK, jnp.arange(N_BLK)[:, None])
    weight_nodes = jnp.broadcast_to(weight_x[None, :, :, None, None] * weight_z[:, None, None, :, None], (N_BLK, N_SUB, NX, NZ, NY)).reshape(devices, NLOC)
    pressure_rhs = pressure_load.reshape(devices, NLOC)
    first_iterate = DAMPING * pressure_rhs / diag_field
    residual = pressure_rhs - apply_pressure(first_iterate)
    second_iterate = first_iterate + DAMPING * residual / diag_field
    residual = pressure_rhs - apply_pressure(second_iterate)
    weighted = (weight_nodes * residual).reshape(devices, NX, NZ, NY)
    restricted = jnp.einsum('dxzy,xa,zb,yc->dabc', weighted, line_x, line_z, line_y, precision=PRECISE)
    element_coefs = jax.vmap(coarse_coefficients)(device_maps, stiffs, masses)
    coarse_diag_part = jax.vmap(lambda values: gather_corners(jnp.einsum('qu,qxzy->uxzy', coarse_diag_table, values, precision=PRECISE)))(element_coefs)
    coarse_pair = assemble_vertices(jnp.stack([restricted, coarse_diag_part], 1))
    coarse_rhs = coarse_pair[:, 0]
    coarse_diag = coarse_pair[:, 1]

    def coarse_apply(vertex):
        partial_value = jax.vmap(lambda values, device_coefs: coarse_local(values, device_coefs, coarse_table))(vertex, element_coefs)
        return assemble_vertices(partial_value[:, None])[:, 0]
    cheb_center = (SPECTRUM_HIGH + SPECTRUM_LOW) / 2.0
    cheb_radius = (SPECTRUM_HIGH - SPECTRUM_LOW) / 2.0
    cheb_ratio = cheb_center / cheb_radius
    cheb_factor = 1.0 / cheb_ratio
    direction_c = coarse_rhs / coarse_diag / cheb_center
    solution_c = direction_c
    residual_c = coarse_rhs
    for sweep_index in range(CHEB_ITERS - 1):
        residual_c = residual_c - coarse_apply(direction_c)
        next_factor = 1.0 / (2.0 * cheb_ratio - cheb_factor)
        direction_c = next_factor * cheb_factor * direction_c + 2.0 * next_factor / cheb_radius * (residual_c / coarse_diag)
        solution_c = solution_c + direction_c
        cheb_factor = next_factor
    correction = jnp.einsum('dabc,xa,zb,yc->dxzy', solution_c, line_x, line_z, line_y, precision=PRECISE).reshape(devices, NLOC)
    third_iterate = second_iterate + correction
    residual = pressure_rhs - apply_pressure(third_iterate)
    fourth_iterate = third_iterate + DAMPING * residual / diag_field
    residual = pressure_rhs - apply_pressure(fourth_iterate)
    smoothed = fourth_iterate + DAMPING * residual / diag_field
    operator_image = apply_pressure(smoothed)
    step_length = jnp.sum(weight_nodes * pressure_rhs * smoothed) / jnp.sum(weight_nodes * smoothed * operator_image)
    pressure = (step_length * smoothed).reshape(-1)
    new_residual = (pressure_rhs - step_length * operator_image).reshape(-1)
    return (vel_applied, pressure, new_residual)
```

```python
import functools
import math

import jax
import jax.numpy as jnp
import numpy as np
from jax import lax
from jax.experimental import pallas as pl
from jax.experimental.pallas import tpu as pltpu
from jax.sharding import PartitionSpec as P

EX = 2
EZ = 4
EY = 32
CHEB_ITERS = 8
NX = 5 * EX + 1
NZ = 5 * EZ + 1
NY = 5 * EY + 1
NLOC = NX * NZ * NY
NZP = 24
NYP = 256
HALO = 2
DEPTH = CHEB_ITERS - 1 + HALO
REACH = -(-DEPTH // EZ)
SPAN = 2 * REACH + 1
NZV = SPAN * EZ + 1
FIRST = REACH * EZ
LAST_V = FIRST + EZ
ZLO = FIRST - DEPTH
ZHI = LAST_V + DEPTH
EXCH = 7
ZT = -(-NX // 4)
LAST = (NX - 1) % 4

DAMPING = 0.3
MASS_SHARE = 0.05
SPECTRUM_LOW = 0.15
SPECTRUM_HIGH = 4.5
MESH = pl.DeviceIdType.MESH
F32 = jnp.float32
BF16 = jnp.bfloat16


def tables():
    seven_root = math.sqrt(7.0)
    inner = math.sqrt(1.0 / 3.0 - 2.0 * seven_root / 21.0)
    outer = math.sqrt(1.0 / 3.0 + 2.0 * seven_root / 21.0)
    xi = np.array([-1.0, -outer, -inner, inner, outer, 1.0])
    leg = (63.0 * xi**5 - 70.0 * xi**3 + 15.0 * xi) / 8.0
    w = 2.0 / (30.0 * leg**2)
    D = np.zeros((6, 6))
    for i in range(6):
        for j in range(6):
            if i != j:
                D[i, j] = leg[i] / (leg[j] * (xi[i] - xi[j]))
    D[0, 0] = -7.5
    D[5, 5] = 7.5
    k1 = D.T @ (w[:, None] * D)
    lin = np.stack([(1.0 - xi) / 2.0, (1.0 + xi) / 2.0], 1)
    kc = lin.T @ k1 @ lin
    mc = lin.T @ (w[:, None] * lin)
    coarse = [
        np.kron(np.kron(kc, mc), mc),
        np.kron(np.kron(mc, kc), mc),
        np.kron(np.kron(mc, mc), kc),
        MASS_SHARE * np.kron(np.kron(mc, mc), mc),
    ]
    return D, w, k1, lin, coarse


def roll_tables(M):
    out = np.zeros((8, 8, 128), np.float32)
    for s in range(8):
        for j in range(6):
            m = (j - s) % 8
            if m < 6:
                out[s, j, :] = M[j, m]
    return out


def col_tile(values):
    tile = np.zeros((1, 8, 128), np.float32)
    tile[0, :6, :] = np.asarray(values)[:, None]
    return tile


def bf16_round(a):
    return np.asarray(a, np.float32).astype(np.dtype(BF16)).astype(np.float64)


def pick_matrices():
    pick = np.zeros((NYP, 6, 128), np.float32)
    put = np.zeros((6, 128, NYP), np.float32)
    for k in range(6):
        for z in range(EZ):
            for e in range(EY):
                pick[5 * e + k, k, z * EY + e] = 1.0
                if k < 5 or e == EY - 1:
                    put[k, z * EY + e, 5 * e + k] = 1.0
    return pick.reshape(NYP, 768), put.reshape(768, NYP)


def mac(pairs):
    total = None
    for coef, value in pairs:
        if isinstance(coef, (float, int)) and coef == 0.0:
            continue
        term = coef * value
        total = term if total is None else total + term
    return total


def kernel(
    n_blk,
    n_sub,
    xs,
    vel_hbm,
    load_hbm,
    map_hbm,
    stiff_hbm,
    mass_hbm,
    tab_hbm,
    pick_hbm,
    put_hbm,
    velout_ref,
    pres_ref,
    res_ref,
    vel_ref,
    load_ref,
    stiff_ref,
    mass_ref,
    tab_ref,
    pick_ref,
    put_ref,
    V,
    W,
    FS,
    map_ref,
    R,
    INV,
    VV,
    VE,
    GX,
    GC,
    GE,
    SG,
    xsend,
    xrecv,
    zsend,
    zrecv,
    drecv,
    csend,
    crecv,
    rsend,
    rrecv,
    bsend,
    brecv,
    CF,
    ST,
    CU,
    CR,
    psend,
    precv,
    ex_send,
    ex_recv,
    c_send,
    c_recv,
    h_send,
    h_recv,
    p_sem,
    in_sem,
):
    D, w, k1, lin, coarse = tables()
    Dh = bf16_round(D)
    n_dev = n_blk * n_sub
    b = lax.axis_index("blk")
    s = lax.axis_index("sub")
    me = b * n_sub + s

    def device_of(linear):
        return (linear // n_sub, lax.rem(linear, n_sub))

    barrier = pltpu.get_barrier_semaphore()

    def greet(d, carry):
        pl.semaphore_signal(
            barrier, inc=1, device_id=device_of(lax.rem(me + d, n_dev)), device_id_type=MESH
        )
        return carry

    lax.fori_loop(1, n_dev, greet, 0)

    fetch = {}
    for at, (name, src, dst) in enumerate(
        (
            ("map", map_hbm.at[0:8, :], map_ref),
            ("stiff", stiff_hbm, stiff_ref),
            ("mass", mass_hbm, mass_ref),
            ("tab", tab_hbm, tab_ref),
            ("load", load_hbm, load_ref),
            ("pick", pick_hbm, pick_ref),
            ("vel", vel_hbm, vel_ref),
            ("put", put_hbm, put_ref),
        )
    ):
        fetch[name] = pltpu.make_async_copy(src, dst, in_sem.at[at])
        fetch[name].start()

    has = {
        "xl": s > 0,
        "xh": s < n_sub - 1,
        "zl": b > 0,
        "zh": b < n_blk - 1,
    }

    def zero(ref_slice):
        ref_slice[...] = jnp.zeros(ref_slice.shape, F32)

    for side, name in ((0, "xl"), (1, "xh")):

        @pl.when(jnp.logical_not(has[name]))
        def _(side=side):
            zero(xrecv.at[:, side])

    for side, name in ((0, "zl"), (1, "zh")):

        @pl.when(jnp.logical_not(has[name]))
        def _(side=side):
            zero(zrecv.at[:, side])
            zero(brecv.at[:, side])

    for zs, zname in ((0, "zl"), (1, "zh")):
        for xside, xname in ((0, "xl"), (1, "xh")):

            @pl.when(jnp.logical_not(jnp.logical_and(has[zname], has[xname])))
            def _(zs=zs, xside=xside):
                zero(drecv.at[:, zs, xside])

    for o in range(SPAN):
        off = o - REACH

        @pl.when(jnp.logical_or(b + off < 0, b + off >= n_blk))
        def _(o=o):
            zero(crecv.at[o])
            zero(rrecv.at[o])

    CF[...] = jnp.zeros(CF.shape, F32)
    FS[...] = jnp.zeros(FS.shape, F32)

    lane = lax.broadcasted_iota(jnp.int32, (8, 128), 1)
    sub_i = lax.broadcasted_iota(jnp.int32, (8, 128), 0)
    lane88 = lax.broadcasted_iota(jnp.int32, (8 * NX, 768), 1) // EY % EZ
    row88 = lax.broadcasted_iota(jnp.int32, (8 * NX, 768), 0) % 8
    ey = lane % EY
    lane6 = lax.broadcasted_iota(jnp.int32, (6, 128), 1)
    group6 = lane6 // EY
    group = lane // EY
    CT = lambda q: tab_ref[q]

    def moved(tile, shift):
        return tile if shift % 128 == 0 else pltpu.roll(tile, shift % 128, 1)

    def to_elements(field, dest, exact):
        FS[:, 0:NZ, 0:NY] = field[...]
        rows = jnp.concatenate(
            [FS[:, 5 * ez : 5 * ez + 8, :].reshape(8 * NX, NYP) for ez in range(EZ)], axis=0
        )
        hi = rows.astype(BF16)
        got = jnp.dot(hi, pick_ref[...], preferred_element_type=F32)
        if exact:
            lo = (rows - hi.astype(F32)).astype(BF16)
            got = got + jnp.dot(lo, pick_ref[...], preferred_element_type=F32)
        result = jnp.zeros((8 * NX, 768), F32)
        for ez in range(EZ):
            piece = got[8 * NX * ez : 8 * NX * (ez + 1)]
            result = jnp.where(jnp.logical_and(lane88 == ez, row88 < 6), piece, result)
        for k in range(6):
            dest[:, k] = result[:, 128 * k : 128 * k + 128].reshape(NX, 8, 128)

    def to_nodes(source, dest):
        full = jnp.concatenate([source[:, k].reshape(8 * NX, 128) for k in range(6)], axis=1)
        hi = full.astype(BF16).astype(F32)
        lo = full - hi
        his = [jnp.where(lane88 == ez, hi, 0.0) for ez in range(EZ)]
        los = [jnp.where(lane88 == ez, lo, 0.0) for ez in range(EZ)]
        got = jnp.dot(
            jnp.concatenate(his, axis=0).astype(BF16), put_ref[...], preferred_element_type=F32
        ) + jnp.dot(
            jnp.concatenate(los, axis=0).astype(BF16), put_ref[...], preferred_element_type=F32
        )
        for ez in range(EZ):
            piece = got[8 * NX * ez : 8 * NX * (ez + 1)].reshape(NX, 8, NYP)
            dest[:, 5 * ez : 5 * ez + 6, :] = piece[:, :6, :NY]

    for name in ("map", "stiff", "mass", "tab"):
        fetch[name].wait()
    WJ = tab_ref[24]
    LJ = (tab_ref[25], tab_ref[26])
    corner = map_ref[0:1, :]
    slot = (corner // (NZ * NY) // 5 * EZ + corner // NY % NZ // 5) * EY + corner % NY // 5
    count = EX * EZ * EY
    hot = (
        lax.broadcasted_iota(jnp.int32, (count, count), 0)
        == jnp.broadcast_to(slot, (count, count))
    ).astype(F32)
    geo = jnp.concatenate(
        [stiff_ref[...], mass_ref[...], jnp.zeros((4, count), F32)], axis=0
    )
    part_hi = geo.astype(BF16).astype(F32)
    part_mid = (geo - part_hi).astype(BF16).astype(F32)
    part_lo = geo - part_hi - part_mid
    pack = jnp.concatenate([part_hi, part_mid, part_lo], axis=0).astype(BF16)
    got = lax.dot_general(
        pack, hot.astype(BF16), (((1,), (1,)), ((), ())), preferred_element_type=F32
    )
    sorted_geo = got[0:8] + got[8:16] + got[16:24]
    stack = jnp.zeros((8, 128), F32)
    for q in range(4):
        for ex in range(EX):
            row = jnp.broadcast_to(
                sorted_geo[q : q + 1, 128 * ex : 128 * ex + 128], (8, 128)
            )
            SG[q, ex] = row
            stack = jnp.where(sub_i == EX * q + ex, row, stack)
    csend[...] = stack

    def geometry(h, tile):
        g = [
            [
                jnp.broadcast_to(tile[EX * q + ex : EX * q + ex + 1, :], (8, 128))
                for ex in range(EX)
            ]
            for q in range(4)
        ]
        for ex in range(EX):
            GX[h, 1 + ex] = WJ * g[0][ex]
        for x in range(NX):
            share = [(ex, x - 5 * ex) for ex in range(EX) if 0 <= x - 5 * ex <= 5]
            GC[h, 0, x] = WJ * mac([(float(w[i]), g[2][ex]) for ex, i in share])
            GC[h, 1, x] = mac([(float(w[i]), g[1][ex]) for ex, i in share])
            GC[h, 2, x] = WJ * mac([(float(MASS_SHARE * w[i]), g[3][ex]) for ex, i in share])

    def face_geometry(h, tiles):
        for face, (tile, ex) in enumerate(zip(tiles, (EX - 1, 0))):
            g = [
                jnp.broadcast_to(tile[EX * q + ex : EX * q + ex + 1, :], (8, 128))
                for q in range(4)
            ]
            x = (NX - 1) * face
            GX[h, (EX + 1) * face] = WJ * g[0]
            GE[h, face, 0] = GC[h, 0, x] + WJ * (float(w[0]) * g[2])
            GE[h, face, 1] = GC[h, 1, x] + float(w[0]) * g[1]
            GE[h, face, 2] = GC[h, 2, x] + WJ * (float(MASS_SHARE * w[0]) * g[3])

    def whole_geometry(h, x):
        if x == 0:
            return tuple(GE[h, 0, q] for q in range(3))
        if x == NX - 1:
            return tuple(GE[h, 1, q] for q in range(3))
        return tuple(GC[h, q, x] for q in range(3))

    def diagonal_part(h):
        kj = tab_ref[27]
        for x in range(NX):
            share = [
                (ex, x - 5 * ex) for ex in range(-1, EX + 1) if 0 <= x - 5 * ex <= 5
            ]
            gx = mac([(float(k1[i, i]), GX[h, 1 + ex]) for ex, i in share])
            gy, gz, gm = whole_geometry(h, x)
            base = gx + gz * kj + gm
            for k in range(6):
                W[h, x, k] = float(w[k]) * base + float(k1[k, k]) * gy

    def apply_part(h):
        src, dst = V.at[h], W.at[h]
        for ex in range(EX):
            gx = GX[h, 1 + ex]
            for k in range(6):
                vs = [src[5 * ex + m, k] for m in range(6)]
                gk = float(w[k]) * gx
                for i in range(6):
                    value = gk * mac([(float(k1[i, m]), vs[m]) for m in range(6)])
                    if i == 0 and ex > 0:
                        value = value + dst[5 * ex, k]
                    dst[5 * ex + i, k] = value
        for x in range(NX):
            gy, gz, gm = GC[h, 0, x], GC[h, 1, x], GC[h, 2, x]
            vs = [src[x, m] for m in range(6)]
            for k in range(6):
                vk = vs[k]
                zterm = CT(0) * vk
                for sh in range(1, 8):
                    zterm = zterm + CT(sh) * pltpu.roll(vk, sh, 0)
                value = float(w[k]) * (gz * zterm + gm * vk)
                value = value + gy * mac([(float(k1[k, m]), vs[m]) for m in range(6)])
                dst[x, k] = dst[x, k] + value

    def fold_y(F):
        for x in range(NX):
            low, high = F[x, 0], F[x, 5]
            F[x, 0] = low + jnp.where(ey > 0, pltpu.roll(high, 1, 1), 0.0)
            F[x, 5] = high + jnp.where(ey < EY - 1, pltpu.roll(low, 127, 1), 0.0)

    def fold_z(F, both):
        for x in range(NX):
            z0, z5 = F[0, x, :, 0, :], F[0, x, :, 5, :]
            h0, h5 = F[1, x, :, 0, :], F[1, x, :, 5, :]
            z0_up, z5_up = pltpu.roll(z0, EY, 1), pltpu.roll(z5, EY, 1)
            z0_down, z5_down = pltpu.roll(z0, 128 - EY, 1), pltpu.roll(z5, 128 - EY, 1)
            h0_up, h5_up = pltpu.roll(h0, EY, 1), pltpu.roll(h5, EY, 1)
            h0_down, h5_down = pltpu.roll(h0, 128 - EY, 1), pltpu.roll(h5, 128 - EY, 1)
            F[0, x, :, 0, :] = z0 + jnp.where(lane6 < EY, h5_down, z5_up)
            F[0, x, :, 5, :] = z5 + jnp.where(lane6 >= 128 - EY, h0_up, z0_down)
            if both:
                add0 = jnp.where(group6 == 2, z5_down, h5_up)
                add5 = jnp.where(group6 == 1, z0_up, h0_down)
                F[1, x, :, 0, :] = h0 + jnp.where(group6 == 0, 0.0, add0)
                F[1, x, :, 5, :] = h5 + jnp.where(group6 == 3, 0.0, add5)

    def link(idx, slot_no, src, dst, device):
        return lambda: pltpu.make_async_remote_copy(
            src_ref=src,
            dst_ref=dst,
            send_sem=ex_send.at[idx, slot_no],
            recv_sem=ex_recv.at[idx, slot_no],
            device_id=device,
            device_id_type=MESH,
        )

    def x_links(idx):
        return [
            (has["xl"], has["xh"], link(idx, 1, xsend.at[idx, 0], xrecv.at[idx, 1], (b, s - 1))),
            (has["xh"], has["xl"], link(idx, 0, xsend.at[idx, 1], xrecv.at[idx, 0], (b, s + 1))),
        ]

    def z_links(idx):
        both = jnp.logical_and
        out = [
            (has["zl"], has["zh"], link(idx, 3, zsend.at[idx, 0], zrecv.at[idx, 1], (b - 1, s))),
            (has["zh"], has["zl"], link(idx, 2, zsend.at[idx, 1], zrecv.at[idx, 0], (b + 1, s))),
        ]
        for zs, db, zn, zr in ((0, -1, "zl", "zh"), (1, 1, "zh", "zl")):
            for xside, ds, xn, xr in ((0, -1, "xl", "xh"), (1, 1, "xh", "xl")):
                out.append(
                    (
                        both(has[zn], has[xn]),
                        both(has[zr], has[xr]),
                        link(
                            idx,
                            4 + 2 * (1 - zs) + (1 - xside),
                            zsend.at[idx, zs, (ZT - 1) * xside],
                            drecv.at[idx, 1 - zs, 1 - xside],
                            (b + db, s + ds),
                        ),
                    )
                )
        return out

    def halo_links(idx):
        def one(side, device):
            return lambda: pltpu.make_async_remote_copy(
                src_ref=bsend.at[idx, side],
                dst_ref=brecv.at[idx, 1 - side],
                send_sem=h_send.at[idx, side],
                recv_sem=h_recv.at[idx, 1 - side],
                device_id=device,
                device_id_type=MESH,
            )

        return [
            (has["zl"], has["zh"], one(0, (b - 1, s))),
            (has["zh"], has["zl"], one(1, (b + 1, s))),
        ]

    def links_start(links):
        for there, _, copy in links:

            @pl.when(there)
            def _(copy=copy):
                copy().start()

    def links_wait(links):
        for _, here, copy in links:

            @pl.when(here)
            def _(copy=copy):
                copy().wait_recv()

    def links_sent(links):
        for there, _, copy in links:

            @pl.when(there)
            def _(copy=copy):
                copy().wait_send()

    def x_start(idx, F):
        xsend[idx, 0] = F[0]
        xsend[idx, 1] = F[NX - 1]
        links_start(x_links(idx))

    def x_end(idx, F):
        links_wait(x_links(idx))
        F[0] = F[0] + xrecv[idx, 0]
        F[NX - 1] = F[NX - 1] + xrecv[idx, 1]

    def exchange_start(idx, F):
        fold_y(F)
        x_start(idx, F)
        for t in range(ZT):
            low = high = jnp.zeros((6, 128), F32)
            for m in range(4):
                x = 4 * t + m
                if x >= NX:
                    continue
                low = jnp.where(group6 == m, moved(F[x, :, 0, :], EY * m), low)
                high = jnp.where(group6 == m, moved(F[x, :, 5, :], EY * (m + 1)), high)
            zsend[idx, 0, t, 0:6, :] = low
            zsend[idx, 1, t, 0:6, :] = high
        links_start(z_links(idx))

    def inner_z(F):
        for x in range(NX):
            z0, z5 = F[x, :, 0, :], F[x, :, 5, :]
            F[x, :, 0, :] = z0 + jnp.where(lane6 < EY, 0.0, pltpu.roll(z5, EY, 1))
            F[x, :, 5, :] = z5 + jnp.where(
                lane6 >= 128 - EY, 0.0, pltpu.roll(z0, 128 - EY, 1)
            )

    def outer_z(idx, F):
        links_wait(z_links(idx))
        for x in range(NX):
            t, m = divmod(x, 4)
            near = moved(zrecv[idx, 0, t, 0:6, :], -EY * m)
            far = moved(zrecv[idx, 1, t, 0:6, :], 128 - EY - EY * m)
            if x == 0:
                near = near + moved(drecv[idx, 0, 0, 0:6, :], -EY * LAST)
                far = far + moved(drecv[idx, 1, 0, 0:6, :], 128 - EY - EY * LAST)
            if x == NX - 1:
                near = near + drecv[idx, 0, 1, 0:6, :]
                far = far + moved(drecv[idx, 1, 1, 0:6, :], 128 - EY)
            F[x, :, 0, :] = F[x, :, 0, :] + jnp.where(lane6 < EY, near, 0.0)
            F[x, :, 5, :] = F[x, :, 5, :] + jnp.where(lane6 >= 128 - EY, far, 0.0)

    def exchange_end(idx, F):
        x_end(idx, F)
        inner_z(F)
        outer_z(idx, F)

    def halo_start(idx, src):
        for t in range(ZT):
            for k in range(6):
                low = high = jnp.zeros((8, 128), F32)
                for m in range(4):
                    x = 4 * t + m
                    if x >= NX:
                        continue
                    tile = src(x, k)
                    low = jnp.where(group == m, moved(tile, EY * m), low)
                    high = jnp.where(group == m, moved(tile, EY * (m + 1)), high)
                bsend[idx, 0, t, k] = low
                bsend[idx, 1, t, k] = high

    def halo_unpack(idx, dst):
        for x in range(NX):
            t, m = divmod(x, 4)
            for k in range(6):
                low = moved(brecv[idx, 0, t, k], EY - EY * m)
                high = moved(brecv[idx, 1, t, k], 2 * EY - EY * m)
                dst[x, k] = jnp.where(group == 1, low, jnp.where(group == 2, high, 0.0))

    def window_copies(which, src, dst):
        out = []
        for off in range(-REACH, REACH + 1):
            for ds in range(n_sub):
                if off == 0 and ds == 0:
                    continue
                peer_s = lax.rem(s + ds, n_sub)
                target = b + off
                sending = jnp.logical_and(target >= 0, target < n_blk)

                def copy(off=off, ds=ds, peer_s=peer_s, target=target):
                    return pltpu.make_async_remote_copy(
                        src_ref=src,
                        dst_ref=dst.at[REACH - off, s],
                        send_sem=c_send.at[which, REACH + off, ds],
                        recv_sem=c_recv.at[which, REACH - off, s],
                        device_id=(target, peer_s),
                        device_id_type=MESH,
                    )

                def arrive(off=off, ds=ds, peer_s=peer_s, target=target):
                    return pltpu.make_async_remote_copy(
                        src_ref=src,
                        dst_ref=dst.at[REACH + off, peer_s],
                        send_sem=c_send.at[which, REACH + off, ds],
                        recv_sem=c_recv.at[which, REACH + off, peer_s],
                        device_id=(target, peer_s),
                        device_id_type=MESH,
                    )

                out.append((sending, copy, arrive))
        return out

    def window_start(which, src, dst):
        for sending, copy, _ in window_copies(which, src, dst):

            @pl.when(sending)
            def _(copy=copy):
                copy().start()

    def window_wait(which, src, dst):
        for sending, _, arrive in window_copies(which, src, dst):

            @pl.when(sending)
            def _(arrive=arrive):
                arrive().wait_recv()

    def window_sent(which, src, dst):
        for sending, copy, _ in window_copies(which, src, dst):

            @pl.when(sending)
            def _(copy=copy):
                copy().wait_send()

    def velocity(c):
        to_elements(vel_ref.at[c], VE, False)
        out = VV.at[c]
        rounded = lambda value: value.astype(BF16).astype(F32)
        for ex in range(EX):
            gx = SG[0, ex]
            for k in range(6):
                vs = [VE[5 * ex + m, k] for m in range(6)]
                flux = []
                for i in range(6):
                    grad = mac([(float(Dh[i, m]), vs[m]) for m in range(6)])
                    flux.append(rounded(grad * (WJ * float(w[i] * w[k])) * gx))
                for i in range(6):
                    value = mac([(float(Dh[m, i]), flux[m]) for m in range(6)])
                    if i == 0 and ex > 0:
                        value = value + out[5 * ex, k]
                    out[5 * ex + i, k] = value
        for ex in range(EX):
            gz, gy, gm = SG[1, ex], SG[2, ex], SG[3, ex]
            for i in range(6):
                x = 5 * ex + i
                vs = [VE[x, m] for m in range(6)]
                flux = []
                for k in range(6):
                    grad = mac([(float(Dh[k, m]), vs[m]) for m in range(6)])
                    flux.append(rounded(grad * (WJ * float(w[i] * w[k])) * gy))
                for k in range(6):
                    vk = vs[k]
                    weight = WJ * float(w[i] * w[k])
                    value = mac([(float(Dh[m, k]), flux[m]) for m in range(6)])
                    grad = tab_ref[8] * vk
                    for sh in range(1, 8):
                        grad = grad + tab_ref[8 + sh] * pltpu.roll(vk, sh, 0)
                    fz = rounded(grad * weight * gz)
                    value = value + tab_ref[16] * fz
                    for sh in range(1, 8):
                        value = value + tab_ref[16 + sh] * pltpu.roll(fz, sh, 0)
                    value = value + gm * weight * vk
                    out[x, k] = out[x, k] + value

    geometry(0, stack)
    fetch["load"].wait()
    fetch["pick"].wait()
    to_elements(load_ref, R.at[0], True)
    halo_start(0, lambda x, k: R[0, x, k])
    crecv[REACH, s] = stack
    fetch["vel"].wait()

    pl.semaphore_wait(barrier, n_dev - 1)

    window_start(0, csend, crecv)
    links_start(halo_links(0))
    def component(c, carry):
        velocity(c)
        exchange_start(c, VV.at[c])
        return carry

    lax.fori_loop(0, 3, component, 0)

    window_wait(0, csend, crecv)

    def beside(t):
        low, high = crecv[REACH - 1, t], crecv[REACH + 1, t]
        return jnp.where(lane < 2 * EY, pltpu.roll(low, 64, 1), pltpu.roll(high, 64, 1))

    left_s, right_s = jnp.maximum(s - 1, 0), jnp.minimum(s + 1, n_sub - 1)
    left_on = jnp.where(has["xl"], 1.0, 0.0)
    right_on = jnp.where(has["xh"], 1.0, 0.0)
    geometry(1, beside(s))
    face_geometry(0, (crecv[REACH, left_s] * left_on, crecv[REACH, right_s] * right_on))
    face_geometry(1, (beside(left_s) * left_on, beside(right_s) * right_on))
    for h in range(2):
        diagonal_part(h)
    fold_z(W, True)
    for h in range(2):
        fold_y(W.at[h])
    for h in range(2):
        for x in range(NX):
            for k in range(6):
                full = W[h, x, k]
                good = full > 0.0
                INV[h, x, k] = jnp.where(good, DAMPING / jnp.where(good, full, 1.0), 0.0)

    for o in range(SPAN):
        for t in range(n_sub):
            packed = crecv[o, t]
            for ez in range(EZ):
                if not ZLO - 1 <= EZ * o + ez <= ZHI:
                    continue
                tile = jnp.where(lane < EY, moved(packed, -EY * ez), 0.0)
                for q in range(4):
                    CF[EZ * o + ez + 1, q, EX * t : EX * t + EX, :] = tile[
                        EX * q : EX * q + EX, :
                    ]

    corners = [(a, c, d) for a in (0, 1) for c in (0, 1) for d in (0, 1)]

    def stencil(z, carry):
        shifted = {}
        for c in (0, 1):
            for q in range(4):
                base = CF[z + 1 - c, q]
                for a in (0, 1):
                    up = pltpu.roll(base, 1, 0) if a else base
                    shifted[a, c, 0, q] = up
                    shifted[a, c, 1, q] = pltpu.roll(up, 1, 1)
        total = {}
        for ui, u in enumerate(corners):
            for vi, v in enumerate(corners):
                key = tuple(v[t] - u[t] for t in range(3))
                term = mac([(float(coarse[q][ui, vi]), shifted[u + (q,)]) for q in range(4)])
                total[key] = term if key not in total else total[key] + term
        for key, value in total.items():
            ST[z, 9 * (key[0] + 1) + 3 * (key[1] + 1) + key[2] + 1] = value
        diag = total[0, 0, 0]
        ST[z, 27] = jnp.where(diag > 0.0, 1.0 / jnp.where(diag > 0.0, diag, 1.0), 0.0)
        return carry

    cut_a = ZLO + (ZHI + 1 - ZLO) // 3
    cut_b = ZLO + (ZHI + 1 - ZLO) * 2 // 3
    lax.fori_loop(ZLO, cut_a, stencil, 0)

    links_wait(halo_links(0))
    halo_unpack(0, R.at[1])
    for h in range(2):
        for x in range(NX):
            for k in range(6):
                V[h, x, k] = R[h, x, k] * INV[h, x, k]
        apply_part(h)
    fold_z(W, False)
    fold_y(W.at[0])
    x_start(5, W.at[0])
    x_end(5, W.at[0])
    for x in range(NX):
        for k in range(6):
            V[0, x, k] = V[0, x, k] + (R[0, x, k] - W[0, x, k]) * INV[0, x, k]
    apply_part(0)

    one = jnp.ones((8, 128), F32)
    wz = jnp.where(sub_i < 5, one, 0.0)
    wz = jnp.where(jnp.logical_and(sub_i == 5, lane >= 128 - EY), 1.0, wz)
    low_half = jnp.where(has["zl"], 0.5, 1.0)
    high_half = jnp.where(has["zh"], 0.5, 1.0)
    wz = wz * jnp.where(jnp.logical_and(sub_i == 0, lane < EY), low_half, 1.0)
    wz = wz * jnp.where(jnp.logical_and(sub_i == 5, lane >= 128 - EY), high_half, 1.0)
    wend = wz * jnp.where(ey == EY - 1, 1.0, 0.0)
    xlow = jnp.where(has["xl"], 0.5, 1.0)
    xhigh = jnp.where(has["xh"], 0.5, 1.0)

    def unique(x, k):
        tile = wz if k < 5 else wend
        if x == 0:
            tile = tile * xlow
        if x == NX - 1:
            tile = tile * xhigh
        return tile

    acc = [[None, None] for _ in range(EX + 1)]
    for x in range(NX):
        rows = [unique(x, k) * R[0, x, k] - W[0, x, k] for k in range(6)]
        lines = [mac([(float(lin[k, d]), rows[k]) for k in range(6)]) for d in (0, 1)]
        ex = min(x // 5, EX - 1)
        i = x - 5 * ex
        for a in (0, 1):
            weight = float(lin[i, a])
            if weight == 0.0:
                continue
            for d in (0, 1):
                term = weight * lines[d]
                old = acc[ex + a][d]
                acc[ex + a][d] = term if old is None else old + term
    pieces = {}
    for c in (0, 1):
        for d in (0, 1):
            tile = jnp.zeros((8, 128), F32)
            for xv in range(EX + 1):
                row = jnp.sum(LJ[c] * acc[xv][d], axis=0, keepdims=True)
                tile = jnp.where(sub_i == xv, jnp.broadcast_to(row, (8, 128)), tile)
            pieces[c, d] = tile
    placed = [None] * (EZ + 1)
    for c in (0, 1):
        for ez in range(EZ):
            sums = None
            for d in (0, 1):
                tile = jnp.where(lane < EY, moved(pieces[c, d], -EY * ez), 0.0)
                if d:
                    tile = pltpu.roll(tile, 1, 1)
                sums = tile if sums is None else sums + tile
            old = placed[ez + c]
            placed[ez + c] = sums if old is None else old + sums
    message = placed[0]
    for zv in range(1, EZ + 1):
        rows_at, lanes_at = divmod(zv, 3)
        tile = moved(placed[zv], (EY + 8) * lanes_at)
        if rows_at:
            tile = pltpu.roll(tile, (EX + 1) * rows_at, 0)
        message = message + tile
    rsend[...] = message
    rrecv[REACH, s] = message
    window_start(1, rsend, rrecv)

    exchange_start(3, W.at[0])
    lax.fori_loop(cut_a, cut_b, stencil, 0)
    x_end(3, W.at[0])
    inner_z(W.at[0])
    halo_start(1, lambda x, k: V[0, x, k] + (R[0, x, k] - W[0, x, k]) * INV[0, x, k])
    links_start(halo_links(1))
    lax.fori_loop(cut_b, ZHI + 1, stencil, 0)
    outer_z(3, W.at[0])
    for x in range(NX):
        for k in range(6):
            V[0, x, k] = V[0, x, k] + (R[0, x, k] - W[0, x, k]) * INV[0, x, k]

    window_wait(1, rsend, rrecv)

    def window_sum(o, zv):
        rows_at, lanes_at = divmod(zv, 3)
        total = None
        for t in range(n_sub):
            tile = moved(rrecv[o, t], -(EY + 8) * lanes_at)
            here = jnp.logical_and(
                sub_i >= (EX + 1) * rows_at, sub_i < (EX + 1) * (rows_at + 1)
            )
            tile = jnp.where(jnp.logical_and(here, lane <= EY), tile, 0.0)
            if xs > 8:
                tile = jnp.concatenate([tile, jnp.zeros((xs - 8, 128), F32)], axis=0)
            shift = (EX * t - (EX + 1) * rows_at) % xs
            if shift:
                tile = pltpu.roll(tile, shift, 0)
            total = tile if total is None else total + tile
        return total

    center = (SPECTRUM_HIGH + SPECTRUM_LOW) / 2.0
    radius = (SPECTRUM_HIGH - SPECTRUM_LOW) / 2.0
    ratio = center / radius
    factor = 1.0 / ratio
    for z in range(ZLO, ZHI + 1):
        o, zv = divmod(z, EZ)
        value = window_sum(o, zv)
        if zv == 0 and o > 0:
            value = value + window_sum(o - 1, EZ)
        CR[z] = value
        CU[0, z] = value * ST[z, 27] * (1.0 / center)
    first, last = FIRST - HALO, LAST_V + HALO
    sol = {z: CU[0, z] for z in range(first, last + 1)}
    for sweep in range(CHEB_ITERS - 1):
        now, later = sweep % 2, (sweep + 1) % 2
        left = CHEB_ITERS - 2 - sweep
        nxt = 1.0 / (2.0 * ratio - factor)
        wide = {}
        for z in range(first - left, last + left + 1):
            for zz in (z - 1, z, z + 1):
                if zz in wide:
                    continue
                base = CU[now, zz]
                sides = {}
                for dx in (-1, 0, 1):
                    mx = base if dx == 0 else pltpu.roll(base, (-dx) % xs, 0)
                    for dy in (-1, 0, 1):
                        sides[dx, dy] = mx if dy == 0 else pltpu.roll(mx, (-dy) % 128, 1)
                wide[zz] = sides
            total = None
            for dz in (-1, 0, 1):
                for dx in (-1, 0, 1):
                    for dy in (-1, 0, 1):
                        term = ST[z, 9 * (dx + 1) + 3 * (dz + 1) + dy + 1] * wide[z + dz][dx, dy]
                        total = term if total is None else total + term
            residual = CR[z] - total
            CR[z] = residual
            fresh = (nxt * factor) * CU[now, z] + (2.0 * nxt / radius) * (residual * ST[z, 27])
            CU[later, z] = fresh
            if first <= z <= last:
                sol[z] = sol[z] + fresh
        factor = nxt

    own = {}
    for z, tile in sol.items():
        shifted_x = tile
        for t in range(1, n_sub):
            shifted_x = jnp.where(s == t, pltpu.roll(tile, (-EX * t) % xs, 0), shifted_x)
        own[z - FIRST] = shifted_x

    links_wait(halo_links(1))
    halo_unpack(1, V.at[1])
    for x in range(NX):
        z0, z5 = V[0, x, :, 0, :], V[0, x, :, 5, :]
        V[1, x, :, 5, :] = jnp.where(
            group6 == 1, pltpu.roll(z0, EY, 1), V[1, x, :, 5, :]
        )
        V[1, x, :, 0, :] = jnp.where(
            group6 == 2, pltpu.roll(z5, 128 - EY, 1), V[1, x, :, 0, :]
        )

    ZJ = tab_ref[28]
    for h in range(2):
        places = range(EZ) if h == 0 else (-2, -1, EZ, EZ + 1)
        corner_tiles = {}
        for c in (0, 1):
            for d in (0, 1):
                total = None
                for at, ez in enumerate(places):
                    tile = own[ez + c]
                    if d:
                        tile = pltpu.roll(tile, 127, 1)
                    tile = moved(jnp.where(lane[0:1] < EY, tile, 0.0), EY * at)
                    total = tile if total is None else total + tile
                corner_tiles[c, d] = total
        val, zdif, ydif = {}, {}, {}
        for xv in range(-1, EX + 2):
            at = xv % xs
            rows = {
                key: jnp.broadcast_to(tile[at : at + 1, :], (8, 128))
                for key, tile in corner_tiles.items()
            }
            ends = [LJ[0] * rows[0, d] + LJ[1] * rows[1, d] for d in (0, 1)]
            val[xv] = [mac([(float(lin[k, d]), ends[d]) for d in (0, 1)]) for k in range(6)]
            if 0 <= xv <= EX:
                jump = [ZJ * (rows[0, d] - rows[1, d]) for d in (0, 1)]
                zdif[xv] = [
                    mac([(float(lin[k, d]), jump[d]) for d in (0, 1)]) for k in range(6)
                ]
                ydif[xv] = 0.5 * (ends[0] - ends[1])
        for x in range(NX):
            ex = min(x // 5, EX - 1)
            i = x - 5 * ex
            parts = [(float(lin[i, a]), ex + a) for a in (0, 1)]
            gy, gz, gm = whole_geometry(h, x)
            slope = gy * mac([(weight, ydif[xv]) for weight, xv in parts])
            for k in range(6):
                u = mac([(weight, val[xv][k]) for weight, xv in parts])
                inside = gz * mac([(weight, zdif[xv][k]) for weight, xv in parts]) + gm * u
                if x % 5 == 0:
                    xv = x // 5
                    inside = inside + GX[h, xv] * (0.5 * (val[xv][k] - val[xv - 1][k]))
                    inside = inside + GX[h, xv + 1] * (0.5 * (val[xv][k] - val[xv + 1][k]))
                value = float(w[k]) * inside
                if k == 0:
                    value = value + slope
                if k == 5:
                    value = value - slope
                W[h, x, k] = value
                V[h, x, k] = V[h, x, k] + u
    fold_z(W, True)
    for h in range(2):
        fold_y(W.at[h])
    for h in range(2):
        for x in range(NX):
            for k in range(6):
                V[h, x, k] = V[h, x, k] - W[h, x, k] * INV[h, x, k]
        apply_part(h)
    fold_z(W, False)
    fold_y(W.at[0])
    x_start(6, W.at[0])
    x_end(6, W.at[0])
    for x in range(NX):
        for k in range(6):
            V[0, x, k] = V[0, x, k] + (R[0, x, k] - W[0, x, k]) * INV[0, x, k]
    apply_part(0)
    num = jnp.zeros((8, 128), F32)
    den = jnp.zeros((8, 128), F32)
    for x in range(NX):
        for k in range(6):
            v = V[0, x, k]
            num = num + unique(x, k) * R[0, x, k] * v
            den = den + v * W[0, x, k]
    num_row = jnp.sum(num, axis=0, keepdims=True)
    den_row = jnp.sum(den, axis=0, keepdims=True)
    num_one = jnp.sum(num_row, axis=1, keepdims=True)
    den_one = jnp.sum(den_row, axis=1, keepdims=True)
    lane1 = lax.broadcasted_iota(jnp.int32, (1, 128), 1)
    psend[...] = jnp.where(lane1 < 64, num_one, den_one)

    def scatter(d, carry):
        pltpu.make_async_remote_copy(
            src_ref=psend,
            dst_ref=precv.at[d - 1],
            send_sem=p_sem.at[0],
            recv_sem=p_sem.at[1],
            device_id=device_of(lax.rem(me + d, n_dev)),
            device_id_type=MESH,
        ).start()
        return carry

    lax.fori_loop(1, n_dev, scatter, 0)
    exchange_start(4, W.at[0])
    fetch["put"].wait()
    to_nodes(V.at[0], pres_ref)
    for c in range(3):
        exchange_end(c, VV.at[c])
        to_nodes(VV.at[c], velout_ref.at[c])
    exchange_end(4, W.at[0])
    to_nodes(W.at[0], res_ref)
    whole = pltpu.make_async_remote_copy(
        src_ref=precv,
        dst_ref=precv,
        send_sem=p_sem.at[0],
        recv_sem=p_sem.at[1],
        device_id=(b, s),
        device_id_type=MESH,
    )
    whole.wait_recv()
    both = psend[...] + jnp.sum(precv[...], axis=0)
    step = both[0:1, 0:1] / both[0:1, 64:65]
    for x in range(NX):
        pres_ref[x] = step * pres_ref[x]
        res_ref[x] = load_ref[x] - step * res_ref[x]
    whole.wait_send()
    for idx in range(5):
        links_sent(x_links(idx) + z_links(idx))
    for idx in range(5, EXCH):
        links_sent(x_links(idx))
    for idx in range(2):
        links_sent(halo_links(idx))
    window_sent(0, csend, crecv)
    window_sent(1, rsend, rrecv)


def solution(mesh):
    n_blk, n_sub = mesh.shape["blk"], mesh.shape["sub"]
    n_dev = n_blk * n_sub
    xs = -(-(EX * n_sub + 2) // 8) * 8
    D, w, k1, lin, coarse = tables()
    Dh = bf16_round(D)
    tab = np.concatenate(
        [
            roll_tables(k1),
            roll_tables(Dh),
            roll_tables(Dh.T),
            col_tile(w),
            col_tile(lin[:, 0]),
            col_tile(lin[:, 1]),
            col_tile(np.diag(k1)),
            col_tile([0.5, 0.0, 0.0, 0.0, 0.0, -0.5]),
        ]
    )
    pick, put = pick_matrices()

    def per_device(velocity, pressure_load, local_map, stiff_geo, mass_geo):
        vm = pl.BlockSpec(memory_space=pltpu.VMEM)
        field = (NX, 6, 8, 128)
        out = pl.pallas_call(
            functools.partial(kernel, n_blk, n_sub, xs),
            out_shape=(
                jax.ShapeDtypeStruct((3, NX, NZ, NY), F32),
                jax.ShapeDtypeStruct((NX, NZ, NY), F32),
                jax.ShapeDtypeStruct((NX, NZ, NY), F32),
            ),
            in_specs=[pl.BlockSpec(memory_space=pl.ANY)] * 8,
            out_specs=(vm, vm, vm),
            scratch_shapes=[
                pltpu.VMEM((3, NX, NZ, NY), F32),
                pltpu.VMEM((NX, NZ, NY), F32),
                pltpu.VMEM((3, EX * EZ * EY), F32),
                pltpu.VMEM((1, EX * EZ * EY), F32),
                pltpu.VMEM(tab.shape, F32),
                pltpu.VMEM(pick.shape, BF16),
                pltpu.VMEM(put.shape, BF16),
                pltpu.VMEM((2,) + field, F32),
                pltpu.VMEM((2,) + field, F32),
                pltpu.VMEM((NX, NZP, NYP), F32),
                pltpu.VMEM((8, EX * EZ * EY), jnp.int32),
                pltpu.VMEM((2,) + field, F32),
                pltpu.VMEM((2,) + field, F32),
                pltpu.VMEM((3,) + field, F32),
                pltpu.VMEM(field, F32),
                pltpu.VMEM((2, EX + 2, 8, 128), F32),
                pltpu.VMEM((2, 3, NX, 8, 128), F32),
                pltpu.VMEM((2, 2, 3, 8, 128), F32),
                pltpu.VMEM((4, EX, 8, 128), F32),
                pltpu.VMEM((EXCH, 2, 6, 8, 128), F32),
                pltpu.VMEM((EXCH, 2, 6, 8, 128), F32),
                pltpu.VMEM((EXCH, 2, ZT, 8, 128), F32),
                pltpu.VMEM((EXCH, 2, ZT, 8, 128), F32),
                pltpu.VMEM((EXCH, 2, 2, 8, 128), F32),
                pltpu.VMEM((8, 128), F32),
                pltpu.VMEM((SPAN, n_sub, 8, 128), F32),
                pltpu.VMEM((8, 128), F32),
                pltpu.VMEM((SPAN, n_sub, 8, 128), F32),
                pltpu.VMEM((2, 2, ZT, 6, 8, 128), F32),
                pltpu.VMEM((2, 2, ZT, 6, 8, 128), F32),
                pltpu.VMEM((NZV + 1, 4, xs, 128), F32),
                pltpu.VMEM((NZV, 28, xs, 128), F32),
                pltpu.VMEM((2, NZV, xs, 128), F32),
                pltpu.VMEM((NZV, xs, 128), F32),
                pltpu.VMEM((1, 128), F32),
                pltpu.VMEM((n_dev - 1, 1, 128), F32),
                pltpu.SemaphoreType.DMA((EXCH, 8)),
                pltpu.SemaphoreType.DMA((EXCH, 8)),
                pltpu.SemaphoreType.DMA((2, SPAN, n_sub)),
                pltpu.SemaphoreType.DMA((2, SPAN, n_sub)),
                pltpu.SemaphoreType.DMA((2, 2)),
                pltpu.SemaphoreType.DMA((2, 2)),
                pltpu.SemaphoreType.DMA((2,)),
                pltpu.SemaphoreType.DMA((8,)),
            ],
            compiler_params=pltpu.CompilerParams(
                collective_id=0, has_side_effects=True, vmem_limit_bytes=60 << 20
            ),
        )(
            velocity.reshape(3, NX, NZ, NY),
            pressure_load.reshape(NX, NZ, NY),
            local_map,
            stiff_geo,
            mass_geo.reshape(1, mass_geo.shape[0]),
            jnp.asarray(tab, F32),
            jnp.asarray(pick, BF16),
            jnp.asarray(put, BF16),
        )
        return (out[0].reshape(3, NLOC), out[1].reshape(NLOC), out[2].reshape(NLOC))

    in_specs = (
        P(None, ("blk", "sub")),
        P(("blk", "sub")),
        P(None, ("blk", "sub")),
        P(None, ("blk", "sub")),
        P(("blk", "sub")),
    )
    out_specs = (P(None, ("blk", "sub")), P(("blk", "sub")), P(("blk", "sub")))
    return jax.shard_map(
        per_device, mesh=mesh, in_specs=in_specs, out_specs=out_specs, check_vma=False
    )
```

```python
import functools
import math

import jax
import jax.numpy as jnp
import numpy as np
from jax import lax
from jax.experimental import pallas as pl
from jax.experimental.pallas import tpu as pltpu
from jax.sharding import PartitionSpec as P

EX = 2
EZ = 4
EY = 32
CHEB_ITERS = 8
NX = 5 * EX + 1
NZ = 5 * EZ + 1
NY = 5 * EY + 1
NLOC = NX * NZ * NY
NZP = 24
NYP = 256
HALO = 2
DEPTH = CHEB_ITERS - 1 + HALO
REACH = -(-DEPTH // EZ)
SPAN = 2 * REACH + 1
NZV = SPAN * EZ + 1
FIRST = REACH * EZ
LAST_V = FIRST + EZ
ZLO = FIRST - DEPTH
ZHI = LAST_V + DEPTH
EXCH = 7
ZT = -(-NX // 4)
ROWS = NX * NZ
IN_STEP = next(k for k in range(1, 129) if NY * k % 128 == 127)
IN_SKIP = (NY * IN_STEP + 1) // 128
IN_ROWS = 8 * IN_STEP
OUT_STEP, OUT_SKIP = next(
    (r, p) for r in range(1, 129) for p in (NY * r // 128,) if 0 < NY * r - 128 * p <= 4
)
OUT_DRIFT = NY * OUT_STEP - 128 * OUT_SKIP
FLAT = -(-NLOC // 128)
FULL = NLOC // 1024
PAD = 8
LAST = (NX - 1) % 4

DAMPING = 0.3
MASS_SHARE = 0.05
SPECTRUM_LOW = 0.15
SPECTRUM_HIGH = 4.5
MESH = pl.DeviceIdType.MESH
F32 = jnp.float32
BF16 = jnp.bfloat16


def tables():
    seven_root = math.sqrt(7.0)
    inner = math.sqrt(1.0 / 3.0 - 2.0 * seven_root / 21.0)
    outer = math.sqrt(1.0 / 3.0 + 2.0 * seven_root / 21.0)
    xi = np.array([-1.0, -outer, -inner, inner, outer, 1.0])
    leg = (63.0 * xi**5 - 70.0 * xi**3 + 15.0 * xi) / 8.0
    w = 2.0 / (30.0 * leg**2)
    D = np.zeros((6, 6))
    for i in range(6):
        for j in range(6):
            if i != j:
                D[i, j] = leg[i] / (leg[j] * (xi[i] - xi[j]))
    D[0, 0] = -7.5
    D[5, 5] = 7.5
    k1 = D.T @ (w[:, None] * D)
    lin = np.stack([(1.0 - xi) / 2.0, (1.0 + xi) / 2.0], 1)
    kc = lin.T @ k1 @ lin
    mc = lin.T @ (w[:, None] * lin)
    coarse = [
        np.kron(np.kron(kc, mc), mc),
        np.kron(np.kron(mc, kc), mc),
        np.kron(np.kron(mc, mc), kc),
        MASS_SHARE * np.kron(np.kron(mc, mc), mc),
    ]
    return D, w, k1, lin, coarse


def roll_tables(M):
    out = np.zeros((8, 8, 128), np.float32)
    for s in range(8):
        for j in range(6):
            m = (j - s) % 8
            if m < 6:
                out[s, j, :] = M[j, m]
    return out


def col_tile(values):
    tile = np.zeros((1, 8, 128), np.float32)
    tile[0, :6, :] = np.asarray(values)[:, None]
    return tile


def bf16_round(a):
    return np.asarray(a, np.float32).astype(np.dtype(BF16)).astype(np.float64)


def pick_matrices():
    pick = np.zeros((NYP, 6, 128), np.float32)
    put = np.zeros((6, 128, NYP), np.float32)
    for k in range(6):
        for z in range(EZ):
            for e in range(EY):
                pick[5 * e + k, k, z * EY + e] = 1.0
                if k < 5 or e == EY - 1:
                    put[k, z * EY + e, 5 * e + k] = 1.0
    return pick.reshape(NYP, 768), put.reshape(768, NYP)


def mac(pairs):
    total = None
    for coef, value in pairs:
        if isinstance(coef, (float, int)) and coef == 0.0:
            continue
        term = coef * value
        total = term if total is None else total + term
    return total


def kernel(
    n_blk,
    n_sub,
    xs,
    vel_hbm,
    load_hbm,
    map_hbm,
    stiff_hbm,
    mass_hbm,
    tab_hbm,
    pick_hbm,
    put_hbm,
    velout_hbm,
    pres_hbm,
    res_hbm,
    vel_flat,
    load_flat,
    vel_back,
    pres_back,
    res_back,
    FL,
    FI,
    FP,
    FR,
    S0,
    S1,
    Y0,
    Y1,
    stiff_ref,
    mass_ref,
    tab_ref,
    pick_ref,
    put_ref,
    V,
    W,
    map_ref,
    R,
    INV,
    VV,
    VE,
    GX,
    GC,
    GE,
    SG,
    xsend,
    xrecv,
    zsend,
    zrecv,
    drecv,
    csend,
    crecv,
    rsend,
    rrecv,
    bsend,
    brecv,
    CF,
    ST,
    CU,
    CR,
    psend,
    precv,
    ex_send,
    ex_recv,
    c_send,
    c_recv,
    h_send,
    h_recv,
    p_sem,
    in_sem,
    out_sem,
):
    D, w, k1, lin, coarse = tables()
    Dh = bf16_round(D)
    n_dev = n_blk * n_sub
    b = lax.axis_index("blk")
    s = lax.axis_index("sub")
    me = b * n_sub + s

    def device_of(linear):
        return (linear // n_sub, lax.rem(linear, n_sub))

    barrier = pltpu.get_barrier_semaphore()

    def greet(d, carry):
        pl.semaphore_signal(
            barrier, inc=1, device_id=device_of(lax.rem(me + d, n_dev)), device_id_type=MESH
        )
        return carry

    lax.fori_loop(1, n_dev, greet, 0)

    fetch = {}
    for at, (name, src, dst) in enumerate(
        (
            ("map", map_hbm.at[0:8, :], map_ref),
            ("stiff", stiff_hbm, stiff_ref),
            ("mass", mass_hbm, mass_ref),
            ("tab", tab_hbm, tab_ref),
            ("load", load_hbm, load_flat),
            ("pick", pick_hbm, pick_ref),
            ("vel0", vel_hbm.at[0:1], vel_flat.at[0]),
            ("vel1", vel_hbm.at[1:2], vel_flat.at[1]),
            ("vel2", vel_hbm.at[2:3], vel_flat.at[2]),
            ("put", put_hbm, put_ref),
        )
    ):
        fetch[name] = pltpu.make_async_copy(src, dst, in_sem.at[at])
        fetch[name].start()

    has = {
        "xl": s > 0,
        "xh": s < n_sub - 1,
        "zl": b > 0,
        "zh": b < n_blk - 1,
    }

    def zero(ref_slice):
        ref_slice[...] = jnp.zeros(ref_slice.shape, F32)

    for side, name in ((0, "xl"), (1, "xh")):

        @pl.when(jnp.logical_not(has[name]))
        def _(side=side):
            zero(xrecv.at[:, side])

    for side, name in ((0, "zl"), (1, "zh")):

        @pl.when(jnp.logical_not(has[name]))
        def _(side=side):
            zero(zrecv.at[:, side])
            zero(brecv.at[:, side])

    for zs, zname in ((0, "zl"), (1, "zh")):
        for xside, xname in ((0, "xl"), (1, "xh")):

            @pl.when(jnp.logical_not(jnp.logical_and(has[zname], has[xname])))
            def _(zs=zs, xside=xside):
                zero(drecv.at[:, zs, xside])

    for o in range(SPAN):
        off = o - REACH

        @pl.when(jnp.logical_or(b + off < 0, b + off >= n_blk))
        def _(o=o):
            zero(crecv.at[o])
            zero(rrecv.at[o])

    CF[...] = jnp.zeros(CF.shape, F32)

    lane = lax.broadcasted_iota(jnp.int32, (8, 128), 1)
    sub_i = lax.broadcasted_iota(jnp.int32, (8, 128), 0)
    lane88 = lax.broadcasted_iota(jnp.int32, (8 * NX, 768), 1) // EY % EZ
    row88 = lax.broadcasted_iota(jnp.int32, (8 * NX, 768), 0) % 8
    ey = lane % EY
    lane6 = lax.broadcasted_iota(jnp.int32, (6, 128), 1)
    group6 = lane6 // EY
    group = lane // EY
    CT = lambda q: tab_ref[q]

    def moved(tile, shift):
        return tile if shift % 128 == 0 else pltpu.roll(tile, shift % 128, 1)

    slant_in = lane - sub_i
    slant_out = lane - OUT_DRIFT * sub_i

    def spin(tile, shift, stride):
        shift = shift % 128
        if shift + 7 * stride > 128:
            tile, shift = pltpu.roll(tile, shift, 1), 0
        return pltpu.roll(tile, shift, 1, stride=stride, stride_axis=0)

    chunks = [(8 * i, 8, 1024) for i in range(FULL)]
    chunks += [(p, 1, min(128, NLOC - 128 * p)) for p in range(8 * FULL, FLAT)]

    def unpack_flat(source, dest):
        for p, n, size in chunks:
            dest[PAD + p : PAD + p + n, 0 : size // n] = source(
                pl.ds(128 * p, size)
            ).reshape(n, size // n)

    def pack_flat(tile, store):
        for p, n, size in chunks:
            store(pl.ds(128 * p, size), tile(p, n)[:, 0 : size // n])

    def flat_to_rows(flat):
        for r in range(IN_STEP):
            q, at = divmod(NY * r, 128)
            if at < 7:
                q, at = q - 1, at + 128
            a, b_, c = (
                spin(flat[pl.ds(PAD + q + n, 8, stride=IN_SKIP), :], -at, 1) for n in range(3)
            )
            first_part = slant_in < 128 - at
            if at > 128:
                b_low = jnp.where(slant_in < 256 - at, b_, c)
            else:
                b_low = b_
            S0[pl.ds(r, 8, stride=IN_STEP), :] = jnp.where(first_part, a, b_low)
            S1[pl.ds(r, 8, stride=IN_STEP), :] = jnp.where(
                lane < NY - 128, jnp.where(first_part, b_, c), 0.0
            )

    def rows_to_flat(dest):
        for block in range(0, FLAT, 8 * OUT_SKIP):
            for step in range(OUT_SKIP):
                p = block + step
                if p >= FLAT:
                    continue
                r, y = divmod(128 * p, NY)
                if y < 7 * OUT_DRIFT:
                    r, y = r - 1, y + NY

                def piece(ref, row, turn):
                    return spin(
                        ref[pl.ds(PAD + row, 8, stride=OUT_STEP), :], turn, OUT_DRIFT
                    )

                value = piece(Y1, r, -y)
                if y - 7 * OUT_DRIFT < 128:
                    value = jnp.where(slant_out < 128 - y, piece(Y0, r, -y), value)
                if y + 127 >= NY:
                    after = piece(Y0, r + 1, NY - y)
                    if y + 127 >= NY + 128:
                        after = jnp.where(
                            slant_out < NY + 128 - y, after, piece(Y1, r + 1, NY - y)
                        )
                    value = jnp.where(slant_out < NY - y, value, after)
                dest[pl.ds(PAD + p, 8, stride=OUT_SKIP), :] = value

    def to_elements(flat, dest, exact):
        flat_to_rows(flat)
        rows = jnp.concatenate(
            [
                jnp.concatenate(
                    [S0[pl.ds(NZ * x + 5 * ez, 8), :], S1[pl.ds(NZ * x + 5 * ez, 8), :]], axis=1
                )
                for ez in range(EZ)
                for x in range(NX)
            ],
            axis=0,
        )
        hi = rows.astype(BF16)
        got = jnp.dot(hi, pick_ref[...], preferred_element_type=F32)
        if exact:
            lo = (rows - hi.astype(F32)).astype(BF16)
            got = got + jnp.dot(lo, pick_ref[...], preferred_element_type=F32)
        result = jnp.zeros((8 * NX, 768), F32)
        for ez in range(EZ):
            piece = got[8 * NX * ez : 8 * NX * (ez + 1)]
            result = jnp.where(jnp.logical_and(lane88 == ez, row88 < 6), piece, result)
        for k in range(6):
            dest[:, k] = result[:, 128 * k : 128 * k + 128].reshape(NX, 8, 128)

    def to_nodes(source, dest):
        full = jnp.concatenate([source[:, k].reshape(8 * NX, 128) for k in range(6)], axis=1)
        hi = full.astype(BF16).astype(F32)
        lo = full - hi
        his = [jnp.where(lane88 == ez, hi, 0.0) for ez in range(EZ)]
        los = [jnp.where(lane88 == ez, lo, 0.0) for ez in range(EZ)]
        got = jnp.dot(
            jnp.concatenate(his, axis=0).astype(BF16), put_ref[...], preferred_element_type=F32
        ) + jnp.dot(
            jnp.concatenate(los, axis=0).astype(BF16), put_ref[...], preferred_element_type=F32
        )
        for ez in range(EZ):
            for x in range(NX):
                at = 8 * NX * ez + 8 * x
                row = PAD + NZ * x + 5 * ez
                Y0[row : row + 6, :] = got[at : at + 6, 0:128]
                Y1[row : row + 6, :] = got[at : at + 6, 128:256]
        rows_to_flat(dest)

    for name in ("map", "stiff", "mass", "tab"):
        fetch[name].wait()
    WJ = tab_ref[24]
    LJ = (tab_ref[25], tab_ref[26])
    corner = map_ref[0:1, :]
    slot = (corner // (NZ * NY) // 5 * EZ + corner // NY % NZ // 5) * EY + corner % NY // 5
    count = EX * EZ * EY
    hot = (
        lax.broadcasted_iota(jnp.int32, (count, count), 0)
        == jnp.broadcast_to(slot, (count, count))
    ).astype(F32)
    geo = jnp.concatenate(
        [stiff_ref[...], mass_ref[...], jnp.zeros((4, count), F32)], axis=0
    )
    part_hi = geo.astype(BF16).astype(F32)
    part_mid = (geo - part_hi).astype(BF16).astype(F32)
    part_lo = geo - part_hi - part_mid
    pack = jnp.concatenate([part_hi, part_mid, part_lo], axis=0).astype(BF16)
    got = lax.dot_general(
        pack, hot.astype(BF16), (((1,), (1,)), ((), ())), preferred_element_type=F32
    )
    sorted_geo = got[0:8] + got[8:16] + got[16:24]
    stack = jnp.zeros((8, 128), F32)
    for q in range(4):
        for ex in range(EX):
            row = jnp.broadcast_to(
                sorted_geo[q : q + 1, 128 * ex : 128 * ex + 128], (8, 128)
            )
            SG[q, ex] = row
            stack = jnp.where(sub_i == EX * q + ex, row, stack)
    csend[...] = stack

    def geometry(h, tile):
        g = [
            [
                jnp.broadcast_to(tile[EX * q + ex : EX * q + ex + 1, :], (8, 128))
                for ex in range(EX)
            ]
            for q in range(4)
        ]
        for ex in range(EX):
            GX[h, 1 + ex] = WJ * g[0][ex]
        for x in range(NX):
            share = [(ex, x - 5 * ex) for ex in range(EX) if 0 <= x - 5 * ex <= 5]
            GC[h, 0, x] = WJ * mac([(float(w[i]), g[2][ex]) for ex, i in share])
            GC[h, 1, x] = mac([(float(w[i]), g[1][ex]) for ex, i in share])
            GC[h, 2, x] = WJ * mac([(float(MASS_SHARE * w[i]), g[3][ex]) for ex, i in share])

    def face_geometry(h, tiles):
        for face, (tile, ex) in enumerate(zip(tiles, (EX - 1, 0))):
            g = [
                jnp.broadcast_to(tile[EX * q + ex : EX * q + ex + 1, :], (8, 128))
                for q in range(4)
            ]
            x = (NX - 1) * face
            GX[h, (EX + 1) * face] = WJ * g[0]
            GE[h, face, 0] = GC[h, 0, x] + WJ * (float(w[0]) * g[2])
            GE[h, face, 1] = GC[h, 1, x] + float(w[0]) * g[1]
            GE[h, face, 2] = GC[h, 2, x] + WJ * (float(MASS_SHARE * w[0]) * g[3])

    def whole_geometry(h, x):
        if x == 0:
            return tuple(GE[h, 0, q] for q in range(3))
        if x == NX - 1:
            return tuple(GE[h, 1, q] for q in range(3))
        return tuple(GC[h, q, x] for q in range(3))

    def diagonal_part(h):
        kj = tab_ref[27]
        for x in range(NX):
            share = [
                (ex, x - 5 * ex) for ex in range(-1, EX + 1) if 0 <= x - 5 * ex <= 5
            ]
            gx = mac([(float(k1[i, i]), GX[h, 1 + ex]) for ex, i in share])
            gy, gz, gm = whole_geometry(h, x)
            base = gx + gz * kj + gm
            for k in range(6):
                W[h, x, k] = float(w[k]) * base + float(k1[k, k]) * gy

    def apply_part(h):
        src, dst = V.at[h], W.at[h]
        for ex in range(EX):
            gx = GX[h, 1 + ex]
            for k in range(6):
                vs = [src[5 * ex + m, k] for m in range(6)]
                gk = float(w[k]) * gx
                for i in range(6):
                    value = gk * mac([(float(k1[i, m]), vs[m]) for m in range(6)])
                    if i == 0 and ex > 0:
                        value = value + dst[5 * ex, k]
                    dst[5 * ex + i, k] = value
        for x in range(NX):
            gy, gz, gm = GC[h, 0, x], GC[h, 1, x], GC[h, 2, x]
            vs = [src[x, m] for m in range(6)]
            for k in range(6):
                vk = vs[k]
                zterm = CT(0) * vk
                for sh in range(1, 8):
                    zterm = zterm + CT(sh) * pltpu.roll(vk, sh, 0)
                value = float(w[k]) * (gz * zterm + gm * vk)
                value = value + gy * mac([(float(k1[k, m]), vs[m]) for m in range(6)])
                dst[x, k] = dst[x, k] + value

    def fold_y(F):
        for x in range(NX):
            low, high = F[x, 0], F[x, 5]
            F[x, 0] = low + jnp.where(ey > 0, pltpu.roll(high, 1, 1), 0.0)
            F[x, 5] = high + jnp.where(ey < EY - 1, pltpu.roll(low, 127, 1), 0.0)

    def fold_z(F, both):
        for x in range(NX):
            z0, z5 = F[0, x, :, 0, :], F[0, x, :, 5, :]
            h0, h5 = F[1, x, :, 0, :], F[1, x, :, 5, :]
            z0_up, z5_up = pltpu.roll(z0, EY, 1), pltpu.roll(z5, EY, 1)
            z0_down, z5_down = pltpu.roll(z0, 128 - EY, 1), pltpu.roll(z5, 128 - EY, 1)
            h0_up, h5_up = pltpu.roll(h0, EY, 1), pltpu.roll(h5, EY, 1)
            h0_down, h5_down = pltpu.roll(h0, 128 - EY, 1), pltpu.roll(h5, 128 - EY, 1)
            F[0, x, :, 0, :] = z0 + jnp.where(lane6 < EY, h5_down, z5_up)
            F[0, x, :, 5, :] = z5 + jnp.where(lane6 >= 128 - EY, h0_up, z0_down)
            if both:
                add0 = jnp.where(group6 == 2, z5_down, h5_up)
                add5 = jnp.where(group6 == 1, z0_up, h0_down)
                F[1, x, :, 0, :] = h0 + jnp.where(group6 == 0, 0.0, add0)
                F[1, x, :, 5, :] = h5 + jnp.where(group6 == 3, 0.0, add5)

    def link(idx, slot_no, src, dst, device):
        return lambda: pltpu.make_async_remote_copy(
            src_ref=src,
            dst_ref=dst,
            send_sem=ex_send.at[idx, slot_no],
            recv_sem=ex_recv.at[idx, slot_no],
            device_id=device,
            device_id_type=MESH,
        )

    def x_links(idx):
        return [
            (has["xl"], has["xh"], link(idx, 1, xsend.at[idx, 0], xrecv.at[idx, 1], (b, s - 1))),
            (has["xh"], has["xl"], link(idx, 0, xsend.at[idx, 1], xrecv.at[idx, 0], (b, s + 1))),
        ]

    def z_links(idx):
        both = jnp.logical_and
        out = [
            (has["zl"], has["zh"], link(idx, 3, zsend.at[idx, 0], zrecv.at[idx, 1], (b - 1, s))),
            (has["zh"], has["zl"], link(idx, 2, zsend.at[idx, 1], zrecv.at[idx, 0], (b + 1, s))),
        ]
        for zs, db, zn, zr in ((0, -1, "zl", "zh"), (1, 1, "zh", "zl")):
            for xside, ds, xn, xr in ((0, -1, "xl", "xh"), (1, 1, "xh", "xl")):
                out.append(
                    (
                        both(has[zn], has[xn]),
                        both(has[zr], has[xr]),
                        link(
                            idx,
                            4 + 2 * (1 - zs) + (1 - xside),
                            zsend.at[idx, zs, (ZT - 1) * xside],
                            drecv.at[idx, 1 - zs, 1 - xside],
                            (b + db, s + ds),
                        ),
                    )
                )
        return out

    def halo_links(idx):
        def one(side, device):
            return lambda: pltpu.make_async_remote_copy(
                src_ref=bsend.at[idx, side],
                dst_ref=brecv.at[idx, 1 - side],
                send_sem=h_send.at[idx, side],
                recv_sem=h_recv.at[idx, 1 - side],
                device_id=device,
                device_id_type=MESH,
            )

        return [
            (has["zl"], has["zh"], one(0, (b - 1, s))),
            (has["zh"], has["zl"], one(1, (b + 1, s))),
        ]

    def links_start(links):
        for there, _, copy in links:

            @pl.when(there)
            def _(copy=copy):
                copy().start()

    def links_wait(links):
        for _, here, copy in links:

            @pl.when(here)
            def _(copy=copy):
                copy().wait_recv()

    def links_sent(links):
        for there, _, copy in links:

            @pl.when(there)
            def _(copy=copy):
                copy().wait_send()

    def x_start(idx, F):
        xsend[idx, 0] = F[0]
        xsend[idx, 1] = F[NX - 1]
        links_start(x_links(idx))

    def x_end(idx, F):
        links_wait(x_links(idx))
        F[0] = F[0] + xrecv[idx, 0]
        F[NX - 1] = F[NX - 1] + xrecv[idx, 1]

    def exchange_start(idx, F):
        fold_y(F)
        x_start(idx, F)
        z_start(idx, F)

    def z_start(idx, F):
        for t in range(ZT):
            low = high = jnp.zeros((6, 128), F32)
            for m in range(4):
                x = 4 * t + m
                if x >= NX:
                    continue
                low = jnp.where(group6 == m, moved(F[x, :, 0, :], EY * m), low)
                high = jnp.where(group6 == m, moved(F[x, :, 5, :], EY * (m + 1)), high)
            zsend[idx, 0, t, 0:6, :] = low
            zsend[idx, 1, t, 0:6, :] = high
        links_start(z_links(idx))

    def inner_z(F):
        for x in range(NX):
            z0, z5 = F[x, :, 0, :], F[x, :, 5, :]
            F[x, :, 0, :] = z0 + jnp.where(lane6 < EY, 0.0, pltpu.roll(z5, EY, 1))
            F[x, :, 5, :] = z5 + jnp.where(
                lane6 >= 128 - EY, 0.0, pltpu.roll(z0, 128 - EY, 1)
            )

    def outer_z(idx, F):
        links_wait(z_links(idx))
        for x in range(NX):
            t, m = divmod(x, 4)
            near = moved(zrecv[idx, 0, t, 0:6, :], -EY * m)
            far = moved(zrecv[idx, 1, t, 0:6, :], 128 - EY - EY * m)
            if x == 0:
                near = near + moved(drecv[idx, 0, 0, 0:6, :], -EY * LAST)
                far = far + moved(drecv[idx, 1, 0, 0:6, :], 128 - EY - EY * LAST)
            if x == NX - 1:
                near = near + drecv[idx, 0, 1, 0:6, :]
                far = far + moved(drecv[idx, 1, 1, 0:6, :], 128 - EY)
            F[x, :, 0, :] = F[x, :, 0, :] + jnp.where(lane6 < EY, near, 0.0)
            F[x, :, 5, :] = F[x, :, 5, :] + jnp.where(lane6 >= 128 - EY, far, 0.0)

    def exchange_end(idx, F):
        x_end(idx, F)
        inner_z(F)
        outer_z(idx, F)

    def halo_start(idx, src):
        for t in range(ZT):
            for k in range(6):
                low = high = jnp.zeros((8, 128), F32)
                for m in range(4):
                    x = 4 * t + m
                    if x >= NX:
                        continue
                    tile = src(x, k)
                    low = jnp.where(group == m, moved(tile, EY * m), low)
                    high = jnp.where(group == m, moved(tile, EY * (m + 1)), high)
                bsend[idx, 0, t, k] = low
                bsend[idx, 1, t, k] = high

    def halo_unpack(idx, dst):
        for x in range(NX):
            t, m = divmod(x, 4)
            for k in range(6):
                low = moved(brecv[idx, 0, t, k], EY - EY * m)
                high = moved(brecv[idx, 1, t, k], 2 * EY - EY * m)
                dst[x, k] = jnp.where(group == 1, low, jnp.where(group == 2, high, 0.0))

    def window_copies(which, src, dst):
        out = []
        for off in range(-REACH, REACH + 1):
            for ds in range(n_sub):
                if off == 0 and ds == 0:
                    continue
                peer_s = lax.rem(s + ds, n_sub)
                target = b + off
                sending = jnp.logical_and(target >= 0, target < n_blk)

                def copy(off=off, ds=ds, peer_s=peer_s, target=target):
                    return pltpu.make_async_remote_copy(
                        src_ref=src,
                        dst_ref=dst.at[REACH - off, s],
                        send_sem=c_send.at[which, REACH + off, ds],
                        recv_sem=c_recv.at[which, REACH - off, s],
                        device_id=(target, peer_s),
                        device_id_type=MESH,
                    )

                def arrive(off=off, ds=ds, peer_s=peer_s, target=target):
                    return pltpu.make_async_remote_copy(
                        src_ref=src,
                        dst_ref=dst.at[REACH + off, peer_s],
                        send_sem=c_send.at[which, REACH + off, ds],
                        recv_sem=c_recv.at[which, REACH + off, peer_s],
                        device_id=(target, peer_s),
                        device_id_type=MESH,
                    )

                out.append((sending, copy, arrive))
        return out

    def window_start(which, src, dst):
        for sending, copy, _ in window_copies(which, src, dst):

            @pl.when(sending)
            def _(copy=copy):
                copy().start()

    def window_wait(which, src, dst):
        for sending, _, arrive in window_copies(which, src, dst):

            @pl.when(sending)
            def _(arrive=arrive):
                arrive().wait_recv()

    def window_sent(which, src, dst):
        for sending, copy, _ in window_copies(which, src, dst):

            @pl.when(sending)
            def _(copy=copy):
                copy().wait_send()

    def velocity(c):
        unpack_flat(lambda at: vel_flat[c, :, at], FL)
        to_elements(FL, VE, False)
        out = VV.at[c]
        rounded = lambda value: value.astype(BF16).astype(F32)
        for ex in range(EX):
            gx = SG[0, ex]
            for k in range(6):
                vs = [VE[5 * ex + m, k] for m in range(6)]
                flux = []
                for i in range(6):
                    grad = mac([(float(Dh[i, m]), vs[m]) for m in range(6)])
                    flux.append(rounded(grad * (WJ * float(w[i] * w[k])) * gx))
                for i in range(6):
                    value = mac([(float(Dh[m, i]), flux[m]) for m in range(6)])
                    if i == 0 and ex > 0:
                        value = value + out[5 * ex, k]
                    out[5 * ex + i, k] = value
        for ex in range(EX):
            gz, gy, gm = SG[1, ex], SG[2, ex], SG[3, ex]
            for i in range(6):
                x = 5 * ex + i
                vs = [VE[x, m] for m in range(6)]
                flux = []
                for k in range(6):
                    grad = mac([(float(Dh[k, m]), vs[m]) for m in range(6)])
                    flux.append(rounded(grad * (WJ * float(w[i] * w[k])) * gy))
                for k in range(6):
                    vk = vs[k]
                    weight = WJ * float(w[i] * w[k])
                    value = mac([(float(Dh[m, k]), flux[m]) for m in range(6)])
                    grad = tab_ref[8] * vk
                    for sh in range(1, 8):
                        grad = grad + tab_ref[8 + sh] * pltpu.roll(vk, sh, 0)
                    fz = rounded(grad * weight * gz)
                    value = value + tab_ref[16] * fz
                    for sh in range(1, 8):
                        value = value + tab_ref[16 + sh] * pltpu.roll(fz, sh, 0)
                    value = value + gm * weight * vk
                    out[x, k] = out[x, k] + value

    geometry(0, stack)
    fetch["load"].wait()
    fetch["pick"].wait()
    unpack_flat(lambda at: load_flat[at], FI)
    to_elements(FI, R.at[0], True)
    halo_start(0, lambda x, k: R[0, x, k])
    crecv[REACH, s] = stack
    for c in range(3):
        fetch["vel%d" % c].wait()

    def component(c, carry):
        velocity(c)

        @pl.when(c == 0)
        def _():
            pl.semaphore_wait(barrier, n_dev - 1)
            window_start(0, csend, crecv)
            links_start(halo_links(0))

        exchange_start(c, VV.at[c])
        return carry

    lax.fori_loop(0, 3, component, 0)

    window_wait(0, csend, crecv)

    def beside(t):
        low, high = crecv[REACH - 1, t], crecv[REACH + 1, t]
        return jnp.where(lane < 2 * EY, pltpu.roll(low, 64, 1), pltpu.roll(high, 64, 1))

    left_s, right_s = jnp.maximum(s - 1, 0), jnp.minimum(s + 1, n_sub - 1)
    left_on = jnp.where(has["xl"], 1.0, 0.0)
    right_on = jnp.where(has["xh"], 1.0, 0.0)
    geometry(1, beside(s))
    face_geometry(0, (crecv[REACH, left_s] * left_on, crecv[REACH, right_s] * right_on))
    face_geometry(1, (beside(left_s) * left_on, beside(right_s) * right_on))
    for h in range(2):
        diagonal_part(h)
    fold_z(W, True)
    for h in range(2):
        fold_y(W.at[h])
    for h in range(2):
        for x in range(NX):
            for k in range(6):
                full = W[h, x, k]
                good = full > 0.0
                INV[h, x, k] = jnp.where(good, DAMPING / jnp.where(good, full, 1.0), 0.0)

    for o in range(SPAN):
        for t in range(n_sub):
            packed = crecv[o, t]
            for ez in range(EZ):
                if not ZLO - 1 <= EZ * o + ez <= ZHI:
                    continue
                tile = jnp.where(lane < EY, moved(packed, -EY * ez), 0.0)
                for q in range(4):
                    CF[EZ * o + ez + 1, q, EX * t : EX * t + EX, :] = tile[
                        EX * q : EX * q + EX, :
                    ]

    corners = [(a, c, d) for a in (0, 1) for c in (0, 1) for d in (0, 1)]

    def stencil(z, carry):
        shifted = {}
        for c in (0, 1):
            for q in range(4):
                base = CF[z + 1 - c, q]
                for a in (0, 1):
                    up = pltpu.roll(base, 1, 0) if a else base
                    shifted[a, c, 0, q] = up
                    shifted[a, c, 1, q] = pltpu.roll(up, 1, 1)
        total = {}
        for ui, u in enumerate(corners):
            for vi, v in enumerate(corners):
                key = tuple(v[t] - u[t] for t in range(3))
                term = mac([(float(coarse[q][ui, vi]), shifted[u + (q,)]) for q in range(4)])
                total[key] = term if key not in total else total[key] + term
        for key, value in total.items():
            ST[z, 9 * (key[0] + 1) + 3 * (key[1] + 1) + key[2] + 1] = value
        diag = total[0, 0, 0]
        ST[z, 27] = jnp.where(diag > 0.0, 1.0 / jnp.where(diag > 0.0, diag, 1.0), 0.0)
        return carry

    cut_a = ZLO + (ZHI + 1 - ZLO) // 3
    lax.fori_loop(ZLO, cut_a, stencil, 0)

    links_wait(halo_links(0))
    halo_unpack(0, R.at[1])
    for h in range(2):
        for x in range(NX):
            for k in range(6):
                V[h, x, k] = R[h, x, k] * INV[h, x, k]
        apply_part(h)
    fold_z(W, False)
    fold_y(W.at[0])
    x_start(5, W.at[0])
    x_end(5, W.at[0])
    for x in range(NX):
        for k in range(6):
            V[0, x, k] = V[0, x, k] + (R[0, x, k] - W[0, x, k]) * INV[0, x, k]
    apply_part(0)
    fold_y(W.at[0])
    x_start(3, W.at[0])

    one = jnp.ones((8, 128), F32)
    wz = jnp.where(sub_i < 5, one, 0.0)
    wz = jnp.where(jnp.logical_and(sub_i == 5, lane >= 128 - EY), 1.0, wz)
    low_half = jnp.where(has["zl"], 0.5, 1.0)
    high_half = jnp.where(has["zh"], 0.5, 1.0)
    wz = wz * jnp.where(jnp.logical_and(sub_i == 0, lane < EY), low_half, 1.0)
    wz = wz * jnp.where(jnp.logical_and(sub_i == 5, lane >= 128 - EY), high_half, 1.0)
    wend = wz * jnp.where(ey == EY - 1, 1.0, 0.0)
    xlow = jnp.where(has["xl"], 0.5, 1.0)
    xhigh = jnp.where(has["xh"], 0.5, 1.0)

    def unique(x, k):
        tile = wz if k < 5 else wend
        if x == 0:
            tile = tile * xlow
        if x == NX - 1:
            tile = tile * xhigh
        return tile

    acc = [[None, None] for _ in range(EX + 1)]
    for x in range(NX):
        rows = [unique(x, k) * R[0, x, k] - W[0, x, k] for k in range(5)]
        last_row = unique(x, 5) * R[0, x, 5] - W[0, x, 5]
        rows.append(jnp.where(ey == EY - 1, last_row, 0.0))
        lines = [mac([(float(lin[k, d]), rows[k]) for k in range(6)]) for d in (0, 1)]
        ex = min(x // 5, EX - 1)
        i = x - 5 * ex
        for a in (0, 1):
            weight = float(lin[i, a])
            if weight == 0.0:
                continue
            for d in (0, 1):
                term = weight * lines[d]
                old = acc[ex + a][d]
                acc[ex + a][d] = term if old is None else old + term
    pieces = {}
    for c in (0, 1):
        for d in (0, 1):
            tile = jnp.zeros((8, 128), F32)
            for xv in range(EX + 1):
                row = jnp.sum(LJ[c] * acc[xv][d], axis=0, keepdims=True)
                tile = jnp.where(sub_i == xv, jnp.broadcast_to(row, (8, 128)), tile)
            pieces[c, d] = tile
    placed = [None] * (EZ + 1)
    for c in (0, 1):
        for ez in range(EZ):
            sums = None
            for d in (0, 1):
                tile = jnp.where(lane < EY, moved(pieces[c, d], -EY * ez), 0.0)
                if d:
                    tile = pltpu.roll(tile, 1, 1)
                sums = tile if sums is None else sums + tile
            old = placed[ez + c]
            placed[ez + c] = sums if old is None else old + sums
    message = placed[0]
    for zv in range(1, EZ + 1):
        rows_at, lanes_at = divmod(zv, 3)
        tile = moved(placed[zv], (EY + 8) * lanes_at)
        if rows_at:
            tile = pltpu.roll(tile, (EX + 1) * rows_at, 0)
        message = message + tile
    rsend[...] = message
    rrecv[REACH, s] = message
    window_start(1, rsend, rrecv)

    z_start(3, W.at[0])
    x_end(3, W.at[0])
    inner_z(W.at[0])
    halo_start(1, lambda x, k: V[0, x, k] + (R[0, x, k] - W[0, x, k]) * INV[0, x, k])
    links_start(halo_links(1))
    lax.fori_loop(cut_a, ZHI + 1, stencil, 0)
    outer_z(3, W.at[0])
    for x in range(NX):
        for k in range(6):
            V[0, x, k] = V[0, x, k] + (R[0, x, k] - W[0, x, k]) * INV[0, x, k]

    fetch["put"].wait()

    def velocity_out(c):
        exchange_end(c, VV.at[c])
        to_nodes(VV.at[c], FP)

        def store(at, tile):
            vel_back[c, :, at] = tile.reshape(1, tile.size)

        pack_flat(lambda p, n: FP[PAD + p : PAD + p + n, :], store)
        pltpu.make_async_copy(
            vel_back.at[c], velout_hbm.at[c], out_sem.at[c]
        ).start()

    velocity_out(0)
    window_wait(1, rsend, rrecv)

    def window_sum(o, zv):
        rows_at, lanes_at = divmod(zv, 3)
        total = None
        for t in range(n_sub):
            tile = moved(rrecv[o, t], -(EY + 8) * lanes_at)
            here = jnp.logical_and(
                sub_i >= (EX + 1) * rows_at, sub_i < (EX + 1) * (rows_at + 1)
            )
            tile = jnp.where(jnp.logical_and(here, lane <= EY), tile, 0.0)
            if xs > 8:
                tile = jnp.concatenate([tile, jnp.zeros((xs - 8, 128), F32)], axis=0)
            shift = (EX * t - (EX + 1) * rows_at) % xs
            if shift:
                tile = pltpu.roll(tile, shift, 0)
            total = tile if total is None else total + tile
        return total

    center = (SPECTRUM_HIGH + SPECTRUM_LOW) / 2.0
    radius = (SPECTRUM_HIGH - SPECTRUM_LOW) / 2.0
    ratio = center / radius
    factor = 1.0 / ratio
    for z in range(ZLO, ZHI + 1):
        o, zv = divmod(z, EZ)
        value = window_sum(o, zv)
        if zv == 0 and o > 0:
            value = value + window_sum(o - 1, EZ)
        CR[z] = value
        CU[0, z] = value * ST[z, 27] * (1.0 / center)
    first, last = FIRST - HALO, LAST_V + HALO
    sol = {z: CU[0, z] for z in range(first, last + 1)}
    for sweep in range(CHEB_ITERS - 1):
        now, later = sweep % 2, (sweep + 1) % 2
        left = CHEB_ITERS - 2 - sweep
        nxt = 1.0 / (2.0 * ratio - factor)
        wide = {}
        for z in range(first - left, last + left + 1):
            for zz in (z - 1, z, z + 1):
                if zz in wide:
                    continue
                base = CU[now, zz]
                sides = {}
                for dx in (-1, 0, 1):
                    mx = base if dx == 0 else pltpu.roll(base, (-dx) % xs, 0)
                    for dy in (-1, 0, 1):
                        sides[dx, dy] = mx if dy == 0 else pltpu.roll(mx, (-dy) % 128, 1)
                wide[zz] = sides
            total = None
            for dz in (-1, 0, 1):
                for dx in (-1, 0, 1):
                    for dy in (-1, 0, 1):
                        term = ST[z, 9 * (dx + 1) + 3 * (dz + 1) + dy + 1] * wide[z + dz][dx, dy]
                        total = term if total is None else total + term
            residual = CR[z] - total
            CR[z] = residual
            fresh = (nxt * factor) * CU[now, z] + (2.0 * nxt / radius) * (residual * ST[z, 27])
            CU[later, z] = fresh
            if first <= z <= last:
                sol[z] = sol[z] + fresh
        factor = nxt

    own = {}
    for z, tile in sol.items():
        shifted_x = tile
        for t in range(1, n_sub):
            shifted_x = jnp.where(s == t, pltpu.roll(tile, (-EX * t) % xs, 0), shifted_x)
        own[z - FIRST] = shifted_x

    velocity_out(1)
    links_wait(halo_links(1))
    halo_unpack(1, V.at[1])
    for x in range(NX):
        z0, z5 = V[0, x, :, 0, :], V[0, x, :, 5, :]
        V[1, x, :, 5, :] = jnp.where(
            group6 == 1, pltpu.roll(z0, EY, 1), V[1, x, :, 5, :]
        )
        V[1, x, :, 0, :] = jnp.where(
            group6 == 2, pltpu.roll(z5, 128 - EY, 1), V[1, x, :, 0, :]
        )

    ZJ = tab_ref[28]
    for h in range(2):
        places = range(EZ) if h == 0 else (-2, -1, EZ, EZ + 1)
        corner_tiles = {}
        for c in (0, 1):
            for d in (0, 1):
                total = None
                for at, ez in enumerate(places):
                    tile = own[ez + c]
                    if d:
                        tile = pltpu.roll(tile, 127, 1)
                    tile = moved(jnp.where(lane[0:1] < EY, tile, 0.0), EY * at)
                    total = tile if total is None else total + tile
                corner_tiles[c, d] = total
        val, zdif, ydif = {}, {}, {}
        for xv in range(-1, EX + 2):
            at = xv % xs
            rows = {
                key: jnp.broadcast_to(tile[at : at + 1, :], (8, 128))
                for key, tile in corner_tiles.items()
            }
            ends = [LJ[0] * rows[0, d] + LJ[1] * rows[1, d] for d in (0, 1)]
            val[xv] = [mac([(float(lin[k, d]), ends[d]) for d in (0, 1)]) for k in range(6)]
            if 0 <= xv <= EX:
                jump = [ZJ * (rows[0, d] - rows[1, d]) for d in (0, 1)]
                zdif[xv] = [
                    mac([(float(lin[k, d]), jump[d]) for d in (0, 1)]) for k in range(6)
                ]
                ydif[xv] = 0.5 * (ends[0] - ends[1])
        for x in range(NX):
            ex = min(x // 5, EX - 1)
            i = x - 5 * ex
            parts = [(float(lin[i, a]), ex + a) for a in (0, 1)]
            gy, gz, gm = whole_geometry(h, x)
            slope = gy * mac([(weight, ydif[xv]) for weight, xv in parts])
            for k in range(6):
                u = mac([(weight, val[xv][k]) for weight, xv in parts])
                inside = gz * mac([(weight, zdif[xv][k]) for weight, xv in parts]) + gm * u
                if x % 5 == 0:
                    xv = x // 5
                    inside = inside + GX[h, xv] * (0.5 * (val[xv][k] - val[xv - 1][k]))
                    inside = inside + GX[h, xv + 1] * (0.5 * (val[xv][k] - val[xv + 1][k]))
                value = float(w[k]) * inside
                if k == 0:
                    value = value + slope
                if k == 5:
                    value = value - slope
                W[h, x, k] = value
                V[h, x, k] = V[h, x, k] + u
    fold_z(W, True)
    for h in range(2):
        fold_y(W.at[h])
    for h in range(2):
        for x in range(NX):
            for k in range(6):
                V[h, x, k] = V[h, x, k] - W[h, x, k] * INV[h, x, k]
        apply_part(h)
    fold_z(W, False)
    fold_y(W.at[0])
    x_start(6, W.at[0])
    x_end(6, W.at[0])
    for x in range(NX):
        for k in range(6):
            V[0, x, k] = V[0, x, k] + (R[0, x, k] - W[0, x, k]) * INV[0, x, k]
    apply_part(0)
    num = jnp.zeros((8, 128), F32)
    den = jnp.zeros((8, 128), F32)
    for x in range(NX):
        for k in range(6):
            v = V[0, x, k]
            num = num + unique(x, k) * R[0, x, k] * v
            den = den + v * W[0, x, k]
    num_row = jnp.sum(num, axis=0, keepdims=True)
    den_row = jnp.sum(den, axis=0, keepdims=True)
    num_one = jnp.sum(num_row, axis=1, keepdims=True)
    den_one = jnp.sum(den_row, axis=1, keepdims=True)
    lane1 = lax.broadcasted_iota(jnp.int32, (1, 128), 1)
    psend[...] = jnp.where(lane1 < 64, num_one, den_one)

    def scatter(d, carry):
        pltpu.make_async_remote_copy(
            src_ref=psend,
            dst_ref=precv.at[d - 1],
            send_sem=p_sem.at[0],
            recv_sem=p_sem.at[1],
            device_id=device_of(lax.rem(me + d, n_dev)),
            device_id_type=MESH,
        ).start()
        return carry

    lax.fori_loop(1, n_dev, scatter, 0)
    exchange_start(4, W.at[0])
    velocity_out(2)
    to_nodes(V.at[0], FP)
    exchange_end(4, W.at[0])
    to_nodes(W.at[0], FR)
    whole = pltpu.make_async_remote_copy(
        src_ref=precv,
        dst_ref=precv,
        send_sem=p_sem.at[0],
        recv_sem=p_sem.at[1],
        device_id=(b, s),
        device_id_type=MESH,
    )
    whole.wait_recv()
    both = psend[...] + jnp.sum(precv[...], axis=0)
    step = both[0:1, 0:1] / both[0:1, 64:65]

    def store_to(back):
        def store(at, tile):
            back[at] = tile.reshape(tile.size)

        return store

    pack_flat(lambda p, n: step * FP[PAD + p : PAD + p + n, :], store_to(pres_back))
    pack_flat(
        lambda p, n: FI[PAD + p : PAD + p + n, :] - step * FR[PAD + p : PAD + p + n, :],
        store_to(res_back),
    )
    backs = [
        pltpu.make_async_copy(pres_back, pres_hbm, out_sem.at[3]),
        pltpu.make_async_copy(res_back, res_hbm, out_sem.at[4]),
    ]
    for copy in backs:
        copy.start()
    whole.wait_send()
    for idx in range(5):
        links_sent(x_links(idx) + z_links(idx))
    for idx in range(5, EXCH):
        links_sent(x_links(idx))
    for idx in range(2):
        links_sent(halo_links(idx))
    window_sent(0, csend, crecv)
    window_sent(1, rsend, rrecv)
    for c in range(3):
        pltpu.make_async_copy(vel_back.at[c], velout_hbm.at[c], out_sem.at[c]).wait()
    for copy in backs:
        copy.wait()


def place(vel_in, pres_in, res_in, vel_out, pres_out, res_out, vel, pres, res, sem):
    pairs = [(vel_in.at[c], vel.at[c], vel_out.at[pl.ds(c, 1)]) for c in range(3)]
    pairs += [(pres_in, pres, pres_out), (res_in, res, res_out)]
    loads = [pltpu.make_async_copy(p[0], p[1], sem.at[0, i]) for i, p in enumerate(pairs)]
    stores = [pltpu.make_async_copy(p[1], p[2], sem.at[1, i]) for i, p in enumerate(pairs)]
    for copy in loads:
        copy.start()
    for load, store in zip(loads, stores):
        load.wait()
        store.start()
    for copy in stores:
        copy.wait()


def solution(mesh):
    n_blk, n_sub = mesh.shape["blk"], mesh.shape["sub"]
    n_dev = n_blk * n_sub
    xs = -(-(EX * n_sub + 2) // 8) * 8
    D, w, k1, lin, coarse = tables()
    Dh = bf16_round(D)
    tab = np.concatenate(
        [
            roll_tables(k1),
            roll_tables(Dh),
            roll_tables(Dh.T),
            col_tile(w),
            col_tile(lin[:, 0]),
            col_tile(lin[:, 1]),
            col_tile(np.diag(k1)),
            col_tile([0.5, 0.0, 0.0, 0.0, 0.0, -0.5]),
        ]
    )
    pick, put = pick_matrices()

    def per_device(velocity, pressure_load, local_map, stiff_geo, mass_geo):
        field = (NX, 6, 8, 128)
        reach_in = NY * (IN_STEP - 1) // 128 + 3 + 7 * IN_SKIP
        reach_out = FLAT + 8 * OUT_SKIP
        flat = pltpu.VMEM((PAD + -(-max(reach_in, reach_out) // 8) * 8, 128), F32)
        out_rows = PAD + -(-(ROWS + 8 * OUT_STEP + 2) // 8) * 8
        out = pl.pallas_call(
            functools.partial(kernel, n_blk, n_sub, xs),
            out_shape=(
                jax.ShapeDtypeStruct((3, 1, NLOC), F32),
                jax.ShapeDtypeStruct((NLOC,), F32),
                jax.ShapeDtypeStruct((NLOC,), F32),
            ),
            in_specs=[pl.BlockSpec(memory_space=pl.ANY)] * 8,
            out_specs=(pl.BlockSpec(memory_space=pl.ANY),) * 3,
            scratch_shapes=[
                pltpu.VMEM((3, 1, NLOC), F32),
                pltpu.VMEM((NLOC,), F32),
                pltpu.VMEM((3, 1, NLOC), F32),
                pltpu.VMEM((NLOC,), F32),
                pltpu.VMEM((NLOC,), F32),
                flat,
                flat,
                flat,
                flat,
                pltpu.VMEM((IN_ROWS, 128), F32),
                pltpu.VMEM((IN_ROWS, 128), F32),
                pltpu.VMEM((out_rows, 128), F32),
                pltpu.VMEM((out_rows, 128), F32),
                pltpu.VMEM((3, EX * EZ * EY), F32),
                pltpu.VMEM((1, EX * EZ * EY), F32),
                pltpu.VMEM(tab.shape, F32),
                pltpu.VMEM(pick.shape, BF16),
                pltpu.VMEM(put.shape, BF16),
                pltpu.VMEM((2,) + field, F32),
                pltpu.VMEM((2,) + field, F32),
                pltpu.VMEM((8, EX * EZ * EY), jnp.int32),
                pltpu.VMEM((2,) + field, F32),
                pltpu.VMEM((2,) + field, F32),
                pltpu.VMEM((3,) + field, F32),
                pltpu.VMEM(field, F32),
                pltpu.VMEM((2, EX + 2, 8, 128), F32),
                pltpu.VMEM((2, 3, NX, 8, 128), F32),
                pltpu.VMEM((2, 2, 3, 8, 128), F32),
                pltpu.VMEM((4, EX, 8, 128), F32),
                pltpu.VMEM((EXCH, 2, 6, 8, 128), F32),
                pltpu.VMEM((EXCH, 2, 6, 8, 128), F32),
                pltpu.VMEM((EXCH, 2, ZT, 8, 128), F32),
                pltpu.VMEM((EXCH, 2, ZT, 8, 128), F32),
                pltpu.VMEM((EXCH, 2, 2, 8, 128), F32),
                pltpu.VMEM((8, 128), F32),
                pltpu.VMEM((SPAN, n_sub, 8, 128), F32),
                pltpu.VMEM((8, 128), F32),
                pltpu.VMEM((SPAN, n_sub, 8, 128), F32),
                pltpu.VMEM((2, 2, ZT, 6, 8, 128), F32),
                pltpu.VMEM((2, 2, ZT, 6, 8, 128), F32),
                pltpu.VMEM((NZV + 1, 4, xs, 128), F32),
                pltpu.VMEM((NZV, 28, xs, 128), F32),
                pltpu.VMEM((2, NZV, xs, 128), F32),
                pltpu.VMEM((NZV, xs, 128), F32),
                pltpu.VMEM((1, 128), F32),
                pltpu.VMEM((n_dev - 1, 1, 128), F32),
                pltpu.SemaphoreType.DMA((EXCH, 8)),
                pltpu.SemaphoreType.DMA((EXCH, 8)),
                pltpu.SemaphoreType.DMA((2, SPAN, n_sub)),
                pltpu.SemaphoreType.DMA((2, SPAN, n_sub)),
                pltpu.SemaphoreType.DMA((2, 2)),
                pltpu.SemaphoreType.DMA((2, 2)),
                pltpu.SemaphoreType.DMA((2,)),
                pltpu.SemaphoreType.DMA((10,)),
                pltpu.SemaphoreType.DMA((5,)),
            ],
            compiler_params=pltpu.CompilerParams(
                collective_id=0, has_side_effects=True, vmem_limit_bytes=60 << 20
            ),
        )(
            velocity,
            pressure_load,
            local_map,
            stiff_geo,
            mass_geo.reshape(1, mass_geo.shape[0]),
            jnp.asarray(tab, F32),
            jnp.asarray(pick, BF16),
            jnp.asarray(put, BF16),
        )
        any_spec = pl.BlockSpec(memory_space=pl.ANY)
        return tuple(
            pl.pallas_call(
                place,
                out_shape=(
                    jax.ShapeDtypeStruct((3, NLOC), F32),
                    jax.ShapeDtypeStruct((NLOC,), F32),
                    jax.ShapeDtypeStruct((NLOC,), F32),
                ),
                in_specs=[any_spec] * 3,
                out_specs=(any_spec,) * 3,
                scratch_shapes=[
                    pltpu.VMEM((3, 1, NLOC), F32),
                    pltpu.VMEM((NLOC,), F32),
                    pltpu.VMEM((NLOC,), F32),
                    pltpu.SemaphoreType.DMA((2, 5)),
                ],
            )(*out)
        )

    in_specs = (
        P(None, ("blk", "sub")),
        P(("blk", "sub")),
        P(None, ("blk", "sub")),
        P(None, ("blk", "sub")),
        P(("blk", "sub")),
    )
    out_specs = (P(None, ("blk", "sub")), P(("blk", "sub")), P(("blk", "sub")))
    return jax.shard_map(
        per_device, mesh=mesh, in_specs=in_specs, out_specs=out_specs, check_vma=False
    )
```

```python
import functools
import math

import jax
import jax.numpy as jnp
import numpy as np
from jax import lax
from jax.experimental import pallas as pl
from jax.experimental.pallas import tpu as pltpu
from jax.sharding import PartitionSpec as P

EX = 2
EZ = 4
EY = 32
CHEB_ITERS = 8
NX = 5 * EX + 1
NZ = 5 * EZ + 1
NY = 5 * EY + 1
NLOC = NX * NZ * NY
NZP = 24
NYP = 256
HALO = 2
DEPTH = CHEB_ITERS - 1 + HALO
REACH = -(-DEPTH // EZ)
SPAN = 2 * REACH + 1
NZV = SPAN * EZ + 1
FIRST = REACH * EZ
LAST_V = FIRST + EZ
ZLO = FIRST - DEPTH
ZHI = LAST_V + DEPTH
EXCH = 7
ZT = -(-NX // 4)
ROWS = NX * NZ
IN_STEP = next(k for k in range(1, 129) if NY * k % 128 == 127)
IN_SKIP = (NY * IN_STEP + 1) // 128
IN_ROWS = 8 * IN_STEP
OUT_STEP, OUT_SKIP = next(
    (r, p) for r in range(1, 129) for p in (NY * r // 128,) if 0 < NY * r - 128 * p <= 4
)
OUT_DRIFT = NY * OUT_STEP - 128 * OUT_SKIP
FLAT = -(-NLOC // 128)
FULL = NLOC // 1024
PAD = 8
LAST = (NX - 1) % 4

DAMPING = 0.3
MASS_SHARE = 0.05
SPECTRUM_LOW = 0.15
SPECTRUM_HIGH = 4.5
MESH = pl.DeviceIdType.MESH
F32 = jnp.float32
BF16 = jnp.bfloat16


def tables():
    seven_root = math.sqrt(7.0)
    inner = math.sqrt(1.0 / 3.0 - 2.0 * seven_root / 21.0)
    outer = math.sqrt(1.0 / 3.0 + 2.0 * seven_root / 21.0)
    xi = np.array([-1.0, -outer, -inner, inner, outer, 1.0])
    leg = (63.0 * xi**5 - 70.0 * xi**3 + 15.0 * xi) / 8.0
    w = 2.0 / (30.0 * leg**2)
    D = np.zeros((6, 6))
    for i in range(6):
        for j in range(6):
            if i != j:
                D[i, j] = leg[i] / (leg[j] * (xi[i] - xi[j]))
    D[0, 0] = -7.5
    D[5, 5] = 7.5
    k1 = D.T @ (w[:, None] * D)
    lin = np.stack([(1.0 - xi) / 2.0, (1.0 + xi) / 2.0], 1)
    kc = lin.T @ k1 @ lin
    mc = lin.T @ (w[:, None] * lin)
    coarse = [
        np.kron(np.kron(kc, mc), mc),
        np.kron(np.kron(mc, kc), mc),
        np.kron(np.kron(mc, mc), kc),
        MASS_SHARE * np.kron(np.kron(mc, mc), mc),
    ]
    return D, w, k1, lin, coarse


def roll_tables(M):
    out = np.zeros((8, 8, 128), np.float32)
    for s in range(8):
        for j in range(6):
            m = (j - s) % 8
            if m < 6:
                out[s, j, :] = M[j, m]
    return out


def col_tile(values):
    tile = np.zeros((1, 8, 128), np.float32)
    tile[0, :6, :] = np.asarray(values)[:, None]
    return tile


def bf16_round(a):
    return np.asarray(a, np.float32).astype(np.dtype(BF16)).astype(np.float64)


def pick_matrices():
    pick = np.zeros((NYP, 6, 128), np.float32)
    put = np.zeros((6, 128, NYP), np.float32)
    for k in range(6):
        for z in range(EZ):
            for e in range(EY):
                pick[5 * e + k, k, z * EY + e] = 1.0
                if k < 5 or e == EY - 1:
                    put[k, z * EY + e, 5 * e + k] = 1.0
    return pick.reshape(NYP, 768), put.reshape(768, NYP)


def mac(pairs):
    total = None
    for coef, value in pairs:
        if isinstance(coef, (float, int)) and coef == 0.0:
            continue
        term = coef * value
        total = term if total is None else total + term
    return total


def kernel(
    n_blk,
    n_sub,
    xs,
    vel_hbm,
    load_hbm,
    map_hbm,
    stiff_hbm,
    mass_hbm,
    tab_hbm,
    pick_hbm,
    put_hbm,
    velout_hbm,
    pres_hbm,
    res_hbm,
    vel_flat,
    load_flat,
    vel_back,
    pres_back,
    res_back,
    FL,
    FI,
    FP,
    FR,
    S0,
    S1,
    Y0,
    Y1,
    stiff_ref,
    mass_ref,
    tab_ref,
    pick_ref,
    put_ref,
    V,
    W,
    map_ref,
    R,
    INV,
    VV,
    VE,
    GX,
    GC,
    GE,
    GP,
    SG,
    xsend,
    xrecv,
    zsend,
    zrecv,
    drecv,
    csend,
    crecv,
    rsend,
    rrecv,
    bsend,
    brecv,
    CF,
    ST,
    CU,
    CR,
    psend,
    precv,
    ex_send,
    ex_recv,
    c_send,
    c_recv,
    h_send,
    h_recv,
    p_sem,
    in_sem,
    out_sem,
):
    D, w, k1, lin, coarse = tables()
    Dh = bf16_round(D)
    n_dev = n_blk * n_sub
    b = lax.axis_index("blk")
    s = lax.axis_index("sub")
    me = b * n_sub + s

    def device_of(linear):
        return (linear // n_sub, lax.rem(linear, n_sub))

    barrier = pltpu.get_barrier_semaphore()

    def greet(d, carry):
        pl.semaphore_signal(
            barrier, inc=1, device_id=device_of(lax.rem(me + d, n_dev)), device_id_type=MESH
        )
        return carry

    lax.fori_loop(1, n_dev, greet, 0)

    fetch = {}
    for at, (name, src, dst) in enumerate(
        (
            ("map", map_hbm.at[0:8, :], map_ref),
            ("stiff", stiff_hbm, stiff_ref),
            ("mass", mass_hbm, mass_ref),
            ("tab", tab_hbm, tab_ref),
            ("load", load_hbm, load_flat),
            ("pick", pick_hbm, pick_ref),
            ("vel0", vel_hbm.at[0:1], vel_flat.at[0]),
            ("vel1", vel_hbm.at[1:2], vel_flat.at[1]),
            ("vel2", vel_hbm.at[2:3], vel_flat.at[2]),
            ("put", put_hbm, put_ref),
        )
    ):
        fetch[name] = pltpu.make_async_copy(src, dst, in_sem.at[at])
        fetch[name].start()

    has = {
        "xl": s > 0,
        "xh": s < n_sub - 1,
        "zl": b > 0,
        "zh": b < n_blk - 1,
    }

    def zero(ref_slice):
        ref_slice[...] = jnp.zeros(ref_slice.shape, F32)

    for side, name in ((0, "xl"), (1, "xh")):

        @pl.when(jnp.logical_not(has[name]))
        def _(side=side):
            zero(xrecv.at[:, side])

    for side, name in ((0, "zl"), (1, "zh")):

        @pl.when(jnp.logical_not(has[name]))
        def _(side=side):
            zero(zrecv.at[:, side])
            zero(brecv.at[:, side])

    for zs, zname in ((0, "zl"), (1, "zh")):
        for xside, xname in ((0, "xl"), (1, "xh")):

            @pl.when(jnp.logical_not(jnp.logical_and(has[zname], has[xname])))
            def _(zs=zs, xside=xside):
                zero(drecv.at[:, zs, xside])

    for o in range(SPAN):
        off = o - REACH

        @pl.when(jnp.logical_or(b + off < 0, b + off >= n_blk))
        def _(o=o):
            zero(crecv.at[o])
            zero(rrecv.at[o])

    CF[...] = jnp.zeros(CF.shape, F32)

    lane = lax.broadcasted_iota(jnp.int32, (8, 128), 1)
    sub_i = lax.broadcasted_iota(jnp.int32, (8, 128), 0)
    lane88 = lax.broadcasted_iota(jnp.int32, (8 * NX, 768), 1) // EY % EZ
    row88 = lax.broadcasted_iota(jnp.int32, (8 * NX, 768), 0) % 8
    ey = lane % EY
    lane6 = lax.broadcasted_iota(jnp.int32, (6, 128), 1)
    group6 = lane6 // EY
    group = lane // EY
    CT = lambda q: tab_ref[q]

    def moved(tile, shift):
        return tile if shift % 128 == 0 else pltpu.roll(tile, shift % 128, 1)

    slant_in = lane - sub_i
    slant_out = lane - OUT_DRIFT * sub_i

    def spin(tile, shift, stride):
        shift = shift % 128
        if shift + 7 * stride > 128:
            tile, shift = pltpu.roll(tile, shift, 1), 0
        return pltpu.roll(tile, shift, 1, stride=stride, stride_axis=0)

    chunks = [(8 * i, 8, 1024) for i in range(FULL)]
    chunks += [(p, 1, min(128, NLOC - 128 * p)) for p in range(8 * FULL, FLAT)]

    def unpack_flat(source, dest):
        for p, n, size in chunks:
            dest[PAD + p : PAD + p + n, 0 : size // n] = source(
                pl.ds(128 * p, size)
            ).reshape(n, size // n)

    def pack_flat(tile, store):
        for p, n, size in chunks:
            store(pl.ds(128 * p, size), tile(p, n)[:, 0 : size // n])

    def flat_to_rows(flat):
        for r in range(IN_STEP):
            q, at = divmod(NY * r, 128)
            if at < 7:
                q, at = q - 1, at + 128
            a, b_, c = (
                spin(flat[pl.ds(PAD + q + n, 8, stride=IN_SKIP), :], -at, 1) for n in range(3)
            )
            first_part = slant_in < 128 - at
            if at > 128:
                b_low = jnp.where(slant_in < 256 - at, b_, c)
            else:
                b_low = b_
            S0[pl.ds(r, 8, stride=IN_STEP), :] = jnp.where(first_part, a, b_low)
            S1[pl.ds(r, 8, stride=IN_STEP), :] = jnp.where(
                lane < NY - 128, jnp.where(first_part, b_, c), 0.0
            )

    def rows_to_flat(dest):
        for block in range(0, FLAT, 8 * OUT_SKIP):
            for step in range(OUT_SKIP):
                p = block + step
                if p >= FLAT:
                    continue
                r, y = divmod(128 * p, NY)
                if y < 7 * OUT_DRIFT:
                    r, y = r - 1, y + NY

                def piece(ref, row, turn):
                    return spin(
                        ref[pl.ds(PAD + row, 8, stride=OUT_STEP), :], turn, OUT_DRIFT
                    )

                value = piece(Y1, r, -y)
                if y - 7 * OUT_DRIFT < 128:
                    value = jnp.where(slant_out < 128 - y, piece(Y0, r, -y), value)
                if y + 127 >= NY:
                    after = piece(Y0, r + 1, NY - y)
                    if y + 127 >= NY + 128:
                        after = jnp.where(
                            slant_out < NY + 128 - y, after, piece(Y1, r + 1, NY - y)
                        )
                    value = jnp.where(slant_out < NY - y, value, after)
                dest[pl.ds(PAD + p, 8, stride=OUT_SKIP), :] = value

    def to_elements(flat, dest, exact):
        flat_to_rows(flat)
        rows = jnp.concatenate(
            [
                jnp.concatenate(
                    [S0[pl.ds(NZ * x + 5 * ez, 8), :], S1[pl.ds(NZ * x + 5 * ez, 8), :]], axis=1
                )
                for ez in range(EZ)
                for x in range(NX)
            ],
            axis=0,
        )
        hi = rows.astype(BF16)
        got = jnp.dot(hi, pick_ref[...], preferred_element_type=F32)
        if exact:
            lo = (rows - hi.astype(F32)).astype(BF16)
            got = got + jnp.dot(lo, pick_ref[...], preferred_element_type=F32)
        result = jnp.zeros((8 * NX, 768), F32)
        for ez in range(EZ):
            piece = got[8 * NX * ez : 8 * NX * (ez + 1)]
            result = jnp.where(jnp.logical_and(lane88 == ez, row88 < 6), piece, result)
        for k in range(6):
            dest[:, k] = result[:, 128 * k : 128 * k + 128].reshape(NX, 8, 128)

    def to_nodes(source, dest):
        full = jnp.concatenate([source[:, k].reshape(8 * NX, 128) for k in range(6)], axis=1)
        hi = full.astype(BF16).astype(F32)
        lo = full - hi
        his = [jnp.where(lane88 == ez, hi, 0.0) for ez in range(EZ)]
        los = [jnp.where(lane88 == ez, lo, 0.0) for ez in range(EZ)]
        got = jnp.dot(
            jnp.concatenate(his, axis=0).astype(BF16), put_ref[...], preferred_element_type=F32
        ) + jnp.dot(
            jnp.concatenate(los, axis=0).astype(BF16), put_ref[...], preferred_element_type=F32
        )
        for ez in range(EZ):
            for x in range(NX):
                at = 8 * NX * ez + 8 * x
                row = PAD + NZ * x + 5 * ez
                Y0[row : row + 6, :] = got[at : at + 6, 0:128]
                Y1[row : row + 6, :] = got[at : at + 6, 128:256]
        rows_to_flat(dest)

    for name in ("map", "stiff", "mass", "tab"):
        fetch[name].wait()
    WJ = tab_ref[24]
    LJ = (tab_ref[25], tab_ref[26])
    corner = map_ref[0:1, :]
    slot = (corner // (NZ * NY) // 5 * EZ + corner // NY % NZ // 5) * EY + corner % NY // 5
    count = EX * EZ * EY
    hot = (
        lax.broadcasted_iota(jnp.int32, (count, count), 0)
        == jnp.broadcast_to(slot, (count, count))
    ).astype(F32)
    geo = jnp.concatenate(
        [stiff_ref[...], mass_ref[...], jnp.zeros((4, count), F32)], axis=0
    )
    part_hi = geo.astype(BF16).astype(F32)
    part_mid = (geo - part_hi).astype(BF16).astype(F32)
    part_lo = geo - part_hi - part_mid
    pack = jnp.concatenate([part_hi, part_mid, part_lo], axis=0).astype(BF16)
    got = lax.dot_general(
        pack, hot.astype(BF16), (((1,), (1,)), ((), ())), preferred_element_type=F32
    )
    sorted_geo = got[0:8] + got[8:16] + got[16:24]
    stack = jnp.zeros((8, 128), F32)
    for q in range(4):
        for ex in range(EX):
            row = jnp.broadcast_to(
                sorted_geo[q : q + 1, 128 * ex : 128 * ex + 128], (8, 128)
            )
            SG[q, ex] = row
            stack = jnp.where(sub_i == EX * q + ex, row, stack)
    csend[...] = stack

    def geometry(h, tile):
        g = [
            [
                jnp.broadcast_to(tile[EX * q + ex : EX * q + ex + 1, :], (8, 128))
                for ex in range(EX)
            ]
            for q in range(4)
        ]
        for ex in range(EX):
            GX[h, 1 + ex] = WJ * g[0][ex]
        for x in range(NX):
            share = [(ex, x - 5 * ex) for ex in range(EX) if 0 <= x - 5 * ex <= 5]
            gy = mac([(float(w[i]), g[2][ex]) for ex, i in share])
            GC[h, 0, x] = WJ * gy
            if h == 1:
                GP[x] = float(w[0]) * gy
            GC[h, 1, x] = mac([(float(w[i]), g[1][ex]) for ex, i in share])
            GC[h, 2, x] = WJ * mac([(float(MASS_SHARE * w[i]), g[3][ex]) for ex, i in share])

    def face_geometry(h, tiles):
        for face, (tile, ex) in enumerate(zip(tiles, (EX - 1, 0))):
            g = [
                jnp.broadcast_to(tile[EX * q + ex : EX * q + ex + 1, :], (8, 128))
                for q in range(4)
            ]
            x = (NX - 1) * face
            GX[h, (EX + 1) * face] = WJ * g[0]
            GE[h, face, 0] = GC[h, 0, x] + WJ * (float(w[0]) * g[2])
            GE[h, face, 1] = GC[h, 1, x] + float(w[0]) * g[1]
            GE[h, face, 2] = GC[h, 2, x] + WJ * (float(MASS_SHARE * w[0]) * g[3])

    def whole_geometry(h, x):
        if x == 0:
            return tuple(GE[h, 0, q] for q in range(3))
        if x == NX - 1:
            return tuple(GE[h, 1, q] for q in range(3))
        return tuple(GC[h, q, x] for q in range(3))

    def diagonal_part(h):
        kj = tab_ref[27]
        for x in range(NX):
            share = [
                (ex, x - 5 * ex) for ex in range(-1, EX + 1) if 0 <= x - 5 * ex <= 5
            ]
            gx = mac([(float(k1[i, i]), GX[h, 1 + ex]) for ex, i in share])
            gy, gz, gm = whole_geometry(h, x)
            base = gx + gz * kj + gm
            for k in range(6):
                W[h, x, k] = float(w[k]) * base + float(k1[k, k]) * gy

    def apply_part(h):
        src, dst = V.at[h], W.at[h]
        for ex in range(EX):
            gx = GX[h, 1 + ex]
            for k in range(6):
                vs = [src[5 * ex + m, k] for m in range(6)]
                gk = float(w[k]) * gx
                for i in range(6):
                    value = gk * mac([(float(k1[i, m]), vs[m]) for m in range(6)])
                    if i == 0 and ex > 0:
                        value = value + dst[5 * ex, k]
                    dst[5 * ex + i, k] = value
        for x in range(NX):
            gy, gz, gm = GC[h, 0, x], GC[h, 1, x], GC[h, 2, x]
            vs = [src[x, m] for m in range(6)]
            for k in range(6):
                vk = vs[k]
                zterm = CT(0) * vk
                for sh in range(1, 8):
                    zterm = zterm + CT(sh) * pltpu.roll(vk, sh, 0)
                value = float(w[k]) * (gz * zterm + gm * vk)
                value = value + gy * mac([(float(k1[k, m]), vs[m]) for m in range(6)])
                dst[x, k] = dst[x, k] + value

    def fold_y(F, planes=range(NX)):
        for x in planes:
            low, high = F[x, 0], F[x, 5]
            F[x, 0] = low + jnp.where(ey > 0, pltpu.roll(high, 1, 1), 0.0)
            F[x, 5] = high + jnp.where(ey < EY - 1, pltpu.roll(low, 127, 1), 0.0)

    def fold_z(F):
        for x in range(NX):
            z0, z5 = F[0, x, :, 0, :], F[0, x, :, 5, :]
            h0, h5 = F[1, x, :, 0, :], F[1, x, :, 5, :]
            z0_up, z5_up = pltpu.roll(z0, EY, 1), pltpu.roll(z5, EY, 1)
            z0_down, z5_down = pltpu.roll(z0, 128 - EY, 1), pltpu.roll(z5, 128 - EY, 1)
            h0_up, h5_up = pltpu.roll(h0, EY, 1), pltpu.roll(h5, EY, 1)
            h0_down, h5_down = pltpu.roll(h0, 128 - EY, 1), pltpu.roll(h5, 128 - EY, 1)
            F[0, x, :, 0, :] = z0 + jnp.where(lane6 < EY, h5_down, z5_up)
            F[0, x, :, 5, :] = z5 + jnp.where(lane6 >= 128 - EY, h0_up, z0_down)
            add0 = jnp.where(group6 == 2, z5_down, h5_up)
            add5 = jnp.where(group6 == 1, z0_up, h0_down)
            F[1, x, :, 0, :] = h0 + jnp.where(group6 == 0, 0.0, add0)
            F[1, x, :, 5, :] = h5 + jnp.where(group6 == 3, 0.0, add5)

    def link(idx, slot_no, src, dst, device):
        return lambda: pltpu.make_async_remote_copy(
            src_ref=src,
            dst_ref=dst,
            send_sem=ex_send.at[idx, slot_no],
            recv_sem=ex_recv.at[idx, slot_no],
            device_id=device,
            device_id_type=MESH,
        )

    def x_links(idx):
        return [
            (has["xl"], has["xh"], link(idx, 1, xsend.at[idx, 0], xrecv.at[idx, 1], (b, s - 1))),
            (has["xh"], has["xl"], link(idx, 0, xsend.at[idx, 1], xrecv.at[idx, 0], (b, s + 1))),
        ]

    def z_links(idx):
        both = jnp.logical_and
        out = [
            (has["zl"], has["zh"], link(idx, 3, zsend.at[idx, 0], zrecv.at[idx, 1], (b - 1, s))),
            (has["zh"], has["zl"], link(idx, 2, zsend.at[idx, 1], zrecv.at[idx, 0], (b + 1, s))),
        ]
        for zs, db, zn, zr in ((0, -1, "zl", "zh"), (1, 1, "zh", "zl")):
            for xside, ds, xn, xr in ((0, -1, "xl", "xh"), (1, 1, "xh", "xl")):
                out.append(
                    (
                        both(has[zn], has[xn]),
                        both(has[zr], has[xr]),
                        link(
                            idx,
                            4 + 2 * (1 - zs) + (1 - xside),
                            zsend.at[idx, zs, (ZT - 1) * xside],
                            drecv.at[idx, 1 - zs, 1 - xside],
                            (b + db, s + ds),
                        ),
                    )
                )
        return out

    def halo_links(idx):
        def one(side, device):
            return lambda: pltpu.make_async_remote_copy(
                src_ref=bsend.at[idx, side, :, :, 0:6, :],
                dst_ref=brecv.at[idx, 1 - side, :, :, 0:6, :],
                send_sem=h_send.at[idx, side],
                recv_sem=h_recv.at[idx, 1 - side],
                device_id=device,
                device_id_type=MESH,
            )

        return [
            (has["zl"], has["zh"], one(0, (b - 1, s))),
            (has["zh"], has["zl"], one(1, (b + 1, s))),
        ]

    def links_start(links):
        for there, _, copy in links:

            @pl.when(there)
            def _(copy=copy):
                copy().start()

    def links_wait(links):
        for _, here, copy in links:

            @pl.when(here)
            def _(copy=copy):
                copy().wait_recv()

    def links_sent(links):
        for there, _, copy in links:

            @pl.when(there)
            def _(copy=copy):
                copy().wait_send()

    def x_start(idx, F):
        xsend[idx, 0] = F[0]
        xsend[idx, 1] = F[NX - 1]
        links_start(x_links(idx))

    def x_end(idx, F):
        links_wait(x_links(idx))
        F[0] = F[0] + xrecv[idx, 0]
        F[NX - 1] = F[NX - 1] + xrecv[idx, 1]

    def exchange_start(idx, F):
        fold_y(F)
        x_start(idx, F)
        z_start(idx, F)

    def z_start(idx, F):
        for t in range(ZT):
            low = high = jnp.zeros((6, 128), F32)
            for m in range(4):
                x = 4 * t + m
                if x >= NX:
                    continue
                low = jnp.where(group6 == m, moved(F[x, :, 0, :], EY * m), low)
                high = jnp.where(group6 == m, moved(F[x, :, 5, :], EY * (m + 1)), high)
            zsend[idx, 0, t, 0:6, :] = low
            zsend[idx, 1, t, 0:6, :] = high
        links_start(z_links(idx))

    def inner_z(F):
        for x in range(NX):
            z0, z5 = F[x, :, 0, :], F[x, :, 5, :]
            F[x, :, 0, :] = z0 + jnp.where(lane6 < EY, 0.0, pltpu.roll(z5, EY, 1))
            F[x, :, 5, :] = z5 + jnp.where(
                lane6 >= 128 - EY, 0.0, pltpu.roll(z0, 128 - EY, 1)
            )

    def outer_z(idx, F):
        links_wait(z_links(idx))
        for x in range(NX):
            t, m = divmod(x, 4)
            near = moved(zrecv[idx, 0, t, 0:6, :], -EY * m)
            far = moved(zrecv[idx, 1, t, 0:6, :], 128 - EY - EY * m)
            if x == 0:
                near = near + moved(drecv[idx, 0, 0, 0:6, :], -EY * LAST)
                far = far + moved(drecv[idx, 1, 0, 0:6, :], 128 - EY - EY * LAST)
            if x == NX - 1:
                near = near + drecv[idx, 0, 1, 0:6, :]
                far = far + moved(drecv[idx, 1, 1, 0:6, :], 128 - EY)
            F[x, :, 0, :] = F[x, :, 0, :] + jnp.where(lane6 < EY, near, 0.0)
            F[x, :, 5, :] = F[x, :, 5, :] + jnp.where(lane6 >= 128 - EY, far, 0.0)

    def exchange_end(idx, F):
        x_end(idx, F)
        inner_z(F)
        outer_z(idx, F)

    def halo_start(idx, src):
        for t in range(ZT):
            for k in range(6):
                low = high = jnp.zeros((8, 128), F32)
                for m in range(4):
                    x = 4 * t + m
                    if x >= NX:
                        continue
                    tile = src(x, k)
                    low = jnp.where(group == m, moved(tile, EY * m), low)
                    high = jnp.where(group == m, moved(tile, EY * (m + 1)), high)
                bsend[idx, 0, t, k] = low
                bsend[idx, 1, t, k] = high

    from_low = jnp.logical_and(group == 1, sub_i < 6)
    from_high = jnp.logical_and(group == 2, sub_i < 6)

    def halo_unpack(idx, store):
        for x in range(NX):
            t, m = divmod(x, 4)
            for k in range(6):
                low = moved(brecv[idx, 0, t, k], EY - EY * m)
                high = moved(brecv[idx, 1, t, k], 2 * EY - EY * m)
                store(x, k, jnp.where(from_low, low, jnp.where(from_high, high, 0.0)))

    near_rows = [
        jnp.where(group6 == 1, float(k1[5, j]), float(k1[0, j])) for j in range(6)
    ]

    def halo_faces():
        rims, faces = [], []
        for x in range(NX):
            rows = [V[1, x, :, j, :] for j in range(6)]
            rim = jnp.where(group6 == 1, rows[5], rows[0])
            across = mac(list(zip(near_rows, rows)))
            rim8 = jnp.concatenate([rim, jnp.zeros((2, 128), F32)], axis=0)
            along = CT(0) * rim8
            for sh in range(1, 8):
                along = along + CT(sh) * pltpu.roll(rim8, sh, 0)
            rims.append(rim)
            faces.append(
                (GC[1, 1, x] * WJ)[0:6] * across
                + GP[x, 0:6] * along[0:6]
                + GC[1, 2, x, 0:6] * (float(w[0]) * rim)
            )
        for ex in range(EX):
            scale = GX[1, 1 + ex, 0:6] * float(w[0])
            for i in range(6):
                x = 5 * ex + i
                faces[x] = faces[x] + scale * mac(
                    [(float(k1[i, m]), rims[5 * ex + m]) for m in range(6)]
                )
        return faces

    def join_halo(F, faces, planes):
        for x in planes:
            z0, z5, face = F[x, :, 0, :], F[x, :, 5, :], faces[x]
            F[x, :, 0, :] = z0 + jnp.where(
                lane6 < EY, pltpu.roll(face, 128 - EY, 1), pltpu.roll(z5, EY, 1)
            )
            F[x, :, 5, :] = z5 + jnp.where(
                lane6 >= 128 - EY, pltpu.roll(face, EY, 1), pltpu.roll(z0, 128 - EY, 1)
            )
        fold_y(F, planes)

    def finish_apply(idx, faces):
        F = W.at[0]
        join_halo(F, faces, (0, NX - 1))
        x_start(idx, F)
        join_halo(F, faces, range(1, NX - 1))
        x_end(idx, F)

    def window_copies(which, src, dst):
        out = []
        for off in range(-REACH, REACH + 1):
            for ds in range(n_sub):
                if off == 0 and ds == 0:
                    continue
                peer_s = lax.rem(s + ds, n_sub)
                target = b + off
                sending = jnp.logical_and(target >= 0, target < n_blk)

                def copy(off=off, ds=ds, peer_s=peer_s, target=target):
                    return pltpu.make_async_remote_copy(
                        src_ref=src,
                        dst_ref=dst.at[REACH - off, s],
                        send_sem=c_send.at[which, REACH + off, ds],
                        recv_sem=c_recv.at[which, REACH - off, s],
                        device_id=(target, peer_s),
                        device_id_type=MESH,
                    )

                def arrive(off=off, ds=ds, peer_s=peer_s, target=target):
                    return pltpu.make_async_remote_copy(
                        src_ref=src,
                        dst_ref=dst.at[REACH + off, peer_s],
                        send_sem=c_send.at[which, REACH + off, ds],
                        recv_sem=c_recv.at[which, REACH + off, peer_s],
                        device_id=(target, peer_s),
                        device_id_type=MESH,
                    )

                out.append((sending, copy, arrive))
        return out

    def window_start(which, src, dst):
        for sending, copy, _ in window_copies(which, src, dst):

            @pl.when(sending)
            def _(copy=copy):
                copy().start()

    def window_wait(which, src, dst):
        for sending, _, arrive in window_copies(which, src, dst):

            @pl.when(sending)
            def _(arrive=arrive):
                arrive().wait_recv()

    def window_sent(which, src, dst):
        for sending, copy, _ in window_copies(which, src, dst):

            @pl.when(sending)
            def _(copy=copy):
                copy().wait_send()

    def velocity(c):
        unpack_flat(lambda at: vel_flat[c, :, at], FL)
        to_elements(FL, VE, False)
        out = VV.at[c]
        rounded = lambda value: value.astype(BF16).astype(F32)
        for ex in range(EX):
            gx = SG[0, ex]
            for k in range(6):
                vs = [VE[5 * ex + m, k] for m in range(6)]
                flux = []
                for i in range(6):
                    grad = mac([(float(Dh[i, m]), vs[m]) for m in range(6)])
                    flux.append(rounded(grad * (WJ * float(w[i] * w[k])) * gx))
                for i in range(6):
                    value = mac([(float(Dh[m, i]), flux[m]) for m in range(6)])
                    if i == 0 and ex > 0:
                        value = value + out[5 * ex, k]
                    out[5 * ex + i, k] = value
        for ex in range(EX):
            gz, gy, gm = SG[1, ex], SG[2, ex], SG[3, ex]
            for i in range(6):
                x = 5 * ex + i
                vs = [VE[x, m] for m in range(6)]
                flux = []
                for k in range(6):
                    grad = mac([(float(Dh[k, m]), vs[m]) for m in range(6)])
                    flux.append(rounded(grad * (WJ * float(w[i] * w[k])) * gy))
                for k in range(6):
                    vk = vs[k]
                    weight = WJ * float(w[i] * w[k])
                    value = mac([(float(Dh[m, k]), flux[m]) for m in range(6)])
                    grad = tab_ref[8] * vk
                    for sh in range(1, 8):
                        grad = grad + tab_ref[8 + sh] * pltpu.roll(vk, sh, 0)
                    fz = rounded(grad * weight * gz)
                    value = value + tab_ref[16] * fz
                    for sh in range(1, 8):
                        value = value + tab_ref[16 + sh] * pltpu.roll(fz, sh, 0)
                    value = value + gm * weight * vk
                    out[x, k] = out[x, k] + value

    geometry(0, stack)
    fetch["load"].wait()
    fetch["pick"].wait()
    unpack_flat(lambda at: load_flat[at], FI)
    to_elements(FI, R.at[0], True)
    halo_start(0, lambda x, k: R[0, x, k])
    crecv[REACH, s] = stack
    for c in range(3):
        fetch["vel%d" % c].wait()

    def component(c, carry):
        velocity(c)

        @pl.when(c == 0)
        def _():
            pl.semaphore_wait(barrier, n_dev - 1)
            window_start(0, csend, crecv)
            links_start(halo_links(0))

        exchange_start(c, VV.at[c])
        return carry

    lax.fori_loop(0, 3, component, 0)

    window_wait(0, csend, crecv)

    def beside(t):
        low, high = crecv[REACH - 1, t], crecv[REACH + 1, t]
        return jnp.where(lane < 2 * EY, pltpu.roll(low, 64, 1), pltpu.roll(high, 64, 1))

    left_s, right_s = jnp.maximum(s - 1, 0), jnp.minimum(s + 1, n_sub - 1)
    left_on = jnp.where(has["xl"], 1.0, 0.0)
    right_on = jnp.where(has["xh"], 1.0, 0.0)
    geometry(1, beside(s))
    face_geometry(0, (crecv[REACH, left_s] * left_on, crecv[REACH, right_s] * right_on))
    face_geometry(1, (beside(left_s) * left_on, beside(right_s) * right_on))
    for h in range(2):
        diagonal_part(h)
    fold_z(W)
    for h in range(2):
        fold_y(W.at[h])
    for h in range(2):
        for x in range(NX):
            for k in range(6):
                full = W[h, x, k]
                good = full > 0.0
                INV[h, x, k] = jnp.where(good, DAMPING / jnp.where(good, full, 1.0), 0.0)

    corners = [(a, c, d) for a in (0, 1) for c in (0, 1) for d in (0, 1)]

    def stencil(z, carry):
        shifted = {}
        for c in (0, 1):
            for q in range(4):
                base = CF[z + 1 - c, q]
                for a in (0, 1):
                    up = pltpu.roll(base, 1, 0) if a else base
                    shifted[a, c, 0, q] = up
                    shifted[a, c, 1, q] = pltpu.roll(up, 1, 1)
        total = {}
        for ui, u in enumerate(corners):
            for vi, v in enumerate(corners):
                key = tuple(v[t] - u[t] for t in range(3))
                term = mac([(float(coarse[q][ui, vi]), shifted[u + (q,)]) for q in range(4)])
                total[key] = term if key not in total else total[key] + term
        for key, value in total.items():
            ST[z, 9 * (key[0] + 1) + 3 * (key[1] + 1) + key[2] + 1] = value
        diag = total[0, 0, 0]
        ST[z, 27] = jnp.where(diag > 0.0, 1.0 / jnp.where(diag > 0.0, diag, 1.0), 0.0)
        return carry

    for x in range(NX):
        for k in range(6):
            V[0, x, k] = R[0, x, k] * INV[0, x, k]
    apply_part(0)
    links_wait(halo_links(0))

    def first_halo(x, k, tile):
        V[1, x, k] = tile * INV[1, x, k]

    halo_unpack(0, first_halo)
    finish_apply(5, halo_faces())
    for x in range(NX):
        for k in range(6):
            V[0, x, k] = V[0, x, k] + (R[0, x, k] - W[0, x, k]) * INV[0, x, k]
    apply_part(0)
    fold_y(W.at[0])
    x_start(3, W.at[0])

    one = jnp.ones((8, 128), F32)
    wz = jnp.where(sub_i < 5, one, 0.0)
    wz = jnp.where(jnp.logical_and(sub_i == 5, lane >= 128 - EY), 1.0, wz)
    low_half = jnp.where(has["zl"], 0.5, 1.0)
    high_half = jnp.where(has["zh"], 0.5, 1.0)
    wz = wz * jnp.where(jnp.logical_and(sub_i == 0, lane < EY), low_half, 1.0)
    wz = wz * jnp.where(jnp.logical_and(sub_i == 5, lane >= 128 - EY), high_half, 1.0)
    wend = wz * jnp.where(ey == EY - 1, 1.0, 0.0)
    xlow = jnp.where(has["xl"], 0.5, 1.0)
    xhigh = jnp.where(has["xh"], 0.5, 1.0)

    def unique(x, k):
        tile = wz if k < 5 else wend
        if x == 0:
            tile = tile * xlow
        if x == NX - 1:
            tile = tile * xhigh
        return tile

    acc = [[None, None] for _ in range(EX + 1)]
    for x in range(NX):
        rows = [unique(x, k) * R[0, x, k] - W[0, x, k] for k in range(5)]
        last_row = unique(x, 5) * R[0, x, 5] - W[0, x, 5]
        rows.append(jnp.where(ey == EY - 1, last_row, 0.0))
        lines = [mac([(float(lin[k, d]), rows[k]) for k in range(6)]) for d in (0, 1)]
        ex = min(x // 5, EX - 1)
        i = x - 5 * ex
        for a in (0, 1):
            weight = float(lin[i, a])
            if weight == 0.0:
                continue
            for d in (0, 1):
                term = weight * lines[d]
                old = acc[ex + a][d]
                acc[ex + a][d] = term if old is None else old + term
    pieces = {}
    for c in (0, 1):
        for d in (0, 1):
            tile = jnp.zeros((8, 128), F32)
            for xv in range(EX + 1):
                row = jnp.sum(LJ[c] * acc[xv][d], axis=0, keepdims=True)
                tile = jnp.where(sub_i == xv, jnp.broadcast_to(row, (8, 128)), tile)
            pieces[c, d] = tile
    placed = [None] * (EZ + 1)
    for c in (0, 1):
        for ez in range(EZ):
            sums = None
            for d in (0, 1):
                tile = jnp.where(lane < EY, moved(pieces[c, d], -EY * ez), 0.0)
                if d:
                    tile = pltpu.roll(tile, 1, 1)
                sums = tile if sums is None else sums + tile
            old = placed[ez + c]
            placed[ez + c] = sums if old is None else old + sums
    message = placed[0]
    for zv in range(1, EZ + 1):
        rows_at, lanes_at = divmod(zv, 3)
        tile = moved(placed[zv], (EY + 8) * lanes_at)
        if rows_at:
            tile = pltpu.roll(tile, (EX + 1) * rows_at, 0)
        message = message + tile
    rsend[...] = message
    rrecv[REACH, s] = message
    window_start(1, rsend, rrecv)

    z_start(3, W.at[0])
    x_end(3, W.at[0])
    inner_z(W.at[0])
    halo_start(1, lambda x, k: V[0, x, k] + (R[0, x, k] - W[0, x, k]) * INV[0, x, k])
    links_start(halo_links(1))
    for o in range(SPAN):
        for t in range(n_sub):
            packed = crecv[o, t]
            for ez in range(EZ):
                if not ZLO - 1 <= EZ * o + ez <= ZHI:
                    continue
                tile = jnp.where(lane < EY, moved(packed, -EY * ez), 0.0)
                for q in range(4):
                    CF[EZ * o + ez + 1, q, EX * t : EX * t + EX, :] = tile[
                        EX * q : EX * q + EX, :
                    ]

    lax.fori_loop(ZLO, ZHI + 1, stencil, 0)
    outer_z(3, W.at[0])
    for x in range(NX):
        for k in range(6):
            V[0, x, k] = V[0, x, k] + (R[0, x, k] - W[0, x, k]) * INV[0, x, k]

    fetch["put"].wait()

    def velocity_out(c):
        exchange_end(c, VV.at[c])
        to_nodes(VV.at[c], FP)

        def store(at, tile):
            vel_back[c, :, at] = tile.reshape(1, tile.size)

        pack_flat(lambda p, n: FP[PAD + p : PAD + p + n, :], store)
        pltpu.make_async_copy(
            vel_back.at[c], velout_hbm.at[c], out_sem.at[c]
        ).start()

    velocity_out(0)
    window_wait(1, rsend, rrecv)

    def window_sum(o, zv):
        rows_at, lanes_at = divmod(zv, 3)
        total = None
        for t in range(n_sub):
            tile = moved(rrecv[o, t], -(EY + 8) * lanes_at)
            here = jnp.logical_and(
                sub_i >= (EX + 1) * rows_at, sub_i < (EX + 1) * (rows_at + 1)
            )
            tile = jnp.where(jnp.logical_and(here, lane <= EY), tile, 0.0)
            if xs > 8:
                tile = jnp.concatenate([tile, jnp.zeros((xs - 8, 128), F32)], axis=0)
            shift = (EX * t - (EX + 1) * rows_at) % xs
            if shift:
                tile = pltpu.roll(tile, shift, 0)
            total = tile if total is None else total + tile
        return total

    center = (SPECTRUM_HIGH + SPECTRUM_LOW) / 2.0
    radius = (SPECTRUM_HIGH - SPECTRUM_LOW) / 2.0
    ratio = center / radius
    factor = 1.0 / ratio
    for z in range(ZLO, ZHI + 1):
        o, zv = divmod(z, EZ)
        value = window_sum(o, zv)
        if zv == 0 and o > 0:
            value = value + window_sum(o - 1, EZ)
        CR[z] = value
        CU[0, z] = value * ST[z, 27] * (1.0 / center)
    first, last = FIRST - HALO, LAST_V + HALO
    sol = {z: CU[0, z] for z in range(first, last + 1)}
    for sweep in range(CHEB_ITERS - 1):
        now, later = sweep % 2, (sweep + 1) % 2
        left = CHEB_ITERS - 2 - sweep
        nxt = 1.0 / (2.0 * ratio - factor)
        wide = {}
        for z in range(first - left, last + left + 1):
            for zz in (z - 1, z, z + 1):
                if zz in wide:
                    continue
                base = CU[now, zz]
                sides = {}
                for dx in (-1, 0, 1):
                    mx = base if dx == 0 else pltpu.roll(base, (-dx) % xs, 0)
                    for dy in (-1, 0, 1):
                        sides[dx, dy] = mx if dy == 0 else pltpu.roll(mx, (-dy) % 128, 1)
                wide[zz] = sides
            total = None
            for dz in (-1, 0, 1):
                for dx in (-1, 0, 1):
                    for dy in (-1, 0, 1):
                        term = ST[z, 9 * (dx + 1) + 3 * (dz + 1) + dy + 1] * wide[z + dz][dx, dy]
                        total = term if total is None else total + term
            residual = CR[z] - total
            CR[z] = residual
            fresh = (nxt * factor) * CU[now, z] + (2.0 * nxt / radius) * (residual * ST[z, 27])
            CU[later, z] = fresh
            if first <= z <= last:
                sol[z] = sol[z] + fresh
        factor = nxt

    own = {}
    for z, tile in sol.items():
        shifted_x = tile
        for t in range(1, n_sub):
            shifted_x = jnp.where(s == t, pltpu.roll(tile, (-EX * t) % xs, 0), shifted_x)
        own[z - FIRST] = shifted_x

    links_wait(halo_links(1))

    def base_halo(x, k, tile):
        V[1, x, k] = tile

    halo_unpack(1, base_halo)
    for x in range(NX):
        z0, z5 = V[0, x, :, 0, :], V[0, x, :, 5, :]
        V[1, x, :, 5, :] = jnp.where(
            group6 == 1, pltpu.roll(z0, EY, 1), V[1, x, :, 5, :]
        )
        V[1, x, :, 0, :] = jnp.where(
            group6 == 2, pltpu.roll(z5, 128 - EY, 1), V[1, x, :, 0, :]
        )

    ZJ = tab_ref[28]
    for h in range(2):
        places = range(EZ) if h == 0 else (-2, -1, EZ, EZ + 1)
        corner_tiles = {}
        for c in (0, 1):
            for d in (0, 1):
                total = None
                for at, ez in enumerate(places):
                    tile = own[ez + c]
                    if d:
                        tile = pltpu.roll(tile, 127, 1)
                    tile = moved(jnp.where(lane[0:1] < EY, tile, 0.0), EY * at)
                    total = tile if total is None else total + tile
                corner_tiles[c, d] = total
        val, zdif, ydif = {}, {}, {}
        for xv in range(-1, EX + 2):
            at = xv % xs
            rows = {
                key: jnp.broadcast_to(tile[at : at + 1, :], (8, 128))
                for key, tile in corner_tiles.items()
            }
            ends = [LJ[0] * rows[0, d] + LJ[1] * rows[1, d] for d in (0, 1)]
            val[xv] = [mac([(float(lin[k, d]), ends[d]) for d in (0, 1)]) for k in range(6)]
            if 0 <= xv <= EX:
                jump = [ZJ * (rows[0, d] - rows[1, d]) for d in (0, 1)]
                zdif[xv] = [
                    mac([(float(lin[k, d]), jump[d]) for d in (0, 1)]) for k in range(6)
                ]
                ydif[xv] = 0.5 * (ends[0] - ends[1])
        for x in range(NX):
            ex = min(x // 5, EX - 1)
            i = x - 5 * ex
            parts = [(float(lin[i, a]), ex + a) for a in (0, 1)]
            gy, gz, gm = whole_geometry(h, x)
            slope = gy * mac([(weight, ydif[xv]) for weight, xv in parts])
            for k in range(6):
                u = mac([(weight, val[xv][k]) for weight, xv in parts])
                inside = gz * mac([(weight, zdif[xv][k]) for weight, xv in parts]) + gm * u
                if x % 5 == 0:
                    xv = x // 5
                    inside = inside + GX[h, xv] * (0.5 * (val[xv][k] - val[xv - 1][k]))
                    inside = inside + GX[h, xv + 1] * (0.5 * (val[xv][k] - val[xv + 1][k]))
                value = float(w[k]) * inside
                if k == 0:
                    value = value + slope
                if k == 5:
                    value = value - slope
                W[h, x, k] = value
                V[h, x, k] = V[h, x, k] + u
    fold_z(W)
    for h in range(2):
        fold_y(W.at[h])
    for h in range(2):
        for x in range(NX):
            for k in range(6):
                V[h, x, k] = V[h, x, k] - W[h, x, k] * INV[h, x, k]
    apply_part(0)
    finish_apply(6, halo_faces())
    for x in range(NX):
        for k in range(6):
            V[0, x, k] = V[0, x, k] + (R[0, x, k] - W[0, x, k]) * INV[0, x, k]
    apply_part(0)
    num = jnp.zeros((8, 128), F32)
    den = jnp.zeros((8, 128), F32)
    for x in range(NX):
        for k in range(6):
            v = V[0, x, k]
            num = num + unique(x, k) * R[0, x, k] * v
            den = den + v * W[0, x, k]
    num_row = jnp.sum(num, axis=0, keepdims=True)
    den_row = jnp.sum(den, axis=0, keepdims=True)
    num_one = jnp.sum(num_row, axis=1, keepdims=True)
    den_one = jnp.sum(den_row, axis=1, keepdims=True)
    lane1 = lax.broadcasted_iota(jnp.int32, (1, 128), 1)
    psend[...] = jnp.where(lane1 < 64, num_one, den_one)

    def scatter(d, carry):
        pltpu.make_async_remote_copy(
            src_ref=psend,
            dst_ref=precv.at[d - 1],
            send_sem=p_sem.at[0],
            recv_sem=p_sem.at[1],
            device_id=device_of(lax.rem(me + d, n_dev)),
            device_id_type=MESH,
        ).start()
        return carry

    lax.fori_loop(1, n_dev, scatter, 0)
    exchange_start(4, W.at[0])
    for c in (1, 2):
        velocity_out(c)
    to_nodes(V.at[0], FP)
    exchange_end(4, W.at[0])
    to_nodes(W.at[0], FR)
    whole = pltpu.make_async_remote_copy(
        src_ref=precv,
        dst_ref=precv,
        send_sem=p_sem.at[0],
        recv_sem=p_sem.at[1],
        device_id=(b, s),
        device_id_type=MESH,
    )
    whole.wait_recv()
    both = psend[...] + jnp.sum(precv[...], axis=0)
    step = both[0:1, 0:1] / both[0:1, 64:65]

    def store_to(back):
        def store(at, tile):
            back[at] = tile.reshape(tile.size)

        return store

    pack_flat(lambda p, n: step * FP[PAD + p : PAD + p + n, :], store_to(pres_back))
    pack_flat(
        lambda p, n: FI[PAD + p : PAD + p + n, :] - step * FR[PAD + p : PAD + p + n, :],
        store_to(res_back),
    )
    backs = [
        pltpu.make_async_copy(pres_back, pres_hbm, out_sem.at[3]),
        pltpu.make_async_copy(res_back, res_hbm, out_sem.at[4]),
    ]
    for copy in backs:
        copy.start()
    whole.wait_send()
    for idx in range(5):
        links_sent(x_links(idx) + z_links(idx))
    for idx in range(5, EXCH):
        links_sent(x_links(idx))
    for idx in range(2):
        links_sent(halo_links(idx))
    window_sent(0, csend, crecv)
    window_sent(1, rsend, rrecv)
    for c in range(3):
        pltpu.make_async_copy(vel_back.at[c], velout_hbm.at[c], out_sem.at[c]).wait()
    for copy in backs:
        copy.wait()


def place(vel_in, pres_in, res_in, vel_out, pres_out, res_out, vel, pres, res, sem):
    pairs = [(vel_in.at[c], vel.at[c], vel_out.at[pl.ds(c, 1)]) for c in range(3)]
    pairs += [(pres_in, pres, pres_out), (res_in, res, res_out)]
    loads = [pltpu.make_async_copy(p[0], p[1], sem.at[0, i]) for i, p in enumerate(pairs)]
    stores = [pltpu.make_async_copy(p[1], p[2], sem.at[1, i]) for i, p in enumerate(pairs)]
    for copy in loads:
        copy.start()
    for load, store in zip(loads, stores):
        load.wait()
        store.start()
    for copy in stores:
        copy.wait()


def solution(mesh):
    n_blk, n_sub = mesh.shape["blk"], mesh.shape["sub"]
    n_dev = n_blk * n_sub
    xs = -(-(EX * n_sub + 2) // 8) * 8
    D, w, k1, lin, coarse = tables()
    Dh = bf16_round(D)
    tab = np.concatenate(
        [
            roll_tables(k1),
            roll_tables(Dh),
            roll_tables(Dh.T),
            col_tile(w),
            col_tile(lin[:, 0]),
            col_tile(lin[:, 1]),
            col_tile(np.diag(k1)),
            col_tile([0.5, 0.0, 0.0, 0.0, 0.0, -0.5]),
        ]
    )
    pick, put = pick_matrices()

    def per_device(velocity, pressure_load, local_map, stiff_geo, mass_geo):
        field = (NX, 6, 8, 128)
        reach_in = NY * (IN_STEP - 1) // 128 + 3 + 7 * IN_SKIP
        reach_out = FLAT + 8 * OUT_SKIP
        flat = pltpu.VMEM((PAD + -(-max(reach_in, reach_out) // 8) * 8, 128), F32)
        out_rows = PAD + -(-(ROWS + 8 * OUT_STEP + 2) // 8) * 8
        out = pl.pallas_call(
            functools.partial(kernel, n_blk, n_sub, xs),
            out_shape=(
                jax.ShapeDtypeStruct((3, 1, NLOC), F32),
                jax.ShapeDtypeStruct((NLOC,), F32),
                jax.ShapeDtypeStruct((NLOC,), F32),
            ),
            in_specs=[pl.BlockSpec(memory_space=pl.ANY)] * 8,
            out_specs=(pl.BlockSpec(memory_space=pl.ANY),) * 3,
            scratch_shapes=[
                pltpu.VMEM((3, 1, NLOC), F32),
                pltpu.VMEM((NLOC,), F32),
                pltpu.VMEM((3, 1, NLOC), F32),
                pltpu.VMEM((NLOC,), F32),
                pltpu.VMEM((NLOC,), F32),
                flat,
                flat,
                flat,
                flat,
                pltpu.VMEM((IN_ROWS, 128), F32),
                pltpu.VMEM((IN_ROWS, 128), F32),
                pltpu.VMEM((out_rows, 128), F32),
                pltpu.VMEM((out_rows, 128), F32),
                pltpu.VMEM((3, EX * EZ * EY), F32),
                pltpu.VMEM((1, EX * EZ * EY), F32),
                pltpu.VMEM(tab.shape, F32),
                pltpu.VMEM(pick.shape, BF16),
                pltpu.VMEM(put.shape, BF16),
                pltpu.VMEM((2,) + field, F32),
                pltpu.VMEM((2,) + field, F32),
                pltpu.VMEM((8, EX * EZ * EY), jnp.int32),
                pltpu.VMEM((1,) + field, F32),
                pltpu.VMEM((2,) + field, F32),
                pltpu.VMEM((3,) + field, F32),
                pltpu.VMEM(field, F32),
                pltpu.VMEM((2, EX + 2, 8, 128), F32),
                pltpu.VMEM((2, 3, NX, 8, 128), F32),
                pltpu.VMEM((2, 2, 3, 8, 128), F32),
                pltpu.VMEM((NX, 8, 128), F32),
                pltpu.VMEM((4, EX, 8, 128), F32),
                pltpu.VMEM((EXCH, 2, 6, 8, 128), F32),
                pltpu.VMEM((EXCH, 2, 6, 8, 128), F32),
                pltpu.VMEM((EXCH, 2, ZT, 8, 128), F32),
                pltpu.VMEM((EXCH, 2, ZT, 8, 128), F32),
                pltpu.VMEM((EXCH, 2, 2, 8, 128), F32),
                pltpu.VMEM((8, 128), F32),
                pltpu.VMEM((SPAN, n_sub, 8, 128), F32),
                pltpu.VMEM((8, 128), F32),
                pltpu.VMEM((SPAN, n_sub, 8, 128), F32),
                pltpu.VMEM((2, 2, ZT, 6, 8, 128), F32),
                pltpu.VMEM((2, 2, ZT, 6, 8, 128), F32),
                pltpu.VMEM((NZV + 1, 4, xs, 128), F32),
                pltpu.VMEM((NZV, 28, xs, 128), F32),
                pltpu.VMEM((2, NZV, xs, 128), F32),
                pltpu.VMEM((NZV, xs, 128), F32),
                pltpu.VMEM((1, 128), F32),
                pltpu.VMEM((n_dev - 1, 1, 128), F32),
                pltpu.SemaphoreType.DMA((EXCH, 8)),
                pltpu.SemaphoreType.DMA((EXCH, 8)),
                pltpu.SemaphoreType.DMA((2, SPAN, n_sub)),
                pltpu.SemaphoreType.DMA((2, SPAN, n_sub)),
                pltpu.SemaphoreType.DMA((2, 2)),
                pltpu.SemaphoreType.DMA((2, 2)),
                pltpu.SemaphoreType.DMA((2,)),
                pltpu.SemaphoreType.DMA((10,)),
                pltpu.SemaphoreType.DMA((5,)),
            ],
            compiler_params=pltpu.CompilerParams(
                collective_id=0, has_side_effects=True, vmem_limit_bytes=60 << 20
            ),
        )(
            velocity,
            pressure_load,
            local_map,
            stiff_geo,
            mass_geo.reshape(1, mass_geo.shape[0]),
            jnp.asarray(tab, F32),
            jnp.asarray(pick, BF16),
            jnp.asarray(put, BF16),
        )
        any_spec = pl.BlockSpec(memory_space=pl.ANY)
        return tuple(
            pl.pallas_call(
                place,
                out_shape=(
                    jax.ShapeDtypeStruct((3, NLOC), F32),
                    jax.ShapeDtypeStruct((NLOC,), F32),
                    jax.ShapeDtypeStruct((NLOC,), F32),
                ),
                in_specs=[any_spec] * 3,
                out_specs=(any_spec,) * 3,
                scratch_shapes=[
                    pltpu.VMEM((3, 1, NLOC), F32),
                    pltpu.VMEM((NLOC,), F32),
                    pltpu.VMEM((NLOC,), F32),
                    pltpu.SemaphoreType.DMA((2, 5)),
                ],
            )(*out)
        )

    in_specs = (
        P(None, ("blk", "sub")),
        P(("blk", "sub")),
        P(None, ("blk", "sub")),
        P(None, ("blk", "sub")),
        P(("blk", "sub")),
    )
    out_specs = (P(None, ("blk", "sub")), P(("blk", "sub")), P(("blk", "sub")))
    return jax.shard_map(
        per_device, mesh=mesh, in_specs=in_specs, out_specs=out_specs, check_vma=False
    )
```

```python
import functools
import math

import jax
import jax.numpy as jnp
import numpy as np
from jax import lax
from jax.experimental import pallas as pl
from jax.experimental.pallas import tpu as pltpu
from jax.sharding import PartitionSpec as P

EX = 2
EZ = 4
EY = 32
CHEB_ITERS = 8
NX = 5 * EX + 1
NZ = 5 * EZ + 1
NY = 5 * EY + 1
NLOC = NX * NZ * NY
NZP = 24
NYP = 256
HALO = 2
DEPTH = CHEB_ITERS - 1 + HALO
REACH = -(-DEPTH // EZ)
SPAN = 2 * REACH + 1
NZV = SPAN * EZ + 1
FIRST = REACH * EZ
LAST_V = FIRST + EZ
ZLO = FIRST - DEPTH
ZHI = LAST_V + DEPTH
EXCH = 7
ZT = -(-NX // 4)
ROWS = NX * NZ
IN_STEP = next(k for k in range(1, 129) if NY * k % 128 == 127)
IN_SKIP = (NY * IN_STEP + 1) // 128
IN_ROWS = 8 * IN_STEP
OUT_STEP, OUT_SKIP = next(
    (r, p) for r in range(1, 129) for p in (NY * r // 128,) if 0 < NY * r - 128 * p <= 4
)
OUT_DRIFT = NY * OUT_STEP - 128 * OUT_SKIP
FLAT = -(-NLOC // 128)
FULL = NLOC // 1024
PAD = 8
LAST = (NX - 1) % 4

DAMPING = 0.3
MASS_SHARE = 0.05
SPECTRUM_LOW = 0.15
SPECTRUM_HIGH = 4.5
MESH = pl.DeviceIdType.MESH
F32 = jnp.float32
BF16 = jnp.bfloat16


def tables():
    seven_root = math.sqrt(7.0)
    inner = math.sqrt(1.0 / 3.0 - 2.0 * seven_root / 21.0)
    outer = math.sqrt(1.0 / 3.0 + 2.0 * seven_root / 21.0)
    xi = np.array([-1.0, -outer, -inner, inner, outer, 1.0])
    leg = (63.0 * xi**5 - 70.0 * xi**3 + 15.0 * xi) / 8.0
    w = 2.0 / (30.0 * leg**2)
    D = np.zeros((6, 6))
    for i in range(6):
        for j in range(6):
            if i != j:
                D[i, j] = leg[i] / (leg[j] * (xi[i] - xi[j]))
    D[0, 0] = -7.5
    D[5, 5] = 7.5
    k1 = D.T @ (w[:, None] * D)
    lin = np.stack([(1.0 - xi) / 2.0, (1.0 + xi) / 2.0], 1)
    kc = lin.T @ k1 @ lin
    mc = lin.T @ (w[:, None] * lin)
    coarse = [
        np.kron(np.kron(kc, mc), mc),
        np.kron(np.kron(mc, kc), mc),
        np.kron(np.kron(mc, mc), kc),
        MASS_SHARE * np.kron(np.kron(mc, mc), mc),
    ]
    return D, w, k1, lin, coarse


def roll_tables(M):
    out = np.zeros((8, 8, 128), np.float32)
    for s in range(8):
        for j in range(6):
            m = (j - s) % 8
            if m < 6:
                out[s, j, :] = M[j, m]
    return out


def col_tile(values):
    tile = np.zeros((1, 8, 128), np.float32)
    tile[0, :6, :] = np.asarray(values)[:, None]
    return tile


def bf16_round(a):
    return np.asarray(a, np.float32).astype(np.dtype(BF16)).astype(np.float64)


def pick_matrices():
    pick = np.zeros((NYP, 6, 128), np.float32)
    put = np.zeros((6, 128, NYP), np.float32)
    for k in range(6):
        for z in range(EZ):
            for e in range(EY):
                pick[5 * e + k, k, z * EY + e] = 1.0
                if k < 5 or e == EY - 1:
                    put[k, z * EY + e, 5 * e + k] = 1.0
    return pick.reshape(NYP, 768), put.reshape(768, NYP)


def mac(pairs):
    total = None
    for coef, value in pairs:
        if isinstance(coef, (float, int)) and coef == 0.0:
            continue
        term = coef * value
        total = term if total is None else total + term
    return total


def kernel(
    n_blk,
    n_sub,
    xs,
    vel_hbm,
    load_hbm,
    map_hbm,
    stiff_hbm,
    mass_hbm,
    tab_hbm,
    pick_hbm,
    put_hbm,
    vel_back,
    pres_back,
    res_back,
    vel_flat,
    load_flat,
    FL,
    FI,
    FP,
    FR,
    S0,
    S1,
    Y0,
    Y1,
    stiff_ref,
    mass_ref,
    tab_ref,
    pick_ref,
    put_ref,
    V,
    W,
    map_ref,
    R,
    INV,
    VV,
    VE,
    GX,
    GC,
    GE,
    GP,
    SG,
    xsend,
    xrecv,
    zsend,
    zrecv,
    drecv,
    csend,
    crecv,
    rsend,
    rrecv,
    bsend,
    brecv,
    CF,
    ST,
    CU,
    CR,
    psend,
    precv,
    ex_send,
    ex_recv,
    c_send,
    c_recv,
    h_send,
    h_recv,
    p_sem,
    in_sem,
):
    D, w, k1, lin, coarse = tables()
    Dh = bf16_round(D)
    n_dev = n_blk * n_sub
    b = lax.axis_index("blk")
    s = lax.axis_index("sub")
    me = b * n_sub + s

    def device_of(linear):
        return (linear // n_sub, lax.rem(linear, n_sub))

    barrier = pltpu.get_barrier_semaphore()

    def greet(d, carry):
        pl.semaphore_signal(
            barrier, inc=1, device_id=device_of(lax.rem(me + d, n_dev)), device_id_type=MESH
        )
        return carry

    lax.fori_loop(1, n_dev, greet, 0)

    fetch = {}
    for at, (name, src, dst) in enumerate(
        (
            ("map", map_hbm.at[0:8, :], map_ref),
            ("stiff", stiff_hbm, stiff_ref),
            ("mass", mass_hbm, mass_ref),
            ("tab", tab_hbm, tab_ref),
            ("load", load_hbm, load_flat),
            ("pick", pick_hbm, pick_ref),
            ("vel0", vel_hbm.at[0:1], vel_flat.at[0]),
            ("vel1", vel_hbm.at[1:2], vel_flat.at[1]),
            ("vel2", vel_hbm.at[2:3], vel_flat.at[2]),
            ("put", put_hbm, put_ref),
        )
    ):
        fetch[name] = pltpu.make_async_copy(src, dst, in_sem.at[at])
        fetch[name].start()

    has = {
        "xl": s > 0,
        "xh": s < n_sub - 1,
        "zl": b > 0,
        "zh": b < n_blk - 1,
    }

    def zero(ref_slice):
        ref_slice[...] = jnp.zeros(ref_slice.shape, F32)

    for side, name in ((0, "xl"), (1, "xh")):

        @pl.when(jnp.logical_not(has[name]))
        def _(side=side):
            zero(xrecv.at[:, side])

    for side, name in ((0, "zl"), (1, "zh")):

        @pl.when(jnp.logical_not(has[name]))
        def _(side=side):
            zero(zrecv.at[:, side])
            zero(brecv.at[:, side])

    for zs, zname in ((0, "zl"), (1, "zh")):
        for xside, xname in ((0, "xl"), (1, "xh")):

            @pl.when(jnp.logical_not(jnp.logical_and(has[zname], has[xname])))
            def _(zs=zs, xside=xside):
                zero(drecv.at[:, zs, xside])

    for o in range(SPAN):
        off = o - REACH

        @pl.when(jnp.logical_or(b + off < 0, b + off >= n_blk))
        def _(o=o):
            zero(crecv.at[o])
            zero(rrecv.at[o])

    CF[...] = jnp.zeros(CF.shape, F32)

    lane = lax.broadcasted_iota(jnp.int32, (8, 128), 1)
    sub_i = lax.broadcasted_iota(jnp.int32, (8, 128), 0)
    lane88 = lax.broadcasted_iota(jnp.int32, (8 * NX, 768), 1) // EY % EZ
    row88 = lax.broadcasted_iota(jnp.int32, (8 * NX, 768), 0) % 8
    ey = lane % EY
    lane6 = lax.broadcasted_iota(jnp.int32, (6, 128), 1)
    group6 = lane6 // EY
    group = lane // EY
    CT = lambda q: tab_ref[q]

    def moved(tile, shift):
        return tile if shift % 128 == 0 else pltpu.roll(tile, shift % 128, 1)

    slant_in = lane - sub_i
    slant_out = lane - OUT_DRIFT * sub_i

    def spin(tile, shift, stride):
        shift = shift % 128
        if shift + 7 * stride > 128:
            tile, shift = pltpu.roll(tile, shift, 1), 0
        return pltpu.roll(tile, shift, 1, stride=stride, stride_axis=0)

    chunks = [(8 * i, 8, 1024) for i in range(FULL)]
    chunks += [(p, 1, min(128, NLOC - 128 * p)) for p in range(8 * FULL, FLAT)]

    def unpack_flat(source, dest):
        for p, n, size in chunks:
            dest[PAD + p : PAD + p + n, 0 : size // n] = source(
                pl.ds(128 * p, size)
            ).reshape(n, size // n)

    def pack_flat(tile, store):
        for p, n, size in chunks:
            store(pl.ds(128 * p, size), tile(p, n)[:, 0 : size // n])

    def flat_to_rows(flat):
        for r in range(IN_STEP):
            q, at = divmod(NY * r, 128)
            if at < 7:
                q, at = q - 1, at + 128
            a, b_, c = (
                spin(flat[pl.ds(PAD + q + n, 8, stride=IN_SKIP), :], -at, 1) for n in range(3)
            )
            first_part = slant_in < 128 - at
            if at > 128:
                b_low = jnp.where(slant_in < 256 - at, b_, c)
            else:
                b_low = b_
            S0[pl.ds(r, 8, stride=IN_STEP), :] = jnp.where(first_part, a, b_low)
            S1[pl.ds(r, 8, stride=IN_STEP), :] = jnp.where(
                lane < NY - 128, jnp.where(first_part, b_, c), 0.0
            )

    def rows_to_flat(dest):
        for block in range(0, FLAT, 8 * OUT_SKIP):
            for step in range(OUT_SKIP):
                p = block + step
                if p >= FLAT:
                    continue
                r, y = divmod(128 * p, NY)
                if y < 7 * OUT_DRIFT:
                    r, y = r - 1, y + NY

                def piece(ref, row, turn):
                    return spin(
                        ref[pl.ds(PAD + row, 8, stride=OUT_STEP), :], turn, OUT_DRIFT
                    )

                value = piece(Y1, r, -y)
                if y - 7 * OUT_DRIFT < 128:
                    value = jnp.where(slant_out < 128 - y, piece(Y0, r, -y), value)
                if y + 127 >= NY:
                    after = piece(Y0, r + 1, NY - y)
                    if y + 127 >= NY + 128:
                        after = jnp.where(
                            slant_out < NY + 128 - y, after, piece(Y1, r + 1, NY - y)
                        )
                    value = jnp.where(slant_out < NY - y, value, after)
                dest[pl.ds(PAD + p, 8, stride=OUT_SKIP), :] = value

    def to_elements(flat, dest, exact):
        flat_to_rows(flat)
        rows = jnp.concatenate(
            [
                jnp.concatenate(
                    [S0[pl.ds(NZ * x + 5 * ez, 8), :], S1[pl.ds(NZ * x + 5 * ez, 8), :]], axis=1
                )
                for ez in range(EZ)
                for x in range(NX)
            ],
            axis=0,
        )
        hi = rows.astype(BF16)
        got = jnp.dot(hi, pick_ref[...], preferred_element_type=F32)
        if exact:
            lo = (rows - hi.astype(F32)).astype(BF16)
            got = got + jnp.dot(lo, pick_ref[...], preferred_element_type=F32)
        result = jnp.zeros((8 * NX, 768), F32)
        for ez in range(EZ):
            piece = got[8 * NX * ez : 8 * NX * (ez + 1)]
            result = jnp.where(jnp.logical_and(lane88 == ez, row88 < 6), piece, result)
        for k in range(6):
            dest[:, k] = result[:, 128 * k : 128 * k + 128].reshape(NX, 8, 128)

    def to_nodes(source, dest):
        full = jnp.concatenate([source[:, k].reshape(8 * NX, 128) for k in range(6)], axis=1)
        hi = full.astype(BF16).astype(F32)
        lo = full - hi
        his = [jnp.where(lane88 == ez, hi, 0.0) for ez in range(EZ)]
        los = [jnp.where(lane88 == ez, lo, 0.0) for ez in range(EZ)]
        got = jnp.dot(
            jnp.concatenate(his, axis=0).astype(BF16), put_ref[...], preferred_element_type=F32
        ) + jnp.dot(
            jnp.concatenate(los, axis=0).astype(BF16), put_ref[...], preferred_element_type=F32
        )
        for ez in range(EZ):
            for x in range(NX):
                at = 8 * NX * ez + 8 * x
                row = PAD + NZ * x + 5 * ez
                Y0[row : row + 6, :] = got[at : at + 6, 0:128]
                Y1[row : row + 6, :] = got[at : at + 6, 128:256]
        rows_to_flat(dest)

    for name in ("map", "stiff", "mass", "tab"):
        fetch[name].wait()
    WJ = tab_ref[24]
    LJ = (tab_ref[25], tab_ref[26])
    corner = map_ref[0:1, :]
    slot = (corner // (NZ * NY) // 5 * EZ + corner // NY % NZ // 5) * EY + corner % NY // 5
    count = EX * EZ * EY
    hot = (
        lax.broadcasted_iota(jnp.int32, (count, count), 0)
        == jnp.broadcast_to(slot, (count, count))
    ).astype(F32)
    geo = jnp.concatenate(
        [stiff_ref[...], mass_ref[...], jnp.zeros((4, count), F32)], axis=0
    )
    part_hi = geo.astype(BF16).astype(F32)
    part_mid = (geo - part_hi).astype(BF16).astype(F32)
    part_lo = geo - part_hi - part_mid
    pack = jnp.concatenate([part_hi, part_mid, part_lo], axis=0).astype(BF16)
    got = lax.dot_general(
        pack, hot.astype(BF16), (((1,), (1,)), ((), ())), preferred_element_type=F32
    )
    sorted_geo = got[0:8] + got[8:16] + got[16:24]
    stack = jnp.zeros((8, 128), F32)
    for q in range(4):
        for ex in range(EX):
            row = jnp.broadcast_to(
                sorted_geo[q : q + 1, 128 * ex : 128 * ex + 128], (8, 128)
            )
            SG[q, ex] = row
            stack = jnp.where(sub_i == EX * q + ex, row, stack)
    csend[...] = stack

    def geometry(h, tile):
        g = [
            [
                jnp.broadcast_to(tile[EX * q + ex : EX * q + ex + 1, :], (8, 128))
                for ex in range(EX)
            ]
            for q in range(4)
        ]
        for ex in range(EX):
            GX[h, 1 + ex] = WJ * g[0][ex]
        for x in range(NX):
            share = [(ex, x - 5 * ex) for ex in range(EX) if 0 <= x - 5 * ex <= 5]
            gy = mac([(float(w[i]), g[2][ex]) for ex, i in share])
            GC[h, 0, x] = WJ * gy
            if h == 1:
                GP[x] = float(w[0]) * gy
            GC[h, 1, x] = mac([(float(w[i]), g[1][ex]) for ex, i in share])
            GC[h, 2, x] = WJ * mac([(float(MASS_SHARE * w[i]), g[3][ex]) for ex, i in share])

    def face_geometry(h, tiles):
        for face, (tile, ex) in enumerate(zip(tiles, (EX - 1, 0))):
            g = [
                jnp.broadcast_to(tile[EX * q + ex : EX * q + ex + 1, :], (8, 128))
                for q in range(4)
            ]
            x = (NX - 1) * face
            GX[h, (EX + 1) * face] = WJ * g[0]
            GE[h, face, 0] = GC[h, 0, x] + WJ * (float(w[0]) * g[2])
            GE[h, face, 1] = GC[h, 1, x] + float(w[0]) * g[1]
            GE[h, face, 2] = GC[h, 2, x] + WJ * (float(MASS_SHARE * w[0]) * g[3])

    def whole_geometry(h, x):
        if x == 0:
            return tuple(GE[h, 0, q] for q in range(3))
        if x == NX - 1:
            return tuple(GE[h, 1, q] for q in range(3))
        return tuple(GC[h, q, x] for q in range(3))

    def diagonal_part(h):
        kj = tab_ref[27]
        for x in range(NX):
            share = [
                (ex, x - 5 * ex) for ex in range(-1, EX + 1) if 0 <= x - 5 * ex <= 5
            ]
            gx = mac([(float(k1[i, i]), GX[h, 1 + ex]) for ex, i in share])
            gy, gz, gm = whole_geometry(h, x)
            base = gx + gz * kj + gm
            for k in range(6):
                W[h, x, k] = float(w[k]) * base + float(k1[k, k]) * gy

    def apply_part(h):
        src, dst = V.at[h], W.at[h]
        for ex in range(EX):
            gx = GX[h, 1 + ex]
            for k in range(6):
                vs = [src[5 * ex + m, k] for m in range(6)]
                gk = float(w[k]) * gx
                for i in range(6):
                    value = gk * mac([(float(k1[i, m]), vs[m]) for m in range(6)])
                    if i == 0 and ex > 0:
                        value = value + dst[5 * ex, k]
                    dst[5 * ex + i, k] = value
        for x in range(NX):
            gy, gz, gm = GC[h, 0, x], GC[h, 1, x], GC[h, 2, x]
            vs = [src[x, m] for m in range(6)]
            for k in range(6):
                vk = vs[k]
                zterm = CT(0) * vk
                for sh in range(1, 8):
                    zterm = zterm + CT(sh) * pltpu.roll(vk, sh, 0)
                value = float(w[k]) * (gz * zterm + gm * vk)
                value = value + gy * mac([(float(k1[k, m]), vs[m]) for m in range(6)])
                dst[x, k] = dst[x, k] + value

    def fold_y(F, planes=range(NX)):
        for x in planes:
            low, high = F[x, 0], F[x, 5]
            F[x, 0] = low + jnp.where(ey > 0, pltpu.roll(high, 1, 1), 0.0)
            F[x, 5] = high + jnp.where(ey < EY - 1, pltpu.roll(low, 127, 1), 0.0)

    def fold_z(F):
        for x in range(NX):
            z0, z5 = F[0, x, :, 0, :], F[0, x, :, 5, :]
            h0, h5 = F[1, x, :, 0, :], F[1, x, :, 5, :]
            z0_up, z5_up = pltpu.roll(z0, EY, 1), pltpu.roll(z5, EY, 1)
            z0_down, z5_down = pltpu.roll(z0, 128 - EY, 1), pltpu.roll(z5, 128 - EY, 1)
            h0_up, h5_up = pltpu.roll(h0, EY, 1), pltpu.roll(h5, EY, 1)
            h0_down, h5_down = pltpu.roll(h0, 128 - EY, 1), pltpu.roll(h5, 128 - EY, 1)
            F[0, x, :, 0, :] = z0 + jnp.where(lane6 < EY, h5_down, z5_up)
            F[0, x, :, 5, :] = z5 + jnp.where(lane6 >= 128 - EY, h0_up, z0_down)
            add0 = jnp.where(group6 == 2, z5_down, h5_up)
            add5 = jnp.where(group6 == 1, z0_up, h0_down)
            F[1, x, :, 0, :] = h0 + jnp.where(group6 == 0, 0.0, add0)
            F[1, x, :, 5, :] = h5 + jnp.where(group6 == 3, 0.0, add5)

    def link(idx, slot_no, src, dst, device):
        return lambda: pltpu.make_async_remote_copy(
            src_ref=src,
            dst_ref=dst,
            send_sem=ex_send.at[idx, slot_no],
            recv_sem=ex_recv.at[idx, slot_no],
            device_id=device,
            device_id_type=MESH,
        )

    def x_links(idx):
        return [
            (has["xl"], has["xh"], link(idx, 1, xsend.at[idx, 0], xrecv.at[idx, 1], (b, s - 1))),
            (has["xh"], has["xl"], link(idx, 0, xsend.at[idx, 1], xrecv.at[idx, 0], (b, s + 1))),
        ]

    def z_links(idx):
        both = jnp.logical_and
        out = [
            (has["zl"], has["zh"], link(idx, 3, zsend.at[idx, 0], zrecv.at[idx, 1], (b - 1, s))),
            (has["zh"], has["zl"], link(idx, 2, zsend.at[idx, 1], zrecv.at[idx, 0], (b + 1, s))),
        ]
        for zs, db, zn, zr in ((0, -1, "zl", "zh"), (1, 1, "zh", "zl")):
            for xside, ds, xn, xr in ((0, -1, "xl", "xh"), (1, 1, "xh", "xl")):
                out.append(
                    (
                        both(has[zn], has[xn]),
                        both(has[zr], has[xr]),
                        link(
                            idx,
                            4 + 2 * (1 - zs) + (1 - xside),
                            zsend.at[idx, zs, (ZT - 1) * xside],
                            drecv.at[idx, 1 - zs, 1 - xside],
                            (b + db, s + ds),
                        ),
                    )
                )
        return out

    def halo_links(idx):
        def one(side, device):
            return lambda: pltpu.make_async_remote_copy(
                src_ref=bsend.at[idx, side, :, :, 0:6, :],
                dst_ref=brecv.at[idx, 1 - side, :, :, 0:6, :],
                send_sem=h_send.at[idx, side],
                recv_sem=h_recv.at[idx, 1 - side],
                device_id=device,
                device_id_type=MESH,
            )

        return [
            (has["zl"], has["zh"], one(0, (b - 1, s))),
            (has["zh"], has["zl"], one(1, (b + 1, s))),
        ]

    def links_start(links):
        for there, _, copy in links:

            @pl.when(there)
            def _(copy=copy):
                copy().start()

    def links_wait(links):
        for _, here, copy in links:

            @pl.when(here)
            def _(copy=copy):
                copy().wait_recv()

    def links_sent(links):
        for there, _, copy in links:

            @pl.when(there)
            def _(copy=copy):
                copy().wait_send()

    def x_start(idx, F):
        xsend[idx, 0] = F[0]
        xsend[idx, 1] = F[NX - 1]
        links_start(x_links(idx))

    def x_end(idx, F):
        links_wait(x_links(idx))
        F[0] = F[0] + xrecv[idx, 0]
        F[NX - 1] = F[NX - 1] + xrecv[idx, 1]

    def exchange_start(idx, F):
        fold_y(F)
        x_start(idx, F)
        z_start(idx, F)

    def z_start(idx, F):
        for t in range(ZT):
            low = high = jnp.zeros((6, 128), F32)
            for m in range(4):
                x = 4 * t + m
                if x >= NX:
                    continue
                low = jnp.where(group6 == m, moved(F[x, :, 0, :], EY * m), low)
                high = jnp.where(group6 == m, moved(F[x, :, 5, :], EY * (m + 1)), high)
            zsend[idx, 0, t, 0:6, :] = low
            zsend[idx, 1, t, 0:6, :] = high
        links_start(z_links(idx))

    def inner_z(F):
        for x in range(NX):
            z0, z5 = F[x, :, 0, :], F[x, :, 5, :]
            F[x, :, 0, :] = z0 + jnp.where(lane6 < EY, 0.0, pltpu.roll(z5, EY, 1))
            F[x, :, 5, :] = z5 + jnp.where(
                lane6 >= 128 - EY, 0.0, pltpu.roll(z0, 128 - EY, 1)
            )

    def outer_z(idx, F):
        links_wait(z_links(idx))
        for x in range(NX):
            t, m = divmod(x, 4)
            near = moved(zrecv[idx, 0, t, 0:6, :], -EY * m)
            far = moved(zrecv[idx, 1, t, 0:6, :], 128 - EY - EY * m)
            if x == 0:
                near = near + moved(drecv[idx, 0, 0, 0:6, :], -EY * LAST)
                far = far + moved(drecv[idx, 1, 0, 0:6, :], 128 - EY - EY * LAST)
            if x == NX - 1:
                near = near + drecv[idx, 0, 1, 0:6, :]
                far = far + moved(drecv[idx, 1, 1, 0:6, :], 128 - EY)
            F[x, :, 0, :] = F[x, :, 0, :] + jnp.where(lane6 < EY, near, 0.0)
            F[x, :, 5, :] = F[x, :, 5, :] + jnp.where(lane6 >= 128 - EY, far, 0.0)

    def exchange_end(idx, F):
        x_end(idx, F)
        inner_z(F)
        outer_z(idx, F)

    def halo_start(idx, src):
        for t in range(ZT):
            for k in range(6):
                low = high = jnp.zeros((8, 128), F32)
                for m in range(4):
                    x = 4 * t + m
                    if x >= NX:
                        continue
                    tile = src(x, k)
                    low = jnp.where(group == m, moved(tile, EY * m), low)
                    high = jnp.where(group == m, moved(tile, EY * (m + 1)), high)
                bsend[idx, 0, t, k] = low
                bsend[idx, 1, t, k] = high

    from_low = jnp.logical_and(group == 1, sub_i < 6)
    from_high = jnp.logical_and(group == 2, sub_i < 6)

    def halo_unpack(idx, store):
        for x in range(NX):
            t, m = divmod(x, 4)
            for k in range(6):
                low = moved(brecv[idx, 0, t, k], EY - EY * m)
                high = moved(brecv[idx, 1, t, k], 2 * EY - EY * m)
                store(x, k, jnp.where(from_low, low, jnp.where(from_high, high, 0.0)))

    near_rows = [
        jnp.where(group6 == 1, float(k1[5, j]), float(k1[0, j])) for j in range(6)
    ]

    def halo_faces():
        rims, faces = [], []
        for x in range(NX):
            rows = [V[1, x, :, j, :] for j in range(6)]
            rim = jnp.where(group6 == 1, rows[5], rows[0])
            across = mac(list(zip(near_rows, rows)))
            rim8 = jnp.concatenate([rim, jnp.zeros((2, 128), F32)], axis=0)
            along = CT(0) * rim8
            for sh in range(1, 8):
                along = along + CT(sh) * pltpu.roll(rim8, sh, 0)
            rims.append(rim)
            faces.append(
                (GC[1, 1, x] * WJ)[0:6] * across
                + GP[x, 0:6] * along[0:6]
                + GC[1, 2, x, 0:6] * (float(w[0]) * rim)
            )
        for ex in range(EX):
            scale = GX[1, 1 + ex, 0:6] * float(w[0])
            for i in range(6):
                x = 5 * ex + i
                faces[x] = faces[x] + scale * mac(
                    [(float(k1[i, m]), rims[5 * ex + m]) for m in range(6)]
                )
        return faces

    def join_halo(F, faces, planes):
        for x in planes:
            z0, z5, face = F[x, :, 0, :], F[x, :, 5, :], faces[x]
            F[x, :, 0, :] = z0 + jnp.where(
                lane6 < EY, pltpu.roll(face, 128 - EY, 1), pltpu.roll(z5, EY, 1)
            )
            F[x, :, 5, :] = z5 + jnp.where(
                lane6 >= 128 - EY, pltpu.roll(face, EY, 1), pltpu.roll(z0, 128 - EY, 1)
            )
        fold_y(F, planes)

    def finish_apply(idx, faces):
        F = W.at[0]
        join_halo(F, faces, (0, NX - 1))
        x_start(idx, F)
        join_halo(F, faces, range(1, NX - 1))
        x_end(idx, F)

    def window_copies(which, src, dst):
        out = []
        for off in range(-REACH, REACH + 1):
            for ds in range(n_sub):
                if off == 0 and ds == 0:
                    continue
                peer_s = lax.rem(s + ds, n_sub)
                target = b + off
                sending = jnp.logical_and(target >= 0, target < n_blk)

                def copy(off=off, ds=ds, peer_s=peer_s, target=target):
                    return pltpu.make_async_remote_copy(
                        src_ref=src,
                        dst_ref=dst.at[REACH - off, s],
                        send_sem=c_send.at[which, REACH + off, ds],
                        recv_sem=c_recv.at[which, REACH - off, s],
                        device_id=(target, peer_s),
                        device_id_type=MESH,
                    )

                def arrive(off=off, ds=ds, peer_s=peer_s, target=target):
                    return pltpu.make_async_remote_copy(
                        src_ref=src,
                        dst_ref=dst.at[REACH + off, peer_s],
                        send_sem=c_send.at[which, REACH + off, ds],
                        recv_sem=c_recv.at[which, REACH + off, peer_s],
                        device_id=(target, peer_s),
                        device_id_type=MESH,
                    )

                out.append((sending, copy, arrive))
        return out

    def window_start(which, src, dst):
        for sending, copy, _ in window_copies(which, src, dst):

            @pl.when(sending)
            def _(copy=copy):
                copy().start()

    def window_wait(which, src, dst):
        for sending, _, arrive in window_copies(which, src, dst):

            @pl.when(sending)
            def _(arrive=arrive):
                arrive().wait_recv()

    def window_sent(which, src, dst):
        for sending, copy, _ in window_copies(which, src, dst):

            @pl.when(sending)
            def _(copy=copy):
                copy().wait_send()

    def velocity(c):
        unpack_flat(lambda at: vel_flat[c, :, at], FL)
        to_elements(FL, VE, False)
        out = VV.at[c]
        rounded = lambda value: value.astype(BF16).astype(F32)
        for ex in range(EX):
            gx = SG[0, ex]
            for k in range(6):
                vs = [VE[5 * ex + m, k] for m in range(6)]
                flux = []
                for i in range(6):
                    grad = mac([(float(Dh[i, m]), vs[m]) for m in range(6)])
                    flux.append(rounded(grad * (WJ * float(w[i] * w[k])) * gx))
                for i in range(6):
                    value = mac([(float(Dh[m, i]), flux[m]) for m in range(6)])
                    if i == 0 and ex > 0:
                        value = value + out[5 * ex, k]
                    out[5 * ex + i, k] = value
        for ex in range(EX):
            gz, gy, gm = SG[1, ex], SG[2, ex], SG[3, ex]
            for i in range(6):
                x = 5 * ex + i
                vs = [VE[x, m] for m in range(6)]
                flux = []
                for k in range(6):
                    grad = mac([(float(Dh[k, m]), vs[m]) for m in range(6)])
                    flux.append(rounded(grad * (WJ * float(w[i] * w[k])) * gy))
                for k in range(6):
                    vk = vs[k]
                    weight = WJ * float(w[i] * w[k])
                    value = mac([(float(Dh[m, k]), flux[m]) for m in range(6)])
                    grad = tab_ref[8] * vk
                    for sh in range(1, 8):
                        grad = grad + tab_ref[8 + sh] * pltpu.roll(vk, sh, 0)
                    fz = rounded(grad * weight * gz)
                    value = value + tab_ref[16] * fz
                    for sh in range(1, 8):
                        value = value + tab_ref[16 + sh] * pltpu.roll(fz, sh, 0)
                    value = value + gm * weight * vk
                    out[x, k] = out[x, k] + value

    geometry(0, stack)
    fetch["load"].wait()
    fetch["pick"].wait()
    unpack_flat(lambda at: load_flat[at], FI)
    to_elements(FI, R.at[0], True)
    halo_start(0, lambda x, k: R[0, x, k])
    crecv[REACH, s] = stack
    for c in range(3):
        fetch["vel%d" % c].wait()

    def component(c, carry):
        velocity(c)

        @pl.when(c == 0)
        def _():
            pl.semaphore_wait(barrier, n_dev - 1)
            window_start(0, csend, crecv)
            links_start(halo_links(0))

        exchange_start(c, VV.at[c])
        return carry

    lax.fori_loop(0, 3, component, 0)

    window_wait(0, csend, crecv)

    def beside(t):
        low, high = crecv[REACH - 1, t], crecv[REACH + 1, t]
        return jnp.where(lane < 2 * EY, pltpu.roll(low, 64, 1), pltpu.roll(high, 64, 1))

    left_s, right_s = jnp.maximum(s - 1, 0), jnp.minimum(s + 1, n_sub - 1)
    left_on = jnp.where(has["xl"], 1.0, 0.0)
    right_on = jnp.where(has["xh"], 1.0, 0.0)
    geometry(1, beside(s))
    face_geometry(0, (crecv[REACH, left_s] * left_on, crecv[REACH, right_s] * right_on))
    face_geometry(1, (beside(left_s) * left_on, beside(right_s) * right_on))
    for h in range(2):
        diagonal_part(h)
    fold_z(W)
    for h in range(2):
        fold_y(W.at[h])
    for h in range(2):
        for x in range(NX):
            for k in range(6):
                full = W[h, x, k]
                good = full > 0.0
                INV[h, x, k] = jnp.where(good, DAMPING / jnp.where(good, full, 1.0), 0.0)

    corners = [(a, c, d) for a in (0, 1) for c in (0, 1) for d in (0, 1)]

    def stencil(z, carry):
        shifted = {}
        for c in (0, 1):
            for q in range(4):
                base = CF[z + 1 - c, q]
                for a in (0, 1):
                    up = pltpu.roll(base, 1, 0) if a else base
                    shifted[a, c, 0, q] = up
                    shifted[a, c, 1, q] = pltpu.roll(up, 1, 1)
        total = {}
        for ui, u in enumerate(corners):
            for vi, v in enumerate(corners):
                key = tuple(v[t] - u[t] for t in range(3))
                term = mac([(float(coarse[q][ui, vi]), shifted[u + (q,)]) for q in range(4)])
                total[key] = term if key not in total else total[key] + term
        for key, value in total.items():
            ST[z, 9 * (key[0] + 1) + 3 * (key[1] + 1) + key[2] + 1] = value
        diag = total[0, 0, 0]
        ST[z, 27] = jnp.where(diag > 0.0, 1.0 / jnp.where(diag > 0.0, diag, 1.0), 0.0)
        return carry

    for x in range(NX):
        for k in range(6):
            V[0, x, k] = R[0, x, k] * INV[0, x, k]
    apply_part(0)
    links_wait(halo_links(0))

    def first_halo(x, k, tile):
        V[1, x, k] = tile * INV[1, x, k]

    halo_unpack(0, first_halo)
    finish_apply(5, halo_faces())
    for x in range(NX):
        for k in range(6):
            V[0, x, k] = V[0, x, k] + (R[0, x, k] - W[0, x, k]) * INV[0, x, k]
    apply_part(0)
    fold_y(W.at[0])
    x_start(3, W.at[0])

    one = jnp.ones((8, 128), F32)
    wz = jnp.where(sub_i < 5, one, 0.0)
    wz = jnp.where(jnp.logical_and(sub_i == 5, lane >= 128 - EY), 1.0, wz)
    low_half = jnp.where(has["zl"], 0.5, 1.0)
    high_half = jnp.where(has["zh"], 0.5, 1.0)
    wz = wz * jnp.where(jnp.logical_and(sub_i == 0, lane < EY), low_half, 1.0)
    wz = wz * jnp.where(jnp.logical_and(sub_i == 5, lane >= 128 - EY), high_half, 1.0)
    wend = wz * jnp.where(ey == EY - 1, 1.0, 0.0)
    xlow = jnp.where(has["xl"], 0.5, 1.0)
    xhigh = jnp.where(has["xh"], 0.5, 1.0)

    def unique(x, k):
        tile = wz if k < 5 else wend
        if x == 0:
            tile = tile * xlow
        if x == NX - 1:
            tile = tile * xhigh
        return tile

    acc = [[None, None] for _ in range(EX + 1)]
    for x in range(NX):
        rows = [unique(x, k) * R[0, x, k] - W[0, x, k] for k in range(5)]
        last_row = unique(x, 5) * R[0, x, 5] - W[0, x, 5]
        rows.append(jnp.where(ey == EY - 1, last_row, 0.0))
        lines = [mac([(float(lin[k, d]), rows[k]) for k in range(6)]) for d in (0, 1)]
        ex = min(x // 5, EX - 1)
        i = x - 5 * ex
        for a in (0, 1):
            weight = float(lin[i, a])
            if weight == 0.0:
                continue
            for d in (0, 1):
                term = weight * lines[d]
                old = acc[ex + a][d]
                acc[ex + a][d] = term if old is None else old + term
    pieces = {}
    for c in (0, 1):
        for d in (0, 1):
            tile = jnp.zeros((8, 128), F32)
            for xv in range(EX + 1):
                row = jnp.sum(LJ[c] * acc[xv][d], axis=0, keepdims=True)
                tile = jnp.where(sub_i == xv, jnp.broadcast_to(row, (8, 128)), tile)
            pieces[c, d] = tile
    placed = [None] * (EZ + 1)
    for c in (0, 1):
        for ez in range(EZ):
            sums = None
            for d in (0, 1):
                tile = jnp.where(lane < EY, moved(pieces[c, d], -EY * ez), 0.0)
                if d:
                    tile = pltpu.roll(tile, 1, 1)
                sums = tile if sums is None else sums + tile
            old = placed[ez + c]
            placed[ez + c] = sums if old is None else old + sums
    message = placed[0]
    for zv in range(1, EZ + 1):
        rows_at, lanes_at = divmod(zv, 3)
        tile = moved(placed[zv], (EY + 8) * lanes_at)
        if rows_at:
            tile = pltpu.roll(tile, (EX + 1) * rows_at, 0)
        message = message + tile
    rsend[...] = message
    rrecv[REACH, s] = message
    window_start(1, rsend, rrecv)

    z_start(3, W.at[0])
    x_end(3, W.at[0])
    inner_z(W.at[0])
    halo_start(1, lambda x, k: V[0, x, k] + (R[0, x, k] - W[0, x, k]) * INV[0, x, k])
    links_start(halo_links(1))
    for o in range(SPAN):
        for t in range(n_sub):
            packed = crecv[o, t]
            for ez in range(EZ):
                if not ZLO - 1 <= EZ * o + ez <= ZHI:
                    continue
                tile = jnp.where(lane < EY, moved(packed, -EY * ez), 0.0)
                for q in range(4):
                    CF[EZ * o + ez + 1, q, EX * t : EX * t + EX, :] = tile[
                        EX * q : EX * q + EX, :
                    ]

    lax.fori_loop(ZLO, ZHI + 1, stencil, 0)
    outer_z(3, W.at[0])
    for x in range(NX):
        for k in range(6):
            V[0, x, k] = V[0, x, k] + (R[0, x, k] - W[0, x, k]) * INV[0, x, k]

    fetch["put"].wait()

    def velocity_out(c):
        exchange_end(c, VV.at[c])
        to_nodes(VV.at[c], FP)

        def store(at, tile):
            vel_back[c, :, at] = tile.reshape(1, tile.size)

        pack_flat(lambda p, n: FP[PAD + p : PAD + p + n, :], store)

    velocity_out(0)
    window_wait(1, rsend, rrecv)

    def window_sum(o, zv):
        rows_at, lanes_at = divmod(zv, 3)
        total = None
        for t in range(n_sub):
            tile = moved(rrecv[o, t], -(EY + 8) * lanes_at)
            here = jnp.logical_and(
                sub_i >= (EX + 1) * rows_at, sub_i < (EX + 1) * (rows_at + 1)
            )
            tile = jnp.where(jnp.logical_and(here, lane <= EY), tile, 0.0)
            if xs > 8:
                tile = jnp.concatenate([tile, jnp.zeros((xs - 8, 128), F32)], axis=0)
            shift = (EX * t - (EX + 1) * rows_at) % xs
            if shift:
                tile = pltpu.roll(tile, shift, 0)
            total = tile if total is None else total + tile
        return total

    center = (SPECTRUM_HIGH + SPECTRUM_LOW) / 2.0
    radius = (SPECTRUM_HIGH - SPECTRUM_LOW) / 2.0
    ratio = center / radius
    factor = 1.0 / ratio
    for z in range(ZLO, ZHI + 1):
        o, zv = divmod(z, EZ)
        value = window_sum(o, zv)
        if zv == 0 and o > 0:
            value = value + window_sum(o - 1, EZ)
        CR[z] = value
        CU[0, z] = value * ST[z, 27] * (1.0 / center)
    first, last = FIRST - HALO, LAST_V + HALO
    sol = {z: CU[0, z] for z in range(first, last + 1)}
    for sweep in range(CHEB_ITERS - 1):
        now, later = sweep % 2, (sweep + 1) % 2
        left = CHEB_ITERS - 2 - sweep
        nxt = 1.0 / (2.0 * ratio - factor)
        wide = {}
        for z in range(first - left, last + left + 1):
            for zz in (z - 1, z, z + 1):
                if zz in wide:
                    continue
                base = CU[now, zz]
                sides = {}
                for dx in (-1, 0, 1):
                    mx = base if dx == 0 else pltpu.roll(base, (-dx) % xs, 0)
                    for dy in (-1, 0, 1):
                        sides[dx, dy] = mx if dy == 0 else pltpu.roll(mx, (-dy) % 128, 1)
                wide[zz] = sides
            total = None
            for dz in (-1, 0, 1):
                for dx in (-1, 0, 1):
                    for dy in (-1, 0, 1):
                        term = ST[z, 9 * (dx + 1) + 3 * (dz + 1) + dy + 1] * wide[z + dz][dx, dy]
                        total = term if total is None else total + term
            residual = CR[z] - total
            CR[z] = residual
            fresh = (nxt * factor) * CU[now, z] + (2.0 * nxt / radius) * (residual * ST[z, 27])
            CU[later, z] = fresh
            if first <= z <= last:
                sol[z] = sol[z] + fresh
        factor = nxt

    own = {}
    for z, tile in sol.items():
        shifted_x = tile
        for t in range(1, n_sub):
            shifted_x = jnp.where(s == t, pltpu.roll(tile, (-EX * t) % xs, 0), shifted_x)
        own[z - FIRST] = shifted_x

    links_wait(halo_links(1))

    def base_halo(x, k, tile):
        V[1, x, k] = tile

    halo_unpack(1, base_halo)
    for x in range(NX):
        z0, z5 = V[0, x, :, 0, :], V[0, x, :, 5, :]
        V[1, x, :, 5, :] = jnp.where(
            group6 == 1, pltpu.roll(z0, EY, 1), V[1, x, :, 5, :]
        )
        V[1, x, :, 0, :] = jnp.where(
            group6 == 2, pltpu.roll(z5, 128 - EY, 1), V[1, x, :, 0, :]
        )

    ZJ = tab_ref[28]
    for h in range(2):
        places = range(EZ) if h == 0 else (-2, -1, EZ, EZ + 1)
        corner_tiles = {}
        for c in (0, 1):
            for d in (0, 1):
                total = None
                for at, ez in enumerate(places):
                    tile = own[ez + c]
                    if d:
                        tile = pltpu.roll(tile, 127, 1)
                    tile = moved(jnp.where(lane[0:1] < EY, tile, 0.0), EY * at)
                    total = tile if total is None else total + tile
                corner_tiles[c, d] = total
        val, zdif, ydif = {}, {}, {}
        for xv in range(-1, EX + 2):
            at = xv % xs
            rows = {
                key: jnp.broadcast_to(tile[at : at + 1, :], (8, 128))
                for key, tile in corner_tiles.items()
            }
            ends = [LJ[0] * rows[0, d] + LJ[1] * rows[1, d] for d in (0, 1)]
            val[xv] = [mac([(float(lin[k, d]), ends[d]) for d in (0, 1)]) for k in range(6)]
            if 0 <= xv <= EX:
                jump = [ZJ * (rows[0, d] - rows[1, d]) for d in (0, 1)]
                zdif[xv] = [
                    mac([(float(lin[k, d]), jump[d]) for d in (0, 1)]) for k in range(6)
                ]
                ydif[xv] = 0.5 * (ends[0] - ends[1])
        for x in range(NX):
            ex = min(x // 5, EX - 1)
            i = x - 5 * ex
            parts = [(float(lin[i, a]), ex + a) for a in (0, 1)]
            gy, gz, gm = whole_geometry(h, x)
            slope = gy * mac([(weight, ydif[xv]) for weight, xv in parts])
            for k in range(6):
                u = mac([(weight, val[xv][k]) for weight, xv in parts])
                inside = gz * mac([(weight, zdif[xv][k]) for weight, xv in parts]) + gm * u
                if x % 5 == 0:
                    xv = x // 5
                    inside = inside + GX[h, xv] * (0.5 * (val[xv][k] - val[xv - 1][k]))
                    inside = inside + GX[h, xv + 1] * (0.5 * (val[xv][k] - val[xv + 1][k]))
                value = float(w[k]) * inside
                if k == 0:
                    value = value + slope
                if k == 5:
                    value = value - slope
                W[h, x, k] = value
                V[h, x, k] = V[h, x, k] + u
    fold_z(W)
    for h in range(2):
        fold_y(W.at[h])
    for h in range(2):
        for x in range(NX):
            for k in range(6):
                V[h, x, k] = V[h, x, k] - W[h, x, k] * INV[h, x, k]
    apply_part(0)
    finish_apply(6, halo_faces())
    for x in range(NX):
        for k in range(6):
            V[0, x, k] = V[0, x, k] + (R[0, x, k] - W[0, x, k]) * INV[0, x, k]
    apply_part(0)
    num = jnp.zeros((8, 128), F32)
    den = jnp.zeros((8, 128), F32)
    for x in range(NX):
        for k in range(6):
            v = V[0, x, k]
            num = num + unique(x, k) * R[0, x, k] * v
            den = den + v * W[0, x, k]
    num_row = jnp.sum(num, axis=0, keepdims=True)
    den_row = jnp.sum(den, axis=0, keepdims=True)
    num_one = jnp.sum(num_row, axis=1, keepdims=True)
    den_one = jnp.sum(den_row, axis=1, keepdims=True)
    lane1 = lax.broadcasted_iota(jnp.int32, (1, 128), 1)
    psend[...] = jnp.where(lane1 < 64, num_one, den_one)

    def scatter(d, carry):
        pltpu.make_async_remote_copy(
            src_ref=psend,
            dst_ref=precv.at[d - 1],
            send_sem=p_sem.at[0],
            recv_sem=p_sem.at[1],
            device_id=device_of(lax.rem(me + d, n_dev)),
            device_id_type=MESH,
        ).start()
        return carry

    lax.fori_loop(1, n_dev, scatter, 0)
    exchange_start(4, W.at[0])
    for c in (1, 2):
        velocity_out(c)
    to_nodes(V.at[0], FP)
    exchange_end(4, W.at[0])
    to_nodes(W.at[0], FR)
    whole = pltpu.make_async_remote_copy(
        src_ref=precv,
        dst_ref=precv,
        send_sem=p_sem.at[0],
        recv_sem=p_sem.at[1],
        device_id=(b, s),
        device_id_type=MESH,
    )
    whole.wait_recv()
    both = psend[...] + jnp.sum(precv[...], axis=0)
    step = both[0:1, 0:1] / both[0:1, 64:65]

    def store_to(back):
        def store(at, tile):
            back[at] = tile.reshape(tile.size)

        return store

    pack_flat(lambda p, n: step * FP[PAD + p : PAD + p + n, :], store_to(pres_back))
    pack_flat(
        lambda p, n: FI[PAD + p : PAD + p + n, :] - step * FR[PAD + p : PAD + p + n, :],
        store_to(res_back),
    )
    whole.wait_send()
    for idx in range(5):
        links_sent(x_links(idx) + z_links(idx))
    for idx in range(5, EXCH):
        links_sent(x_links(idx))
    for idx in range(2):
        links_sent(halo_links(idx))
    window_sent(0, csend, crecv)
    window_sent(1, rsend, rrecv)


def place(vel, pres, res, vel_out, pres_out, res_out, sem):
    stores = [
        pltpu.make_async_copy(vel.at[c], vel_out.at[pl.ds(c, 1)], sem.at[c]) for c in range(3)
    ]
    stores.append(pltpu.make_async_copy(pres, pres_out, sem.at[3]))
    stores.append(pltpu.make_async_copy(res, res_out, sem.at[4]))
    for copy in stores:
        copy.start()
    for copy in stores:
        copy.wait()


def solution(mesh):
    n_blk, n_sub = mesh.shape["blk"], mesh.shape["sub"]
    n_dev = n_blk * n_sub
    xs = -(-(EX * n_sub + 2) // 8) * 8
    D, w, k1, lin, coarse = tables()
    Dh = bf16_round(D)
    tab = np.concatenate(
        [
            roll_tables(k1),
            roll_tables(Dh),
            roll_tables(Dh.T),
            col_tile(w),
            col_tile(lin[:, 0]),
            col_tile(lin[:, 1]),
            col_tile(np.diag(k1)),
            col_tile([0.5, 0.0, 0.0, 0.0, 0.0, -0.5]),
        ]
    )
    pick, put = pick_matrices()

    def per_device(velocity, pressure_load, local_map, stiff_geo, mass_geo):
        field = (NX, 6, 8, 128)
        reach_in = NY * (IN_STEP - 1) // 128 + 3 + 7 * IN_SKIP
        reach_out = FLAT + 8 * OUT_SKIP
        flat = pltpu.VMEM((PAD + -(-max(reach_in, reach_out) // 8) * 8, 128), F32)
        out_rows = PAD + -(-(ROWS + 8 * OUT_STEP + 2) // 8) * 8
        out = pl.pallas_call(
            functools.partial(kernel, n_blk, n_sub, xs),
            out_shape=(
                pltpu.VMEM((3, 1, NLOC), F32),
                pltpu.VMEM((NLOC,), F32),
                pltpu.VMEM((NLOC,), F32),
            ),
            in_specs=[pl.BlockSpec(memory_space=pl.ANY)] * 8,
            out_specs=(pl.BlockSpec(memory_space=pltpu.VMEM),) * 3,
            scratch_shapes=[
                pltpu.VMEM((3, 1, NLOC), F32),
                pltpu.VMEM((NLOC,), F32),
                flat,
                flat,
                flat,
                flat,
                pltpu.VMEM((IN_ROWS, 128), F32),
                pltpu.VMEM((IN_ROWS, 128), F32),
                pltpu.VMEM((out_rows, 128), F32),
                pltpu.VMEM((out_rows, 128), F32),
                pltpu.VMEM((3, EX * EZ * EY), F32),
                pltpu.VMEM((1, EX * EZ * EY), F32),
                pltpu.VMEM(tab.shape, F32),
                pltpu.VMEM(pick.shape, BF16),
                pltpu.VMEM(put.shape, BF16),
                pltpu.VMEM((2,) + field, F32),
                pltpu.VMEM((2,) + field, F32),
                pltpu.VMEM((8, EX * EZ * EY), jnp.int32),
                pltpu.VMEM((1,) + field, F32),
                pltpu.VMEM((2,) + field, F32),
                pltpu.VMEM((3,) + field, F32),
                pltpu.VMEM(field, F32),
                pltpu.VMEM((2, EX + 2, 8, 128), F32),
                pltpu.VMEM((2, 3, NX, 8, 128), F32),
                pltpu.VMEM((2, 2, 3, 8, 128), F32),
                pltpu.VMEM((NX, 8, 128), F32),
                pltpu.VMEM((4, EX, 8, 128), F32),
                pltpu.VMEM((EXCH, 2, 6, 8, 128), F32),
                pltpu.VMEM((EXCH, 2, 6, 8, 128), F32),
                pltpu.VMEM((EXCH, 2, ZT, 8, 128), F32),
                pltpu.VMEM((EXCH, 2, ZT, 8, 128), F32),
                pltpu.VMEM((EXCH, 2, 2, 8, 128), F32),
                pltpu.VMEM((8, 128), F32),
                pltpu.VMEM((SPAN, n_sub, 8, 128), F32),
                pltpu.VMEM((8, 128), F32),
                pltpu.VMEM((SPAN, n_sub, 8, 128), F32),
                pltpu.VMEM((2, 2, ZT, 6, 8, 128), F32),
                pltpu.VMEM((2, 2, ZT, 6, 8, 128), F32),
                pltpu.VMEM((NZV + 1, 4, xs, 128), F32),
                pltpu.VMEM((NZV, 28, xs, 128), F32),
                pltpu.VMEM((2, NZV, xs, 128), F32),
                pltpu.VMEM((NZV, xs, 128), F32),
                pltpu.VMEM((1, 128), F32),
                pltpu.VMEM((n_dev - 1, 1, 128), F32),
                pltpu.SemaphoreType.DMA((EXCH, 8)),
                pltpu.SemaphoreType.DMA((EXCH, 8)),
                pltpu.SemaphoreType.DMA((2, SPAN, n_sub)),
                pltpu.SemaphoreType.DMA((2, SPAN, n_sub)),
                pltpu.SemaphoreType.DMA((2, 2)),
                pltpu.SemaphoreType.DMA((2, 2)),
                pltpu.SemaphoreType.DMA((2,)),
                pltpu.SemaphoreType.DMA((10,)),
            ],
            compiler_params=pltpu.CompilerParams(
                collective_id=0, has_side_effects=True, vmem_limit_bytes=60 << 20
            ),
        )(
            velocity,
            pressure_load,
            local_map,
            stiff_geo,
            mass_geo.reshape(1, mass_geo.shape[0]),
            jnp.asarray(tab, F32),
            jnp.asarray(pick, BF16),
            jnp.asarray(put, BF16),
        )
        any_spec = pl.BlockSpec(memory_space=pl.ANY)
        return tuple(
            pl.pallas_call(
                place,
                out_shape=(
                    jax.ShapeDtypeStruct((3, NLOC), F32),
                    jax.ShapeDtypeStruct((NLOC,), F32),
                    jax.ShapeDtypeStruct((NLOC,), F32),
                ),
                in_specs=[pl.BlockSpec(memory_space=pltpu.VMEM)] * 3,
                out_specs=(any_spec,) * 3,
                scratch_shapes=[pltpu.SemaphoreType.DMA((5,))],
            )(*(pltpu.with_memory_space_constraint(o, pltpu.VMEM) for o in out))
        )

    in_specs = (
        P(None, ("blk", "sub")),
        P(("blk", "sub")),
        P(None, ("blk", "sub")),
        P(None, ("blk", "sub")),
        P(("blk", "sub")),
    )
    out_specs = (P(None, ("blk", "sub")), P(("blk", "sub")), P(("blk", "sub")))
    return jax.shard_map(
        per_device, mesh=mesh, in_specs=in_specs, out_specs=out_specs, check_vma=False
    )
```
